32 devices in a mesh: rep: 2 (over y), ep: 8 (over z, core), tp: 2 (over x).
Axes of the slice: x: 2, y: 2, z: 4, core: 2. Of those that a mesh axis runs over, the one named last changes fastest.
Arguments:
- hidden_states: bfloat16 [2, 1024, 2048], P(None, ('rep', 'ep'), 'tp'), parts along dimension 1, may hold values from -8 to 8
- queries: bfloat16 [2, 1024, 4096], P(None, ('rep', 'ep'), 'tp'), parts along dimension 1, may hold values from -8 to 8
- fresh_key_value: bfloat16 [2, 1024, 2, 512], P(None, ('rep', 'ep'), None, 'tp'), parts along dimension 1, may hold values from -8 to 8
- cache: bfloat16 [16, 2, 1024, 512], P(('rep', 'ep'), None, None, 'tp'), parts along dimension 0, may hold values from -8 to 8
- cache_lengths: int32 [16], P(('rep', 'ep')), parts along dimension 0, may hold values from 1 to 1024, 4096 in all
- out_weight: bfloat16 [4096, 2048], P('tp', 'ep'), may hold values from -1 to 1
- router_weight: bfloat16 [2048, 16], P('tp'), may hold values from -0.125 to 0.125
- expert_weights: bfloat16 [16, 3, 2048, 384], P('ep', None, 'tp'), may hold values from -0.21875 to 0.21875
- expert_ids: int32 [2, 1024, 8], P(None, ('rep', 'ep')), parts along dimension 1, may hold values from 0 to 15, all different within a row; in each aligned block of 64 rows (0 to 63, 64 to 127, ..., all dimensions but the last counted through in order) at most 48 rows name the same one
- old_slots: int32 [16], replicated, may hold values from 0 to 15, as said below
- new_slots: int32 [16], replicated, may hold values from 0 to 15, as said below
- moved_experts: int32 [4], replicated, may hold values from 0 to 15, as said below
Outputs:
- mixed: bfloat16 [2, 1024, 2048], P(None, ('rep', 'ep'), 'tp'), parts along dimension 1
The draws below stay inside these ranges and needn't reach their ends.
There are 2 independent parts, one for each index of `rep`. The reference program is written for one: setup_inputs(seed, part) draws one part's arguments, and reference() takes and returns one part's arrays. A program takes and returns all parts, laid end to end along the dimension named above; an argument that names none is the same for every part. Nothing has to cross between parts.
Inputs may be any that keep to these rules, and one draw needn't show every extreme that they name: `expert_ids`: each row names 8 different experts. Within the 64 rows of one request in one token block, no expert is named by more than 48 rows, a bound that some block reaches. `old_slots`: A permutation: each slot holds one expert. `new_slots`: equal to old_slots except at the moved experts, which take one another's old slots, none keeping its own. `moved_experts`: 4 different experts; no two of their old slots s share the same s // 2.
All inputs are finite; a program needn't handle non-finite values. No bound on the sum of `cache_lengths` on one device may be relied on, other than what follows from the above.
Results may differ from the reference program's by a relative error of at most 0.017.
Values may be sent and summed in bfloat16 or wider, within the bound.
A program may use at most 64 MiB of HBM per device.

```python
import math
import jax
import jax.numpy as jnp
import numpy as np
from jax import lax

D = 2048
QUERY_HEADS = 32
KEY_VALUE_HEADS = 4
HEAD_SIZE = 128
FFW = 384
TOP = 8
EXP_DEV = 2
REQUEST_TOKENS = 64
CACHED_POSITIONS = 1024
EXPERTS = 16
REQUEST_COUNT = 8
BLOCK_TOKENS = 512
CAP = 48
MOVED = 4
QUARTER = 1024
N_TP = 2


def slot_plan(key):
    base_key = jax.random.fold_in(key, 5)
    perm_key, device_key, local_key = jax.random.split(base_key, 3)
    old_table = jax.random.permutation(perm_key, EXPERTS).astype(jnp.int32)
    devices = jax.random.permutation(device_key, REQUEST_COUNT)[:MOVED].astype(jnp.int32)
    local_pick = jax.random.randint(local_key, (MOVED,), 0, EXP_DEV).astype(jnp.int32)
    chosen = (devices * EXP_DEV + local_pick).astype(jnp.int32)
    owners = jnp.argsort(old_table).astype(jnp.int32)
    moved_list = owners[chosen].astype(jnp.int32)
    new_table = old_table.at[moved_list].set(jnp.roll(chosen, -1))
    return (old_table, new_table, moved_list)


def draw_old_slots(key, part):
    return slot_plan(key)[0]


def draw_new_slots(key, part):
    return slot_plan(key)[1]


def draw_moved_experts(key, part):
    return slot_plan(key)[2]


def draw_queries(key, part):
    array_extent = (2, BLOCK_TOKENS, QUERY_HEADS * HEAD_SIZE)
    return jnp.clip(jax.random.normal(jax.random.fold_in(key, 1), array_extent), -8.0, 8.0).astype(jnp.bfloat16)


def draw_fresh_key_value(key, part):
    array_extent = (2, BLOCK_TOKENS, 2, KEY_VALUE_HEADS * HEAD_SIZE)
    return jnp.clip(jax.random.normal(jax.random.fold_in(key, 2), array_extent), -8.0, 8.0).astype(jnp.bfloat16)


def draw_hidden_states(key, part):
    array_extent = (2, BLOCK_TOKENS, D)
    along = jnp.arange(D, dtype=jnp.float32) / (D - 1)
    rough = jnp.exp(jax.random.uniform(jax.random.fold_in(key, 8), (D,), minval=jnp.log(0.7), maxval=jnp.log(1.4)))
    base_values = jax.random.normal(jax.random.fold_in(key, 4), array_extent)
    row_scale = jnp.exp(jax.random.uniform(jax.random.fold_in(key, 7), (2, BLOCK_TOKENS, 1), minval=jnp.log(0.2), maxval=jnp.log(2.0)))
    column_scale = jnp.exp(jnp.log(0.4) + (jnp.log(4.0) - jnp.log(0.4)) * along) * rough
    return jnp.clip(0.5 * base_values * row_scale * column_scale, -8.0, 8.0).astype(jnp.bfloat16)


def level_of(key, dims, cuts, least, high):
    def one(dim, blocks):
        draws = jax.random.uniform(jax.random.fold_in(jax.random.fold_in(key, 6), dim), (blocks,), jnp.float32, least / len(cuts), high / len(cuts))
        return jnp.repeat(jnp.exp(draws), dims[dim] // blocks).reshape((-1,) + (1,) * (len(dims) - dim - 1))

    gain = one(*cuts[0])
    for cut in cuts[1:]:
        gain = gain * one(*cut)
    return gain


def profile(number_of, total, bound, skew):
    portions = [(1 << 20) // math.isqrt(grade ** skew) + 1 for grade in range(2, number_of + 1)]
    spare, counts = total - bound - (number_of - 1), [1] * (number_of - 1)
    while spare > 0:
        candidates = [i for i in range(number_of - 1) if counts[i] < bound]
        mass, remaining = sum([portions[i] for i in candidates]), spare
        for i in candidates:
            more = min(bound - counts[i], max(1, remaining * portions[i] // mass), spare)
            counts[i] = counts[i] + more
            spare = spare - more
    return np.array([bound] + counts)


def ragged_sizes(rng, count, total, bound, lean):
    if count == 2:
        one = jax.random.randint(rng, (), max(1, total - bound), min(bound, total - 1) + 1)
        return jnp.stack([one, total - one])
    sizes = jnp.asarray(profile(count, total, bound, lean), jnp.int32)
    twos = (count - 1) // 2
    giver, receiver = sizes[1:1 + 2 * twos:2], sizes[2:2 + 2 * twos:2]
    margin = jnp.minimum(giver - 1, bound - receiver)
    shifted = jax.random.randint(jax.random.fold_in(rng, 1), (twos,), 0, 1 << 20) % (margin + 1)
    sizes = sizes.at[1:1 + 2 * twos:2].set(giver - shifted).at[2:2 + 2 * twos:2].set(receiver + shifted)
    return sizes[jax.random.permutation(jax.random.fold_in(rng, 2), count)]


def deal_out(rng, own, number, rows, amount, top, most, lean):
    sequence = jax.random.permutation(rng, amount)
    heavy_load, ordinary = portions_of(amount, rows * top, most, lean, True), portions_of(amount, rows * top, most, lean, False)
    places = jnp.arange(amount)

    def named(tallies, rotation):
        used = int((tallies > 0).sum())
        fixed = max(1, used // 4)
        moved = fixed + (places - fixed + rotation * (used - fixed)) % max(1, amount - fixed)
        return jnp.zeros((amount,), jnp.int32).at[sequence[jnp.where(places < fixed, places, moved)]].set(jnp.asarray(tallies, jnp.int32))

    tallies = jnp.where(number % 4 == 0, named(heavy_load, number // 4), named(ordinary, number - number // 4 - 1))
    mixed = jax.random.permutation(jax.random.fold_in(own, 3), amount)
    giver, taker = mixed[0:amount // 2 * 2:2], mixed[1:amount // 2 * 2:2]
    room = jnp.minimum(tallies[giver] - 1, most - tallies[taker]) // 2
    room = jnp.where((giver == sequence[0]) | (taker == sequence[0]) | (tallies[taker] == 0), 0, jnp.maximum(room, 0))
    moved = jax.random.randint(jax.random.fold_in(own, 4), (amount // 2,), 0, 1 << 20) % (room + 1)
    tallies = tallies.at[giver].add(-moved).at[taker].add(moved)
    members = jnp.searchsorted(jnp.cumsum(tallies), jnp.arange(rows * top), side="right").astype(jnp.int32)
    grid = members.reshape(top, rows).T
    grid = grid[jax.random.permutation(jax.random.fold_in(own, 1), rows)]
    rotation = jax.random.randint(jax.random.fold_in(own, 2), (rows, 1), 0, top)
    return jnp.take_along_axis(grid, (jnp.arange(top)[None, :] + rotation) % top, axis=1)


def portions_of(amount, total, bound, slope, full):
    portions = [(1 << 20) // math.isqrt(standing ** slope) + 1 for standing in range(1, amount + 1)]
    largest = bound if full else min(bound, max(-(-total // amount), total * portions[0] // sum(portions)))
    least = 1 if total - largest >= amount - 1 else 0
    holding, surplus = [largest] + [least] * (amount - 1), total - largest - least * (amount - 1)
    while surplus > 0:
        candidates = [i for i in range(1, amount) if holding[i] < largest] or [i for i in range(1, amount) if holding[i] < bound]
        pool, remaining = sum([portions[i] for i in candidates]), surplus
        for i in candidates:
            more = min(bound - holding[i], max(1, remaining * portions[i] // pool), surplus)
            holding[i] = holding[i] + more
            surplus = surplus - more
    return np.array(holding)


def bell_draw(own_key, extent, deviation, limit, cuts=(), kind=jnp.bfloat16):
    values = jax.random.normal(own_key, extent, jnp.float32) * deviation
    if len(cuts) > 0:
        values = level_of(own_key, extent, cuts, -0.22, 0.18) * values
    return jnp.clip(values, min=-limit, max=limit).astype(kind)


def setup_inputs(seed: int = 0, part: int = 0) -> dict:
    key_of = jax.random.split(jax.random.key(seed), 13)
    own_keys = jax.random.split(jax.random.fold_in(key_of[12], part), 13)
    hidden_states = draw_hidden_states(jax.random.fold_in(jax.random.fold_in(key_of[12], part), 71), part)
    queries = draw_queries(jax.random.fold_in(jax.random.fold_in(key_of[12], part), 71), part)
    fresh_key_value = draw_fresh_key_value(jax.random.fold_in(jax.random.fold_in(key_of[12], part), 71), part)
    cache = bell_draw(own_keys[3], (REQUEST_COUNT, 2, CACHED_POSITIONS, KEY_VALUE_HEADS * HEAD_SIZE), 1.0, 8.0, ((0, 8), (3, 2)))
    cache_lengths = ragged_sizes(own_keys[4], REQUEST_COUNT, REQUEST_COUNT * CACHED_POSITIONS // 2, CACHED_POSITIONS, 1).astype(jnp.int32)
    out_weight = bell_draw(key_of[5], (QUERY_HEADS * HEAD_SIZE, D), 0.125, 1.0, ((0, 2), (1, 8)))
    router_weight = bell_draw(key_of[6], (D, EXPERTS), D ** -0.5, 0.125, ((0, 2),))
    expert_weights = bell_draw(key_of[7], (EXPERTS, 3, D, FFW), (2 * FFW) ** -0.5, 0.21875, ((0, 8), (2, 2)))
    expert_ids_keys = jax.random.split(jax.random.fold_in(own_keys[8], 1), 2 * BLOCK_TOKENS // REQUEST_TOKENS)
    expert_ids_turns = jax.random.permutation(jax.random.fold_in(own_keys[8], 3), 2 * BLOCK_TOKENS // REQUEST_TOKENS)
    expert_ids = jax.vmap(lambda own, number: deal_out(jax.random.fold_in(own_keys[8], 2), own, number, REQUEST_TOKENS, EXPERTS, TOP, CAP, 2))(expert_ids_keys, expert_ids_turns).reshape((2, BLOCK_TOKENS, TOP))
    old_slots = draw_old_slots(jax.random.fold_in(key_of[12], 71), part)
    new_slots = draw_new_slots(jax.random.fold_in(key_of[12], 71), part)
    moved_experts = draw_moved_experts(jax.random.fold_in(key_of[12], 71), part)
    return dict(hidden_states=hidden_states, queries=queries, fresh_key_value=fresh_key_value, cache=cache, cache_lengths=cache_lengths, out_weight=out_weight, router_weight=router_weight, expert_weights=expert_weights, expert_ids=expert_ids, old_slots=old_slots, new_slots=new_slots, moved_experts=moved_experts)


def lookup(entries, wanted_keys):
    return lax.optimization_barrier(jnp.sum(jnp.where(wanted_keys[..., None] == jnp.arange(entries.shape[0], dtype=jnp.int32), entries, 0), -1)).astype(jnp.int32)

def slot_source(old_slots, new_slots, moved_experts):
    slots_all = jnp.arange(EXPERTS, dtype=jnp.int32)
    new_moved = lookup(new_slots, moved_experts)
    old_moved = lookup(old_slots, moved_experts)
    matches = slots_all[:, None] == new_moved[None, :]
    return jnp.where(matches.any(1), lax.optimization_barrier(jnp.sum(jnp.where(matches, old_moved[None, :], 0), 1)), slots_all).astype(jnp.int32)

def attend_request(packed):
    query_portion, new_part, cached, length = packed
    row_total = query_portion.shape[1]
    key_matrix = jnp.concatenate([cached[0], new_part[0, :, 0], new_part[1, :, 0]], 0)
    value_matrix = jnp.concatenate([cached[1], new_part[0, :, 1], new_part[1, :, 1]], 0)
    key_total = key_matrix.shape[0]
    query_group_width = QUERY_HEADS // KEY_VALUE_HEADS
    query_matrix = query_portion.reshape(2 * row_total, KEY_VALUE_HEADS, query_group_width, HEAD_SIZE).astype(jnp.float32)
    attention_scores = jnp.einsum('meqt,wet->eqmw', query_matrix, key_matrix.reshape(key_total, KEY_VALUE_HEADS, HEAD_SIZE).astype(jnp.float32)) * HEAD_SIZE ** (-0.5)
    position = jnp.arange(key_total, dtype=jnp.int32)[None, :]
    row_index = jnp.arange(2 * row_total, dtype=jnp.int32)[:, None]
    visible = jnp.where(position < CACHED_POSITIONS, position < length, position - CACHED_POSITIONS <= row_index)
    attention_scores = jnp.where(visible, attention_scores, jnp.float32(-1e+30))
    largest = lax.optimization_barrier(jnp.max(attention_scores, -1, keepdims=True))
    weights = jnp.where(visible, jnp.exp(attention_scores - largest), jnp.float32(0.0))
    route_probability = (weights / lax.optimization_barrier(jnp.sum(weights, -1, keepdims=True))).astype(jnp.bfloat16)
    layer_result = jnp.einsum('qizo,oqx->zqix', route_probability.astype(jnp.float32), value_matrix.reshape(key_total, KEY_VALUE_HEADS, HEAD_SIZE).astype(jnp.float32))
    return layer_result.reshape(2 * row_total, QUERY_HEADS * HEAD_SIZE).astype(jnp.bfloat16)

def expert_block(token_rows, weight):
    row_total = token_rows.shape[0]
    pieces = token_rows.reshape(row_total, N_TP, QUARTER).astype(jnp.float32)
    gate_up_w = weight[:2].reshape(2, N_TP, QUARTER, FFW).astype(jnp.float32)
    partial_value = jnp.einsum('rqc,gqcf->rgqf', pieces, gate_up_w)
    rounded = lax.optimization_barrier(partial_value.astype(jnp.bfloat16)).astype(jnp.float32)
    summed = lax.optimization_barrier(jnp.sum(rounded, 2))
    hidden = (jax.nn.silu(summed[:, 0]) * summed[:, 1]).astype(jnp.bfloat16)
    return jnp.dot(hidden, weight[2].T, preferred_element_type=jnp.float32).astype(jnp.bfloat16)

def mix_block(normed_rows, resid_rows, routed, combine, slot_of_expert, expert_weights):
    expert_marks = (routed[:, :, None] == jnp.arange(EXPERTS, dtype=jnp.int32)[None, None, :]).any(1).astype(jnp.int32)
    grouped = expert_marks.reshape(REQUEST_COUNT, REQUEST_TOKENS, EXPERTS)
    before = (jnp.cumsum(grouped, 1) - grouped).reshape(BLOCK_TOKENS, EXPERTS)
    slot_rank = jnp.take_along_axis(before, routed, 1).astype(jnp.int32)
    block_of = (jnp.arange(BLOCK_TOKENS, dtype=jnp.int32) // REQUEST_TOKENS)[:, None]
    slot_width = REQUEST_COUNT * CAP
    buffer_row = ((routed * REQUEST_COUNT + block_of) * CAP + slot_rank).astype(jnp.int32)
    token_source = jnp.repeat(jnp.arange(BLOCK_TOKENS, dtype=jnp.int32), TOP)
    token_table = jnp.zeros((EXPERTS * slot_width,), jnp.int32).at[buffer_row.reshape(-1)].set(token_source)
    token_table = token_table.reshape(EXPERTS, slot_width)

    def run_expert(expert):
        token_rows = normed_rows[token_table[expert]]
        return expert_block(token_rows, expert_weights[slot_of_expert[expert]])
    outputs = lax.map(run_expert, jnp.arange(EXPERTS, dtype=jnp.int32))
    gathered = outputs.reshape(EXPERTS * slot_width, D)[buffer_row.reshape(-1)].reshape(BLOCK_TOKENS, TOP, D)
    mixed_rows = resid_rows.astype(jnp.float32) + lax.optimization_barrier(jnp.sum(combine[:, :, None] * gathered.astype(jnp.float32), 1))
    return mixed_rows.astype(jnp.bfloat16)

def reference(hidden_states, queries, fresh_key_value, cache, cache_lengths, out_weight, router_weight, expert_weights, expert_ids, old_slots, new_slots, moved_experts):
    query_parts = queries.reshape(2, REQUEST_COUNT, REQUEST_TOKENS, QUERY_HEADS * HEAD_SIZE).transpose(1, 0, 2, 3)
    fresh_pieces_list = fresh_key_value.reshape(2, REQUEST_COUNT, REQUEST_TOKENS, 2, KEY_VALUE_HEADS * HEAD_SIZE).transpose(1, 0, 2, 3, 4)
    attention = lax.map(attend_request, (query_parts, fresh_pieces_list, cache, cache_lengths))
    attention = attention.reshape(REQUEST_COUNT, 2, REQUEST_TOKENS, QUERY_HEADS * HEAD_SIZE).transpose(1, 0, 2, 3).reshape(2 * BLOCK_TOKENS, QUERY_HEADS * HEAD_SIZE)
    attn_out = jnp.dot(attention, out_weight, preferred_element_type=jnp.float32)
    residual = (hidden_states.reshape(2 * BLOCK_TOKENS, D).astype(jnp.float32) + attn_out).astype(jnp.bfloat16)
    wide = residual.astype(jnp.float32)
    squares = lax.optimization_barrier(jnp.sum(wide * wide, 1))
    normed = (wide * lax.rsqrt(squares / D + 1e-06)[:, None]).astype(jnp.bfloat16)
    logits = jnp.dot(normed, router_weight, preferred_element_type=jnp.float32)
    routed = expert_ids.reshape(2 * BLOCK_TOKENS, TOP)
    selected = jnp.take_along_axis(logits, routed, 1)
    raised = jnp.exp(selected)
    combine = raised / lax.optimization_barrier(jnp.sum(raised, 1, keepdims=True))
    first_mix = mix_block(normed[:BLOCK_TOKENS], residual[:BLOCK_TOKENS], routed[:BLOCK_TOKENS], combine[:BLOCK_TOKENS], old_slots, expert_weights)
    source = slot_source(old_slots, new_slots, moved_experts)
    second_slot = lookup(source, new_slots)
    second_mix = mix_block(normed[BLOCK_TOKENS:], residual[BLOCK_TOKENS:], routed[BLOCK_TOKENS:], combine[BLOCK_TOKENS:], second_slot, expert_weights)
    return jnp.stack([first_mix, second_mix])
```

```python
import functools

import jax
import jax.numpy as jnp
from jax import lax
from jax.experimental import pallas as pl
from jax.experimental.pallas import tpu as pltpu
from jax.sharding import PartitionSpec as P

D = 2048
HEAD_SIZE = 128


def lookup(entries, wanted_keys):
    return jnp.sum(
        jnp.where(
            wanted_keys[..., None] == jnp.arange(entries.shape[0], dtype=jnp.int32), entries, 0
        ),
        -1,
    )


def attend_local(queries, fresh_key_value, cache, cache_lengths):
    tokens_dev = queries.shape[1]
    kv_heads = fresh_key_value.shape[3] // HEAD_SIZE
    query_group_width = queries.shape[2] // HEAD_SIZE // kv_heads
    key_matrix = jnp.concatenate(
        [cache[0, 0], fresh_key_value[0, :, 0], fresh_key_value[1, :, 0]], 0
    )
    value_matrix = jnp.concatenate(
        [cache[0, 1], fresh_key_value[0, :, 1], fresh_key_value[1, :, 1]], 0
    )
    key_total = key_matrix.shape[0]
    context = cache.shape[2]
    query_matrix = queries.reshape(2 * tokens_dev, kv_heads, query_group_width, HEAD_SIZE)
    attention_scores = jnp.einsum(
        "meqt,wet->eqmw",
        query_matrix,
        key_matrix.reshape(key_total, kv_heads, HEAD_SIZE),
        preferred_element_type=jnp.float32,
    ) * HEAD_SIZE ** (-0.5)
    position = jnp.arange(key_total, dtype=jnp.int32)[None, :]
    row_index = jnp.arange(2 * tokens_dev, dtype=jnp.int32)[:, None]
    visible = jnp.where(
        position < context, position < cache_lengths[0], position - context <= row_index
    )
    attention_scores = jnp.where(visible, attention_scores, jnp.float32(-1e30))
    largest = jnp.max(attention_scores, -1, keepdims=True)
    weights = jnp.where(visible, jnp.exp(attention_scores - largest), jnp.float32(0.0))
    route_probability = (weights / jnp.sum(weights, -1, keepdims=True)).astype(jnp.bfloat16)
    layer_result = jnp.einsum(
        "qizo,oqx->zqix",
        route_probability,
        value_matrix.reshape(key_total, kv_heads, HEAD_SIZE),
        preferred_element_type=jnp.float32,
    )
    return layer_result.reshape(2 * tokens_dev, -1).astype(jnp.bfloat16)


def run_slots(weights, received):
    gate_up = jnp.einsum(
        "secq,egqf->secgf", received, weights[:, :2], preferred_element_type=jnp.float32
    )
    summed = lax.psum(gate_up.astype(jnp.bfloat16), "tp").astype(jnp.float32)
    hidden = (jax.nn.silu(summed[:, :, :, 0]) * summed[:, :, :, 1]).astype(jnp.bfloat16)
    layer_result = jnp.einsum(
        "secf,eqf->secq", hidden, weights[:, 2], preferred_element_type=jnp.float32
    ).astype(jnp.bfloat16)
    return lax.all_to_all(layer_result, "ep", split_axis=0, concat_axis=0, tiled=True)


def mix_block(normed_rows, resid_rows, routed, combine, slot_table, weights, capacity, groups):
    tokens_dev, top_count = routed.shape
    experts = slot_table.shape[0]
    local_slots = weights.shape[0]
    quarter = normed_rows.shape[1]
    slot_index = lookup(slot_table, routed)
    picked_mask = routed[:, :, None] == jnp.arange(experts, dtype=jnp.int32)[None, None, :]
    expert_marks = picked_mask.any(1).astype(jnp.bfloat16)
    earlier = (jnp.arange(tokens_dev)[:, None] > jnp.arange(tokens_dev)[None, :]).astype(
        jnp.bfloat16
    )
    before = jnp.dot(earlier, expert_marks, preferred_element_type=jnp.float32)
    slot_rank = jnp.sum(jnp.where(picked_mask, before[:, None, :], 0.0), -1).astype(jnp.int32)
    buffer_row = (slot_index * capacity + slot_rank).reshape(-1)
    buffer_rows = (
        jnp.zeros((groups * local_slots * capacity, quarter), jnp.bfloat16)
        .at[buffer_row]
        .set(jnp.repeat(normed_rows, top_count, axis=0))
    )
    outgoing = buffer_rows.reshape(groups, local_slots, capacity, quarter)
    returned = run_slots(
        weights, lax.all_to_all(outgoing, "ep", split_axis=0, concat_axis=0, tiled=True)
    )
    gathered = returned.reshape(-1, quarter)[buffer_row].reshape(tokens_dev, top_count, quarter)
    mixed_rows = resid_rows.astype(jnp.float32) + jnp.sum(
        combine[:, :, None] * gathered.astype(jnp.float32), 1
    )
    return mixed_rows.astype(jnp.bfloat16)


MESH = pl.DeviceIdType.MESH
PIECES = 2


def line_order(planes):
    table = []
    for z in range(planes):
        table.append(
            sorted(
                range(planes),
                key=lambda t: (abs(t - z), (z if t < z else planes - 1 - z) if t != z else 0),
            )
        )
    return table


def plane_at(table, z, p):
    value = jnp.int32(0)
    for i, row in enumerate(table):
        value = value + jnp.where(z == i, jnp.int32(row[p]), 0)
    return value


def layer_kernel(
    planes,
    tokens,
    head_group,
    queries,
    fresh,
    cache,
    lengths,
    out_weight,
    hidden_states,
    router,
    experts,
    marks,
    slots,
    out,
    keys,
    values,
    bias,
    attention,
    out_blocks,
    hidden_in,
    kept,
    parts_out,
    parts_in,
    resid,
    gate_up,
    down,
    routers,
    all_marks,
    hidden,
    product,
    own_total,
    core_out,
    core_in,
    line_out,
    line_in,
    local_sem,
    weight_send,
    weight_recv,
    router_send,
    router_recv,
    rows_send,
    rows_recv,
    heads_send,
    heads_recv,
    marks_send,
    marks_recv,
    block_line_send,
    block_line_recv,
    block_rep_send,
    block_rep_recv,
    parts_send,
    parts_recv,
    piece_line_send,
    piece_line_recv,
    piece_tp_send,
    piece_tp_recv,
    piece_core_send,
    piece_core_recv,
    hidden_send,
    hidden_recv,
    core_send,
    core_recv,
    line_send,
    line_recv,
):
    y, e, x = lax.axis_index("rep"), lax.axis_index("ep"), lax.axis_index("tp")
    z, c = e // 2, e % 2
    group = 2 * planes
    half_planes = planes // 2
    table = line_order(planes)
    width = out_weight.shape[1]
    depth = out_weight.shape[0]
    half = hidden_states.shape[1]
    has = (z > 0, z < planes - 1)
    beside = (e - 2, e + 2)
    tp_mate = (y, e, 1 - x)
    rep_mate = (1 - y, e, x)
    mate = e + 1 - 2 * c
    core_mate = (y, mate, x)
    chunk = depth // 2 // PIECES
    own_rows = pl.ds(pl.multiple_of(c * tokens, tokens), tokens)
    mate_rows = pl.ds(pl.multiple_of((1 - c) * tokens, tokens), tokens)

    def remote(src, dst, send, recv, target):
        return pltpu.make_async_remote_copy(
            src_ref=src,
            dst_ref=dst,
            send_sem=send,
            recv_sem=recv,
            device_id=target,
            device_id_type=MESH,
        )

    context = cache.shape[2]
    local = [
        pltpu.make_async_copy(cache.at[0, 0], keys.at[pl.ds(0, context)], local_sem.at[0]),
        pltpu.make_async_copy(cache.at[0, 1], values.at[pl.ds(0, context)], local_sem.at[1]),
        pltpu.make_async_copy(fresh.at[0], keys.at[pl.ds(context, tokens)], local_sem.at[2]),
        pltpu.make_async_copy(fresh.at[1], values.at[pl.ds(context, tokens)], local_sem.at[3]),
    ]
    late = [
        pltpu.make_async_copy(out_weight, out_blocks.at[z], local_sem.at[4]),
        pltpu.make_async_copy(hidden_states, hidden_in.at[own_rows], local_sem.at[5]),
        pltpu.make_async_copy(
            experts.at[x, pl.ds(0, 2)],
            gate_up.at[:, pl.ds(pl.multiple_of(x * half, half), half)],
            local_sem.at[6],
        ),
        pltpu.make_async_copy(experts.at[0, 2], down.at[0], local_sem.at[7]),
        pltpu.make_async_copy(experts.at[1, 2], down.at[1], local_sem.at[8]),
        pltpu.make_async_copy(
            router, routers.at[:, pl.ds(pl.multiple_of(x * half, half), half)], local_sem.at[9]
        ),
        pltpu.make_async_copy(marks, all_marks.at[e], local_sem.at[10]),
    ]
    for copy in local:
        copy.start()

    barrier = pltpu.get_barrier_semaphore()
    for step in range(1, group):
        pl.semaphore_signal(
            barrier, inc=1, device_id=(y, (e + step) % group, x), device_id_type=MESH
        )
    pl.semaphore_signal(barrier, inc=1, device_id=tp_mate, device_id_type=MESH)
    pl.semaphore_signal(barrier, inc=1, device_id=rep_mate, device_id_type=MESH)
    pl.semaphore_wait(barrier, group + 1)

    def block_chunk(block, side, s):
        return out_blocks.at[
            block, pl.ds(pl.multiple_of(side * (depth // 2) + s * chunk, chunk), chunk)
        ]

    def block_line(block, s, way):
        piece = block_chunk(block, y, s)
        return remote(
            piece,
            piece,
            block_line_send.at[way, block, s],
            block_line_recv.at[block, s],
            (y, beside[way], x),
        )

    def block_own(s, way):
        return remote(
            out_weight.at[pl.ds(pl.multiple_of(y * (depth // 2) + s * chunk, chunk), chunk)],
            block_chunk(z, y, s),
            block_line_send.at[way, z, s],
            block_line_recv.at[z, s],
            (y, beside[way], x),
        )

    def block_rep(block, side, s):
        piece = block_chunk(block, side, s)
        return remote(piece, piece, block_rep_send.at[block, s], block_rep_recv.at[block, s], rep_mate)

    for s in range(PIECES):
        for way in range(2):
            pl.when(has[way])(block_own(s, way).start)
    rows_copy = remote(hidden_states, hidden_in.at[own_rows], rows_send, rows_recv, core_mate)
    rows_copy.start()
    marks_copies = []
    for step in range(1, group):
        copy = remote(
            marks,
            all_marks.at[e],
            marks_send.at[step - 1],
            marks_recv.at[step - 1],
            (y, (e + step) % group, x),
        )
        copy.start()
        marks_copies.append(copy)
    router_copy = remote(
        router,
        routers.at[:, pl.ds(pl.multiple_of(x * half, half), half)],
        router_send,
        router_recv,
        tp_mate,
    )
    router_copy.start()
    weight_copy = remote(
        experts.at[1 - x, pl.ds(0, 2)],
        gate_up.at[:, pl.ds(pl.multiple_of(x * half, half), half)],
        weight_send,
        weight_recv,
        tp_mate,
    )
    weight_copy.start()
    for copy in late:
        copy.start()

    key_total = keys.shape[0]
    position = lax.broadcasted_iota(jnp.int32, (tokens, key_total), 1)
    row = lax.broadcasted_iota(jnp.int32, (tokens, key_total), 0)
    visible = jnp.where(
        position < context,
        (position < lengths[0]).astype(jnp.int32),
        (position - context <= row).astype(jnp.int32),
    )
    bias[...] = jnp.where(visible > 0, jnp.float32(0.0), jnp.float32(-1e30))
    for copy in local:
        copy.wait()
    kv_heads = keys.shape[1] // HEAD_SIZE

    def attend(kv):
        key_part = keys[:, kv * HEAD_SIZE : (kv + 1) * HEAD_SIZE]
        value_part = values[:, kv * HEAD_SIZE : (kv + 1) * HEAD_SIZE]

        def one(q, _):
            column = pl.ds(
                pl.multiple_of((kv * head_group + q) * HEAD_SIZE, HEAD_SIZE), HEAD_SIZE
            )
            query = queries[:, column]
            scores = (
                lax.dot_general(
                    query, key_part, (((1,), (1,)), ((), ())), preferred_element_type=jnp.float32
                )
                * HEAD_SIZE ** (-0.5)
                + bias[...]
            )
            raised = jnp.exp(scores - jnp.max(scores, -1, keepdims=True))
            total = jnp.sum(raised, -1, keepdims=True)
            mixed = jnp.dot(
                raised.astype(jnp.bfloat16), value_part, preferred_element_type=jnp.float32
            )
            attention[own_rows, column] = (mixed / total).astype(jnp.bfloat16)
            return 0

        lax.fori_loop(0, head_group, one, 0)

    for kv in range(kv_heads):
        attend(kv)
    heads_copy = remote(
        attention.at[own_rows], attention.at[own_rows], heads_send, heads_recv, core_mate
    )
    heads_copy.start()

    def column_block(side, core, b):
        return 2 * (half_planes * side + b) + core

    def piece(t, side, core, b):
        start = pl.multiple_of(column_block(side, core, b) * width, width)
        return resid.at[t, :, pl.ds(start, width)]

    def piece_line(t, b, way):
        ref = piece(t, x, c, b)
        return remote(
            ref,
            ref,
            piece_line_send.at[way, t, b],
            piece_line_recv.at[t, b],
            (y, beside[way], x),
        )

    def piece_tp(t, b, side):
        ref = piece(t, side, c, b)
        return remote(ref, ref, piece_tp_send.at[t, b], piece_tp_recv.at[t, b], tp_mate)

    def piece_core(t, b, kind, core):
        ref = piece(t, x if kind == 0 else 1 - x, core, b)
        return remote(
            ref, ref, piece_core_send.at[kind, t, b], piece_core_recv.at[kind, t, b], core_mate
        )

    def parts_copy(b):
        return remote(parts_out.at[b], parts_in.at[b], parts_send.at[b], parts_recv.at[b], tp_mate)

    def project(p):
        block = plane_at(table, z, p)
        if p == 0:
            late[0].wait()
            heads_copy.wait_recv()
        else:
            for s in range(PIECES):
                block_rep(block, 1 - y, s).wait_recv()
        part = jnp.dot(attention[...], out_blocks[block], preferred_element_type=jnp.float32)
        b = block % half_planes
        mine = block // half_planes == x

        @pl.when(mine)
        def _():
            kept[b] = part

        @pl.when(block // half_planes != x)
        def _():
            parts_out[b] = part.astype(jnp.bfloat16)
            parts_copy(b).start()

    def settle(p):
        block = plane_at(table, z, p)
        b = block % half_planes

        @pl.when(block // half_planes == x)
        def _():
            parts_copy(b).wait_recv()
            start = pl.multiple_of((2 * b + c) * width, width)
            summed = (
                hidden_in[:, pl.ds(start, width)].astype(jnp.float32)
                + kept[b]
                + parts_in[b].astype(jnp.float32)
            )
            target = pl.multiple_of(column_block(x, c, b) * width, width)
            resid[z, :, pl.ds(target, width)] = summed.astype(jnp.bfloat16)
            for way in range(2):
                pl.when(has[way])(piece_line(z, b, way).start)
            piece_tp(z, b, x).start()
            piece_core(z, b, 0, c).start()

    late[1].wait()
    rows_copy.wait_recv()
    for p in range(1, planes + 1):
        if p < planes:
            block = plane_at(table, z, p)
            for s in range(PIECES):
                block_line(block, s, 0).wait_recv()
                pl.when((block > z) & has[0])(block_line(block, s, 0).start)
                pl.when((block < z) & has[1])(block_line(block, s, 1).start)
                block_rep(block, y, s).start()
        if p >= 2:
            settle(p - 2)
        project(p - 1)
    settle(planes - 1)

    for p in range(1, planes + 1):
        if p < planes:
            t = plane_at(table, z, p)
            for b in range(half_planes):
                piece_line(t, b, 0).wait_recv()
                pl.when((t > z) & has[0])(piece_line(t, b, 0).start)
                pl.when((t < z) & has[1])(piece_line(t, b, 1).start)
                piece_tp(t, b, x).start()
                piece_core(t, b, 0, c).start()
        t = plane_at(table, z, p - 1)
        for b in range(half_planes):
            piece_tp(t, b, 1 - x).wait_recv()
            piece_core(t, b, 1, c).start()

    for copy in late[2:]:
        copy.wait()
    weight_copy.wait_recv()
    router_copy.wait_recv()
    for copy in marks_copies:
        copy.wait_recv()
    number = router.shape[0]
    eye = (
        lax.broadcasted_iota(jnp.int32, (number, number), 0)
        == lax.broadcasted_iota(jnp.int32, (number, number), 1)
    ).astype(jnp.bfloat16)

    def hidden_copy(t, side):
        ref = hidden.at[side, t]
        return remote(ref, ref, hidden_send.at[t], hidden_recv.at[t], tp_mate)

    def open_plane(t):
        for b in range(half_planes):
            for kind in range(2):
                piece_core(t, b, kind, 1 - c).wait_recv()
        rows = resid[t]
        wide = rows.astype(jnp.float32)
        scale = lax.rsqrt(jnp.sum(wide * wide, 1, keepdims=True) / D + 1e-06)
        gate = jnp.dot(rows, gate_up[0], preferred_element_type=jnp.float32) * scale
        up = jnp.dot(rows, gate_up[1], preferred_element_type=jnp.float32) * scale
        logits = (
            lax.dot_general(
                rows, routers[...], (((1,), (1,)), ((), ())), preferred_element_type=jnp.float32
            )
            * scale
        )
        chosen = jnp.concatenate(
            [
                lax.dot_general(
                    all_marks[2 * t + core],
                    eye,
                    (((0,), (0,)), ((), ())),
                    preferred_element_type=jnp.float32,
                )
                for core in range(2)
            ],
            0,
        )
        raised = jnp.where(chosen > 0.5, jnp.exp(logits), 0.0)
        share = jnp.sum(
            jnp.where(slots[...] == 2 * e + x, raised, 0.0), 1, keepdims=True
        ) / jnp.sum(raised, 1, keepdims=True)
        hidden[x, t] = (gate / (1.0 + jnp.exp(-gate)) * up * share).astype(jnp.bfloat16)
        hidden_copy(t, x).start()

    for p in reversed(range(planes)):
        open_plane(plane_at(table, z, p))

    def core_copy(t):
        return remote(core_out.at[t], core_in.at[t], core_send.at[t], core_recv.at[t], core_mate)

    def line_copy(t, way):
        return remote(
            line_out.at[t],
            line_in.at[way, t],
            line_send.at[t],
            line_recv.at[way, t],
            (y, beside[way], x),
        )

    def close_plane(t):
        hidden_copy(t, 1 - x).wait_recv()
        product[...] = lax.dot_general(
            hidden[0, t], down[0], (((1,), (1,)), ((), ())), preferred_element_type=jnp.float32
        ) + lax.dot_general(
            hidden[1, t], down[1], (((1,), (1,)), ((), ())), preferred_element_type=jnp.float32
        )
        core_out[t] = product[mate_rows].astype(jnp.bfloat16)
        core_copy(t).start()
        own_total[t] = product[own_rows]

    def pass_on(t):
        core_copy(t).wait_recv()
        own_total[t] += core_in[t].astype(jnp.float32)

        @pl.when((t >= z) & has[0])
        def _():
            line_copy(t, 1).wait_recv()
            own_total[t] += line_in[1, t].astype(jnp.float32)

        @pl.when((t <= z) & has[1])
        def _():
            line_copy(t, 0).wait_recv()
            own_total[t] += line_in[0, t].astype(jnp.float32)

        @pl.when(t > z)
        def _():
            line_out[t] = own_total[t].astype(jnp.bfloat16)
            line_copy(t, 1).start()

        @pl.when(t < z)
        def _():
            line_out[t] = own_total[t].astype(jnp.bfloat16)
            line_copy(t, 0).start()

    for p in reversed(range(planes)):
        close_plane(plane_at(table, z, p))
        if p + 1 < planes:
            pass_on(plane_at(table, z, p + 1))
    pass_on(z)
    own_resid = resid[z, own_rows, pl.ds(pl.multiple_of(x * half, half), half)]
    out[...] = (own_resid.astype(jnp.float32) + own_total[z]).astype(jnp.bfloat16)

    rows_copy.wait_send()
    heads_copy.wait_send()
    router_copy.wait_send()
    weight_copy.wait_send()
    for copy in marks_copies:
        copy.wait_send()
    for s in range(PIECES):
        for way in range(2):
            pl.when(has[way])(block_own(s, way).wait_send)
    for p in range(1, planes):
        t = plane_at(table, z, p)
        for s in range(PIECES):
            pl.when((t > z) & has[0])(block_line(t, s, 0).wait_send)
            pl.when((t < z) & has[1])(block_line(t, s, 1).wait_send)
            block_rep(t, y, s).wait_send()
        for b in range(half_planes):
            pl.when((t > z) & has[0])(piece_line(t, b, 0).wait_send)
            pl.when((t < z) & has[1])(piece_line(t, b, 1).wait_send)
        pl.when(t > z)(line_copy(t, 1).wait_send)
        pl.when(t < z)(line_copy(t, 0).wait_send)
    for b in range(half_planes):
        parts_copy(b).wait_send()
        for way in range(2):
            pl.when(has[way])(piece_line(z, b, way).wait_send)
    for t in range(planes):
        for b in range(half_planes):
            piece_tp(t, b, x).wait_send()
            piece_core(t, b, 0, c).wait_send()
            piece_core(t, b, 1, c).wait_send()
        hidden_copy(t, x).wait_send()
        core_copy(t).wait_send()


def one_kernel_layer(
    hidden_states, queries, fresh_key_value, cache, lengths, out_weight, router, experts, routed, slots
):
    group = lax.axis_size("ep")
    planes = group // 2
    half_planes = planes // 2
    tokens, half = hidden_states.shape
    depth, width = out_weight.shape
    number = router.shape[1]
    kv_width = cache.shape[3]
    key_total = cache.shape[2] + tokens
    units = experts.shape[3]
    fresh = jnp.moveaxis(fresh_key_value, 2, 0).reshape(2, tokens, kv_width)
    ids = jnp.arange(number, dtype=jnp.int32)[:, None, None]
    marks = (routed.T[None] == ids).any(1).astype(jnp.bfloat16)
    vmem, anywhere = (pl.BlockSpec(memory_space=m) for m in (pltpu.VMEM, pl.ANY))
    dma = pltpu.SemaphoreType.DMA
    bf16, f32 = jnp.bfloat16, jnp.float32
    return pl.pallas_call(
        functools.partial(layer_kernel, planes, tokens, queries.shape[1] // kv_width),
        out_shape=jax.ShapeDtypeStruct((tokens, half), bf16),
        in_specs=[
            vmem,
            anywhere,
            anywhere,
            pl.BlockSpec(memory_space=pltpu.SMEM),
            anywhere,
            anywhere,
            vmem,
            anywhere,
            vmem,
            vmem,
        ],
        out_specs=vmem,
        scratch_shapes=[
            pltpu.VMEM((key_total, kv_width), bf16),
            pltpu.VMEM((key_total, kv_width), bf16),
            pltpu.VMEM((tokens, key_total), f32),
            pltpu.VMEM((2 * tokens, depth), bf16),
            pltpu.VMEM((planes, depth, width), bf16),
            pltpu.VMEM((2 * tokens, half), bf16),
            pltpu.VMEM((half_planes, 2 * tokens, width), f32),
            pltpu.VMEM((half_planes, 2 * tokens, width), bf16),
            pltpu.VMEM((half_planes, 2 * tokens, width), bf16),
            pltpu.VMEM((planes, 2 * tokens, 2 * half), bf16),
            pltpu.VMEM((2, 2 * half, units), bf16),
            pltpu.VMEM((2, half, units), bf16),
            pltpu.VMEM((number, 2 * half), bf16),
            pltpu.VMEM((group, number, tokens), bf16),
            pltpu.VMEM((2, planes, 2 * tokens, units), bf16),
            pltpu.VMEM((2 * tokens, half), f32),
            pltpu.VMEM((planes, tokens, half), f32),
            pltpu.VMEM((planes, tokens, half), bf16),
            pltpu.VMEM((planes, tokens, half), bf16),
            pltpu.VMEM((planes, tokens, half), bf16),
            pltpu.VMEM((2, planes, tokens, half), bf16),
            dma((11,)),
            dma,
            dma,
            dma,
            dma,
            dma,
            dma,
            dma,
            dma,
            dma((group - 1,)),
            dma((group - 1,)),
            dma((2, planes, PIECES)),
            dma((planes, PIECES)),
            dma((planes, PIECES)),
            dma((planes, PIECES)),
            dma((half_planes,)),
            dma((half_planes,)),
            dma((2, planes, half_planes)),
            dma((planes, half_planes)),
            dma((planes, half_planes)),
            dma((planes, half_planes)),
            dma((2, planes, half_planes)),
            dma((2, planes, half_planes)),
            dma((planes,)),
            dma((planes,)),
            dma((planes,)),
            dma((planes,)),
            dma((planes,)),
            dma((2, planes)),
        ],
        compiler_params=pltpu.CompilerParams(
            collective_id=0, has_side_effects=True, vmem_limit_bytes=56 * 1024 * 1024
        ),
    )(
        queries,
        fresh,
        cache,
        lengths,
        out_weight,
        hidden_states,
        router.T,
        experts,
        marks,
        slots.reshape(1, number),
    )


def per_device(
    hidden_states,
    queries,
    fresh_key_value,
    cache,
    cache_lengths,
    out_weight,
    router_weight,
    expert_weights,
    expert_ids,
    old_slots,
    new_slots,
    moved_experts,
):
    tokens_dev = hidden_states.shape[1]
    quarter = hidden_states.shape[2]
    experts = router_weight.shape[1]
    top_count = expert_ids.shape[2]
    groups = lax.axis_size("ep")
    local_slots = expert_weights.shape[0]
    capacity = min(tokens_dev, 3 * tokens_dev * top_count // (2 * experts))
    routed = expert_ids.reshape(2 * tokens_dev, top_count)
    if (
        lax.axis_size("rep") == 2
        and lax.axis_size("tp") == 2
        and groups == 8
        and local_slots == 2
        and tokens_dev % 16 == 0
    ):
        mixed = one_kernel_layer(
            hidden_states.reshape(2 * tokens_dev, quarter),
            queries.reshape(2 * tokens_dev, queries.shape[2]),
            fresh_key_value,
            cache,
            cache_lengths,
            out_weight,
            router_weight,
            expert_weights,
            routed,
            old_slots,
        )
        return mixed.reshape(2, tokens_dev, quarter)
    attention = attend_local(queries, fresh_key_value, cache, cache_lengths)
    head_terms = jnp.dot(
        attention,
        lax.all_gather(out_weight, "ep", axis=1, tiled=True),
        preferred_element_type=jnp.float32,
    )
    attn_out = lax.psum_scatter(
        head_terms.astype(jnp.bfloat16), "tp", scatter_dimension=1, tiled=True
    ).astype(jnp.float32)
    residual = (
        hidden_states.reshape(2 * tokens_dev, quarter).astype(jnp.float32) + attn_out
    ).astype(jnp.bfloat16)
    wide = residual.astype(jnp.float32)
    squares = lax.psum(jnp.sum(wide * wide, 1), "tp")
    normed = (wide * lax.rsqrt(squares / D + 1e-06)[:, None]).astype(jnp.bfloat16)
    logits = lax.psum(
        jnp.dot(normed, router_weight, preferred_element_type=jnp.float32).astype(jnp.bfloat16),
        "tp",
    ).astype(jnp.float32)
    selected = jnp.sum(
        jnp.where(
            routed[:, :, None] == jnp.arange(experts, dtype=jnp.int32)[None, None, :],
            logits[:, None, :],
            0.0,
        ),
        -1,
    )
    raised = jnp.exp(selected)
    combine = raised / jnp.sum(raised, 1, keepdims=True)
    outputs = []
    for lower in (0, tokens_dev):
        upper = lower + tokens_dev
        outputs.append(
            mix_block(
                normed[lower:upper],
                residual[lower:upper],
                routed[lower:upper],
                combine[lower:upper],
                old_slots,
                expert_weights,
                capacity,
                groups,
            )
        )
    return jnp.stack(outputs)


def solution(mesh):
    return jax.shard_map(
        per_device,
        mesh=mesh,
        in_specs=(
            P(None, ("rep", "ep"), "tp"),
            P(None, ("rep", "ep"), "tp"),
            P(None, ("rep", "ep"), None, "tp"),
            P(("rep", "ep"), None, None, "tp"),
            P(("rep", "ep")),
            P("tp", "ep"),
            P("tp", None),
            P("ep", None, "tp", None),
            P(None, ("rep", "ep"), None),
            P(),
            P(),
            P(),
        ),
        out_specs=P(None, ("rep", "ep"), "tp"),
        check_vma=False,
    )
```

```python
import functools

import jax
import jax.numpy as jnp
from jax import lax
from jax.experimental import pallas as pl
from jax.experimental.pallas import tpu as pltpu
from jax.sharding import PartitionSpec as P

D = 2048
HEAD_SIZE = 128


def lookup(entries, wanted_keys):
    return jnp.sum(
        jnp.where(
            wanted_keys[..., None] == jnp.arange(entries.shape[0], dtype=jnp.int32), entries, 0
        ),
        -1,
    )


def attend_local(queries, fresh_key_value, cache, cache_lengths):
    tokens_dev = queries.shape[1]
    kv_heads = fresh_key_value.shape[3] // HEAD_SIZE
    query_group_width = queries.shape[2] // HEAD_SIZE // kv_heads
    key_matrix = jnp.concatenate(
        [cache[0, 0], fresh_key_value[0, :, 0], fresh_key_value[1, :, 0]], 0
    )
    value_matrix = jnp.concatenate(
        [cache[0, 1], fresh_key_value[0, :, 1], fresh_key_value[1, :, 1]], 0
    )
    key_total = key_matrix.shape[0]
    context = cache.shape[2]
    query_matrix = queries.reshape(2 * tokens_dev, kv_heads, query_group_width, HEAD_SIZE)
    attention_scores = jnp.einsum(
        "meqt,wet->eqmw",
        query_matrix,
        key_matrix.reshape(key_total, kv_heads, HEAD_SIZE),
        preferred_element_type=jnp.float32,
    ) * HEAD_SIZE ** (-0.5)
    position = jnp.arange(key_total, dtype=jnp.int32)[None, :]
    row_index = jnp.arange(2 * tokens_dev, dtype=jnp.int32)[:, None]
    visible = jnp.where(
        position < context, position < cache_lengths[0], position - context <= row_index
    )
    attention_scores = jnp.where(visible, attention_scores, jnp.float32(-1e30))
    largest = jnp.max(attention_scores, -1, keepdims=True)
    weights = jnp.where(visible, jnp.exp(attention_scores - largest), jnp.float32(0.0))
    route_probability = (weights / jnp.sum(weights, -1, keepdims=True)).astype(jnp.bfloat16)
    layer_result = jnp.einsum(
        "qizo,oqx->zqix",
        route_probability,
        value_matrix.reshape(key_total, kv_heads, HEAD_SIZE),
        preferred_element_type=jnp.float32,
    )
    return layer_result.reshape(2 * tokens_dev, -1).astype(jnp.bfloat16)


def run_slots(weights, received):
    gate_up = jnp.einsum(
        "secq,egqf->secgf", received, weights[:, :2], preferred_element_type=jnp.float32
    )
    summed = lax.psum(gate_up.astype(jnp.bfloat16), "tp").astype(jnp.float32)
    hidden = (jax.nn.silu(summed[:, :, :, 0]) * summed[:, :, :, 1]).astype(jnp.bfloat16)
    layer_result = jnp.einsum(
        "secf,eqf->secq", hidden, weights[:, 2], preferred_element_type=jnp.float32
    ).astype(jnp.bfloat16)
    return lax.all_to_all(layer_result, "ep", split_axis=0, concat_axis=0, tiled=True)


def mix_block(normed_rows, resid_rows, routed, combine, slot_table, weights, capacity, groups):
    tokens_dev, top_count = routed.shape
    experts = slot_table.shape[0]
    local_slots = weights.shape[0]
    quarter = normed_rows.shape[1]
    slot_index = lookup(slot_table, routed)
    picked_mask = routed[:, :, None] == jnp.arange(experts, dtype=jnp.int32)[None, None, :]
    expert_marks = picked_mask.any(1).astype(jnp.bfloat16)
    earlier = (jnp.arange(tokens_dev)[:, None] > jnp.arange(tokens_dev)[None, :]).astype(
        jnp.bfloat16
    )
    before = jnp.dot(earlier, expert_marks, preferred_element_type=jnp.float32)
    slot_rank = jnp.sum(jnp.where(picked_mask, before[:, None, :], 0.0), -1).astype(jnp.int32)
    buffer_row = (slot_index * capacity + slot_rank).reshape(-1)
    buffer_rows = (
        jnp.zeros((groups * local_slots * capacity, quarter), jnp.bfloat16)
        .at[buffer_row]
        .set(jnp.repeat(normed_rows, top_count, axis=0))
    )
    outgoing = buffer_rows.reshape(groups, local_slots, capacity, quarter)
    returned = run_slots(
        weights, lax.all_to_all(outgoing, "ep", split_axis=0, concat_axis=0, tiled=True)
    )
    gathered = returned.reshape(-1, quarter)[buffer_row].reshape(tokens_dev, top_count, quarter)
    mixed_rows = resid_rows.astype(jnp.float32) + jnp.sum(
        combine[:, :, None] * gathered.astype(jnp.float32), 1
    )
    return mixed_rows.astype(jnp.bfloat16)


MESH = pl.DeviceIdType.MESH
PIECES = 4
LINE_PIECES = 2
WEIGHT_PIECES = 2


def line_order(planes):
    table = []
    for z in range(planes):
        table.append(
            sorted(
                range(planes),
                key=lambda t: (abs(t - z), (z if t < z else planes - 1 - z) if t != z else 0),
            )
        )
    return table


def plane_at(table, z, p):
    value = jnp.int32(0)
    for i, row in enumerate(table):
        value = value + jnp.where(z == i, jnp.int32(row[p]), 0)
    return value


def layer_kernel(
    planes,
    tokens,
    head_group,
    queries,
    fresh,
    cache,
    lengths,
    out_weight,
    hidden_states,
    router,
    experts,
    routed,
    slots,
    out,
    keys,
    values,
    bias,
    attention,
    out_blocks,
    hidden_in,
    kept,
    parts_out,
    parts_in,
    resid,
    gate_up,
    down,
    routers,
    all_marks,
    hidden,
    product,
    own_total,
    core_out,
    core_in,
    line_out,
    line_in,
    local_sem,
    weight_send,
    weight_recv,
    weight_rep_send,
    weight_rep_recv,
    router_send,
    router_recv,
    rows_send,
    rows_recv,
    heads_send,
    heads_recv,
    marks_send,
    marks_recv,
    block_line_send,
    block_line_recv,
    block_rep_send,
    block_rep_recv,
    parts_send,
    parts_recv,
    piece_line_send,
    piece_line_recv,
    piece_tp_send,
    piece_tp_recv,
    piece_core_send,
    piece_core_recv,
    hidden_send,
    hidden_recv,
    core_send,
    core_recv,
    line_send,
    line_recv,
):
    y, e, x = lax.axis_index("rep"), lax.axis_index("ep"), lax.axis_index("tp")
    z, c = e // 2, e % 2
    group = 2 * planes
    half_planes = planes // 2
    table = line_order(planes)
    width = out_weight.shape[1]
    depth = out_weight.shape[0]
    half = hidden_states.shape[1]
    has = (z > 0, z < planes - 1)
    beside = (e - 2, e + 2)
    tp_mate = (y, e, 1 - x)
    rep_mate = (1 - y, e, x)
    mate = e + 1 - 2 * c
    core_mate = (y, mate, x)
    chunk = depth // 2 // PIECES
    own_rows = pl.ds(pl.multiple_of(c * tokens, tokens), tokens)
    mate_rows = pl.ds(pl.multiple_of((1 - c) * tokens, tokens), tokens)

    def remote(src, dst, send, recv, target):
        return pltpu.make_async_remote_copy(
            src_ref=src,
            dst_ref=dst,
            send_sem=send,
            recv_sem=recv,
            device_id=target,
            device_id_type=MESH,
        )

    barrier = pltpu.get_barrier_semaphore()
    for step in range(1, group):
        pl.semaphore_signal(
            barrier, inc=1, device_id=(y, (e + step) % group, x), device_id_type=MESH
        )
    pl.semaphore_signal(barrier, inc=1, device_id=tp_mate, device_id_type=MESH)
    pl.semaphore_signal(barrier, inc=1, device_id=rep_mate, device_id_type=MESH)

    context = cache.shape[2]
    local = [
        pltpu.make_async_copy(cache.at[0, 0], keys.at[pl.ds(0, context)], local_sem.at[0]),
        pltpu.make_async_copy(cache.at[0, 1], values.at[pl.ds(0, context)], local_sem.at[1]),
        pltpu.make_async_copy(fresh.at[0], keys.at[pl.ds(context, tokens)], local_sem.at[2]),
        pltpu.make_async_copy(fresh.at[1], values.at[pl.ds(context, tokens)], local_sem.at[3]),
    ]
    late = [
        pltpu.make_async_copy(out_weight, out_blocks.at[z], local_sem.at[4]),
        pltpu.make_async_copy(hidden_states, hidden_in.at[own_rows], local_sem.at[5]),
        pltpu.make_async_copy(
            experts.at[x, pl.ds(0, 2)],
            gate_up.at[:, pl.ds(pl.multiple_of(x * half, half), half)],
            local_sem.at[6],
        ),
        pltpu.make_async_copy(experts.at[0, 2], down.at[0], local_sem.at[7]),
        pltpu.make_async_copy(experts.at[1, 2], down.at[1], local_sem.at[8]),
        pltpu.make_async_copy(
            router, routers.at[:, pl.ds(pl.multiple_of(x * half, half), half)], local_sem.at[9]
        ),
    ]
    for copy in local:
        copy.start()

    number = router.shape[0]
    eye = (
        lax.broadcasted_iota(jnp.int32, (number, number), 0)
        == lax.broadcasted_iota(jnp.int32, (number, number), 1)
    ).astype(jnp.bfloat16)
    blocks, top_count, block_tokens = routed.shape
    expert = lax.broadcasted_iota(jnp.int32, (number, block_tokens), 0)
    for block in range(blocks):
        named = jnp.zeros((number, block_tokens), jnp.int32)
        for k in range(top_count):
            named += (routed[block, k : k + 1, :] == expert).astype(jnp.int32)
        all_marks[e, :, block * block_tokens : (block + 1) * block_tokens] = named.astype(
            jnp.float32
        ).astype(jnp.bfloat16)

    pl.semaphore_wait(barrier, group + 1)

    def block_chunk(block, side, s):
        return out_blocks.at[
            block, pl.ds(pl.multiple_of(side * (depth // 2) + s * chunk, chunk), chunk)
        ]

    def block_line(block, s, way):
        piece = block_chunk(block, y, s)
        return remote(
            piece,
            piece,
            block_line_send.at[way, block, s],
            block_line_recv.at[block, s],
            (y, beside[way], x),
        )

    def block_own(s, way):
        return remote(
            out_weight.at[pl.ds(pl.multiple_of(y * (depth // 2) + s * chunk, chunk), chunk)],
            block_chunk(z, y, s),
            block_line_send.at[way, z, s],
            block_line_recv.at[z, s],
            (y, beside[way], x),
        )

    def block_rep(block, side, s):
        piece = block_chunk(block, side, s)
        return remote(piece, piece, block_rep_send.at[block, s], block_rep_recv.at[block, s], rep_mate)

    for s in range(PIECES):
        for way in range(2):
            pl.when(has[way])(block_own(s, way).start)
    rows_copy = remote(hidden_states, hidden_in.at[own_rows], rows_send, rows_recv, core_mate)
    rows_copy.start()
    marks_copies = []
    for step in range(1, group):
        copy = remote(
            all_marks.at[e],
            all_marks.at[e],
            marks_send.at[step - 1],
            marks_recv.at[step - 1],
            (y, (e + step) % group, x),
        )
        copy.start()
        marks_copies.append(copy)
    router_copy = remote(
        router,
        routers.at[:, pl.ds(pl.multiple_of(x * half, half), half)],
        router_send,
        router_recv,
        tp_mate,
    )
    router_copy.start()
    share_rows = half // (2 * WEIGHT_PIECES)

    def weight_share(kind, s, tp_side, rep_side):
        start = tp_side * half + (rep_side * WEIGHT_PIECES + s) * share_rows
        return gate_up.at[kind, pl.ds(pl.multiple_of(start, share_rows), share_rows)]

    def weight_tp(kind, s):
        start = pl.multiple_of((y * WEIGHT_PIECES + s) * share_rows, share_rows)
        return remote(
            experts.at[1 - x, kind, pl.ds(start, share_rows)],
            weight_share(kind, s, x, y),
            weight_send.at[kind, s],
            weight_recv.at[kind, s],
            tp_mate,
        )

    def weight_rep(kind, s, side):
        ref = weight_share(kind, s, 1 - x, side)
        return remote(
            ref, ref, weight_rep_send.at[kind, s], weight_rep_recv.at[kind, s], rep_mate
        )

    weight_list = [(kind, s) for s in range(WEIGHT_PIECES) for kind in range(2)]
    for kind, s in weight_list:
        weight_tp(kind, s).start()
    for copy in late:
        copy.start()

    key_total = keys.shape[0]
    position = lax.broadcasted_iota(jnp.int32, (tokens, key_total), 1)
    row = lax.broadcasted_iota(jnp.int32, (tokens, key_total), 0)
    visible = jnp.where(
        position < context,
        (position < lengths[0]).astype(jnp.int32),
        (position - context <= row).astype(jnp.int32),
    )
    bias[...] = jnp.where(visible > 0, jnp.float32(0.0), jnp.float32(-1e30))
    for copy in local:
        copy.wait()
    kv_heads = keys.shape[1] // HEAD_SIZE

    def attend(kv):
        key_part = keys[:, kv * HEAD_SIZE : (kv + 1) * HEAD_SIZE]
        value_part = values[:, kv * HEAD_SIZE : (kv + 1) * HEAD_SIZE]

        def one(q, _):
            column = pl.ds(
                pl.multiple_of((kv * head_group + q) * HEAD_SIZE, HEAD_SIZE), HEAD_SIZE
            )
            query = queries[:, column]
            scores = (
                lax.dot_general(
                    query, key_part, (((1,), (1,)), ((), ())), preferred_element_type=jnp.float32
                )
                * HEAD_SIZE ** (-0.5)
                + bias[...]
            )
            raised = jnp.exp(scores - jnp.max(scores, -1, keepdims=True))
            total = jnp.sum(raised, -1, keepdims=True)
            mixed = jnp.dot(
                raised.astype(jnp.bfloat16), value_part, preferred_element_type=jnp.float32
            )
            attention[own_rows, column] = (mixed / total).astype(jnp.bfloat16)
            return 0

        lax.fori_loop(0, head_group, one, 0)

    for kv in range(kv_heads):
        attend(kv)
    heads_copy = remote(
        attention.at[own_rows], attention.at[own_rows], heads_send, heads_recv, core_mate
    )
    heads_copy.start()

    def column_block(side, core, b):
        return 2 * (half_planes * side + b) + core

    def piece(t, side, core, b):
        start = pl.multiple_of(column_block(side, core, b) * width, width)
        return resid.at[t, :, pl.ds(start, width)]

    def piece_line(t, b, way):
        ref = piece(t, x, c, b)
        return remote(
            ref,
            ref,
            piece_line_send.at[way, t, b],
            piece_line_recv.at[t, b],
            (y, beside[way], x),
        )

    def piece_tp(t, b, side):
        ref = piece(t, side, c, b)
        return remote(ref, ref, piece_tp_send.at[t, b], piece_tp_recv.at[t, b], tp_mate)

    def piece_core(t, b, kind, core):
        ref = piece(t, x if kind == 0 else 1 - x, core, b)
        return remote(
            ref, ref, piece_core_send.at[kind, t, b], piece_core_recv.at[kind, t, b], core_mate
        )

    def parts_copy(b):
        return remote(parts_out.at[b], parts_in.at[b], parts_send.at[b], parts_recv.at[b], tp_mate)

    def project(p):
        block = plane_at(table, z, p)
        if p == 0:
            late[0].wait()
            heads_copy.wait_recv()
        else:
            for s in range(PIECES):
                block_rep(block, 1 - y, s).wait_recv()
        part = jnp.dot(attention[...], out_blocks[block], preferred_element_type=jnp.float32)
        b = block % half_planes
        mine = block // half_planes == x

        @pl.when(mine)
        def _():
            kept[b] = part

        @pl.when(block // half_planes != x)
        def _():
            parts_out[b] = part.astype(jnp.bfloat16)
            parts_copy(b).start()

    def settle(p):
        block = plane_at(table, z, p)
        b = block % half_planes

        @pl.when(block // half_planes == x)
        def _():
            parts_copy(b).wait_recv()
            start = pl.multiple_of((2 * b + c) * width, width)
            summed = (
                hidden_in[:, pl.ds(start, width)].astype(jnp.float32)
                + kept[b]
                + parts_in[b].astype(jnp.float32)
            )
            target = pl.multiple_of(column_block(x, c, b) * width, width)
            resid[z, :, pl.ds(target, width)] = summed.astype(jnp.bfloat16)
            for way in range(2):
                pl.when(has[way])(piece_line(z, b, way).start)
            piece_tp(z, b, x).start()
            piece_core(z, b, 0, c).start()

    late[1].wait()
    rows_copy.wait_recv()
    for p in range(1, planes + 1):
        if p < planes:
            block = plane_at(table, z, p)
            for s in range(PIECES):
                block_line(block, s, 0).wait_recv()
                pl.when((block > z) & has[0])(block_line(block, s, 0).start)
                pl.when((block < z) & has[1])(block_line(block, s, 1).start)
                block_rep(block, y, s).start()
        if p == planes - 1:
            for kind, s in weight_list:
                weight_tp(kind, s).wait_recv()
                weight_rep(kind, s, y).start()
        if p >= 2:
            settle(p - 2)
        project(p - 1)
    settle(planes - 1)

    for p in range(1, planes + 1):
        if p < planes:
            t = plane_at(table, z, p)
            for i in range(half_planes):
                b = x * i + (1 - x) * (half_planes - 1 - i)
                piece_line(t, b, 0).wait_recv()
                pl.when((t > z) & has[0])(piece_line(t, b, 0).start)
                pl.when((t < z) & has[1])(piece_line(t, b, 1).start)
                piece_tp(t, b, x).start()
                piece_core(t, b, 0, c).start()
        t = plane_at(table, z, p - 1)
        for b in range(half_planes):
            piece_tp(t, b, 1 - x).wait_recv()
            piece_core(t, b, 1, c).start()

    for copy in late[2:]:
        copy.wait()
    for kind, s in weight_list:
        weight_rep(kind, s, 1 - y).wait_recv()
    router_copy.wait_recv()
    for copy in marks_copies:
        copy.wait_recv()
    def hidden_copy(t, side):
        ref = hidden.at[side, t]
        return remote(ref, ref, hidden_send.at[t], hidden_recv.at[t], tp_mate)

    def open_plane(t):
        for b in range(half_planes):
            for kind in range(2):
                piece_core(t, b, kind, 1 - c).wait_recv()
        rows = resid[t]
        wide = rows.astype(jnp.float32)
        scale = lax.rsqrt(jnp.sum(wide * wide, 1, keepdims=True) / D + 1e-06)
        gate = jnp.dot(rows, gate_up[0], preferred_element_type=jnp.float32) * scale
        up = jnp.dot(rows, gate_up[1], preferred_element_type=jnp.float32) * scale
        logits = (
            lax.dot_general(
                rows, routers[...], (((1,), (1,)), ((), ())), preferred_element_type=jnp.float32
            )
            * scale
        )
        chosen = jnp.concatenate(
            [
                lax.dot_general(
                    all_marks[2 * t + core],
                    eye,
                    (((0,), (0,)), ((), ())),
                    preferred_element_type=jnp.float32,
                )
                for core in range(2)
            ],
            0,
        )
        raised = jnp.where(chosen > 0.5, jnp.exp(logits), 0.0)
        share = jnp.sum(
            jnp.where(slots[...] == 2 * e + x, raised, 0.0), 1, keepdims=True
        ) / jnp.sum(raised, 1, keepdims=True)
        hidden[x, t] = (gate / (1.0 + jnp.exp(-gate)) * up * share).astype(jnp.bfloat16)
        hidden_copy(t, x).start()

    for p in reversed(range(planes)):
        open_plane(plane_at(table, z, p))

    def core_copy(t):
        return remote(core_out.at[t], core_in.at[t], core_send.at[t], core_recv.at[t], core_mate)

    part_width = half // LINE_PIECES

    def line_copy(t, i, way):
        columns = pl.ds(i * part_width, part_width)
        return remote(
            line_out.at[t, :, columns],
            line_in.at[way, t, :, columns],
            line_send.at[t, i],
            line_recv.at[way, t, i],
            (y, beside[way], x),
        )

    def close_plane(t):
        hidden_copy(t, 1 - x).wait_recv()
        product[...] = lax.dot_general(
            hidden[0, t], down[0], (((1,), (1,)), ((), ())), preferred_element_type=jnp.float32
        ) + lax.dot_general(
            hidden[1, t], down[1], (((1,), (1,)), ((), ())), preferred_element_type=jnp.float32
        )
        core_out[t] = product[mate_rows].astype(jnp.bfloat16)
        core_copy(t).start()
        own_total[t] = product[own_rows]

    def pass_on(t):
        core_copy(t).wait_recv()
        for i in range(LINE_PIECES):
            columns = pl.ds(i * part_width, part_width)
            own_total[t, :, columns] += core_in[t, :, columns].astype(jnp.float32)

            @pl.when((t >= z) & has[0])
            def _():
                line_copy(t, i, 1).wait_recv()
                own_total[t, :, columns] += line_in[1, t, :, columns].astype(jnp.float32)

            @pl.when((t <= z) & has[1])
            def _():
                line_copy(t, i, 0).wait_recv()
                own_total[t, :, columns] += line_in[0, t, :, columns].astype(jnp.float32)

            @pl.when(t != z)
            def _():
                line_out[t, :, columns] = own_total[t, :, columns].astype(jnp.bfloat16)

            pl.when(t > z)(line_copy(t, i, 1).start)
            pl.when(t < z)(line_copy(t, i, 0).start)

    at_end = (z == 0) | (z == planes - 1)
    inside = (z > 0) & (z < planes - 1)
    for p in reversed(range(planes)):
        close_plane(plane_at(table, z, p))
        if p > 0:
            pl.when(at_end)(functools.partial(pass_on, plane_at(table, z, p)))
        if p + 1 < planes:
            pl.when(inside)(functools.partial(pass_on, plane_at(table, z, p + 1)))
    pass_on(z)
    own_resid = resid[z, own_rows, pl.ds(pl.multiple_of(x * half, half), half)]
    out[...] = (own_resid.astype(jnp.float32) + own_total[z]).astype(jnp.bfloat16)

    rows_copy.wait_send()
    heads_copy.wait_send()
    router_copy.wait_send()
    for kind, s in weight_list:
        weight_tp(kind, s).wait_send()
        weight_rep(kind, s, y).wait_send()
    for copy in marks_copies:
        copy.wait_send()
    for s in range(PIECES):
        for way in range(2):
            pl.when(has[way])(block_own(s, way).wait_send)
    for p in range(1, planes):
        t = plane_at(table, z, p)
        for s in range(PIECES):
            pl.when((t > z) & has[0])(block_line(t, s, 0).wait_send)
            pl.when((t < z) & has[1])(block_line(t, s, 1).wait_send)
            block_rep(t, y, s).wait_send()
        for b in range(half_planes):
            pl.when((t > z) & has[0])(piece_line(t, b, 0).wait_send)
            pl.when((t < z) & has[1])(piece_line(t, b, 1).wait_send)
        for i in range(LINE_PIECES):
            pl.when(t > z)(line_copy(t, i, 1).wait_send)
            pl.when(t < z)(line_copy(t, i, 0).wait_send)
    for b in range(half_planes):
        parts_copy(b).wait_send()
        for way in range(2):
            pl.when(has[way])(piece_line(z, b, way).wait_send)
    for t in range(planes):
        for b in range(half_planes):
            piece_tp(t, b, x).wait_send()
            piece_core(t, b, 0, c).wait_send()
            piece_core(t, b, 1, c).wait_send()
        hidden_copy(t, x).wait_send()
        core_copy(t).wait_send()


def one_kernel_layer(
    hidden_states, queries, fresh_key_value, cache, lengths, out_weight, router, experts, expert_ids, slots
):
    group = lax.axis_size("ep")
    planes = group // 2
    half_planes = planes // 2
    tokens, half = hidden_states.shape
    depth, width = out_weight.shape
    number = router.shape[1]
    kv_width = cache.shape[3]
    key_total = cache.shape[2] + tokens
    units = experts.shape[3]
    fresh = jnp.moveaxis(fresh_key_value, 2, 0).reshape(2, tokens, kv_width)
    vmem, anywhere = (pl.BlockSpec(memory_space=m) for m in (pltpu.VMEM, pl.ANY))
    dma = pltpu.SemaphoreType.DMA
    bf16, f32 = jnp.bfloat16, jnp.float32
    return pl.pallas_call(
        functools.partial(layer_kernel, planes, tokens, queries.shape[1] // kv_width),
        out_shape=jax.ShapeDtypeStruct((tokens, half), bf16),
        in_specs=[
            vmem,
            anywhere,
            anywhere,
            pl.BlockSpec(memory_space=pltpu.SMEM),
            anywhere,
            anywhere,
            vmem,
            anywhere,
            vmem,
            vmem,
        ],
        out_specs=vmem,
        scratch_shapes=[
            pltpu.VMEM((key_total, kv_width), bf16),
            pltpu.VMEM((key_total, kv_width), bf16),
            pltpu.VMEM((tokens, key_total), f32),
            pltpu.VMEM((2 * tokens, depth), bf16),
            pltpu.VMEM((planes, depth, width), bf16),
            pltpu.VMEM((2 * tokens, half), bf16),
            pltpu.VMEM((half_planes, 2 * tokens, width), f32),
            pltpu.VMEM((half_planes, 2 * tokens, width), bf16),
            pltpu.VMEM((half_planes, 2 * tokens, width), bf16),
            pltpu.VMEM((planes, 2 * tokens, 2 * half), bf16),
            pltpu.VMEM((2, 2 * half, units), bf16),
            pltpu.VMEM((2, half, units), bf16),
            pltpu.VMEM((number, 2 * half), bf16),
            pltpu.VMEM((group, number, tokens), bf16),
            pltpu.VMEM((2, planes, 2 * tokens, units), bf16),
            pltpu.VMEM((2 * tokens, half), f32),
            pltpu.VMEM((planes, tokens, half), f32),
            pltpu.VMEM((planes, tokens, half), bf16),
            pltpu.VMEM((planes, tokens, half), bf16),
            pltpu.VMEM((planes, tokens, half), bf16),
            pltpu.VMEM((2, planes, tokens, half), bf16),
            dma((10,)),
            dma((2, WEIGHT_PIECES)),
            dma((2, WEIGHT_PIECES)),
            dma((2, WEIGHT_PIECES)),
            dma((2, WEIGHT_PIECES)),
            dma,
            dma,
            dma,
            dma,
            dma,
            dma,
            dma((group - 1,)),
            dma((group - 1,)),
            dma((2, planes, PIECES)),
            dma((planes, PIECES)),
            dma((planes, PIECES)),
            dma((planes, PIECES)),
            dma((half_planes,)),
            dma((half_planes,)),
            dma((2, planes, half_planes)),
            dma((planes, half_planes)),
            dma((planes, half_planes)),
            dma((planes, half_planes)),
            dma((2, planes, half_planes)),
            dma((2, planes, half_planes)),
            dma((planes,)),
            dma((planes,)),
            dma((planes,)),
            dma((planes,)),
            dma((planes, LINE_PIECES)),
            dma((2, planes, LINE_PIECES)),
        ],
        compiler_params=pltpu.CompilerParams(
            collective_id=0, has_side_effects=True, vmem_limit_bytes=56 * 1024 * 1024
        ),
    )(
        queries,
        fresh,
        cache,
        lengths,
        out_weight,
        hidden_states,
        router.T,
        experts,
        jnp.swapaxes(expert_ids, 1, 2),
        slots.reshape(1, number),
    )


def per_device(
    hidden_states,
    queries,
    fresh_key_value,
    cache,
    cache_lengths,
    out_weight,
    router_weight,
    expert_weights,
    expert_ids,
    old_slots,
    new_slots,
    moved_experts,
):
    tokens_dev = hidden_states.shape[1]
    quarter = hidden_states.shape[2]
    experts = router_weight.shape[1]
    top_count = expert_ids.shape[2]
    groups = lax.axis_size("ep")
    local_slots = expert_weights.shape[0]
    capacity = min(tokens_dev, 3 * tokens_dev * top_count // (2 * experts))
    routed = expert_ids.reshape(2 * tokens_dev, top_count)
    if (
        lax.axis_size("rep") == 2
        and lax.axis_size("tp") == 2
        and groups == 8
        and local_slots == 2
        and tokens_dev % 16 == 0
    ):
        mixed = one_kernel_layer(
            hidden_states.reshape(2 * tokens_dev, quarter),
            queries.reshape(2 * tokens_dev, queries.shape[2]),
            fresh_key_value,
            cache,
            cache_lengths,
            out_weight,
            router_weight,
            expert_weights,
            expert_ids,
            old_slots,
        )
        return mixed.reshape(2, tokens_dev, quarter)
    attention = attend_local(queries, fresh_key_value, cache, cache_lengths)
    head_terms = jnp.dot(
        attention,
        lax.all_gather(out_weight, "ep", axis=1, tiled=True),
        preferred_element_type=jnp.float32,
    )
    attn_out = lax.psum_scatter(
        head_terms.astype(jnp.bfloat16), "tp", scatter_dimension=1, tiled=True
    ).astype(jnp.float32)
    residual = (
        hidden_states.reshape(2 * tokens_dev, quarter).astype(jnp.float32) + attn_out
    ).astype(jnp.bfloat16)
    wide = residual.astype(jnp.float32)
    squares = lax.psum(jnp.sum(wide * wide, 1), "tp")
    normed = (wide * lax.rsqrt(squares / D + 1e-06)[:, None]).astype(jnp.bfloat16)
    logits = lax.psum(
        jnp.dot(normed, router_weight, preferred_element_type=jnp.float32).astype(jnp.bfloat16),
        "tp",
    ).astype(jnp.float32)
    selected = jnp.sum(
        jnp.where(
            routed[:, :, None] == jnp.arange(experts, dtype=jnp.int32)[None, None, :],
            logits[:, None, :],
            0.0,
        ),
        -1,
    )
    raised = jnp.exp(selected)
    combine = raised / jnp.sum(raised, 1, keepdims=True)
    outputs = []
    for lower in (0, tokens_dev):
        upper = lower + tokens_dev
        outputs.append(
            mix_block(
                normed[lower:upper],
                residual[lower:upper],
                routed[lower:upper],
                combine[lower:upper],
                old_slots,
                expert_weights,
                capacity,
                groups,
            )
        )
    return jnp.stack(outputs)


def solution(mesh):
    return jax.shard_map(
        per_device,
        mesh=mesh,
        in_specs=(
            P(None, ("rep", "ep"), "tp"),
            P(None, ("rep", "ep"), "tp"),
            P(None, ("rep", "ep"), None, "tp"),
            P(("rep", "ep"), None, None, "tp"),
            P(("rep", "ep")),
            P("tp", "ep"),
            P("tp", None),
            P("ep", None, "tp", None),
            P(None, ("rep", "ep"), None),
            P(),
            P(),
            P(),
        ),
        out_specs=P(None, ("rep", "ep"), "tp"),
        check_vma=False,
    )
```

```python
import functools

import jax
import jax.numpy as jnp
from jax import lax
from jax.experimental import pallas as pl
from jax.experimental.pallas import tpu as pltpu
from jax.sharding import PartitionSpec as P

D = 2048
HEAD_SIZE = 128


def lookup(entries, wanted_keys):
    return jnp.sum(
        jnp.where(
            wanted_keys[..., None] == jnp.arange(entries.shape[0], dtype=jnp.int32), entries, 0
        ),
        -1,
    )


def attend_local(queries, fresh_key_value, cache, cache_lengths):
    tokens_dev = queries.shape[1]
    kv_heads = fresh_key_value.shape[3] // HEAD_SIZE
    query_group_width = queries.shape[2] // HEAD_SIZE // kv_heads
    key_matrix = jnp.concatenate(
        [cache[0, 0], fresh_key_value[0, :, 0], fresh_key_value[1, :, 0]], 0
    )
    value_matrix = jnp.concatenate(
        [cache[0, 1], fresh_key_value[0, :, 1], fresh_key_value[1, :, 1]], 0
    )
    key_total = key_matrix.shape[0]
    context = cache.shape[2]
    query_matrix = queries.reshape(2 * tokens_dev, kv_heads, query_group_width, HEAD_SIZE)
    attention_scores = jnp.einsum(
        "meqt,wet->eqmw",
        query_matrix,
        key_matrix.reshape(key_total, kv_heads, HEAD_SIZE),
        preferred_element_type=jnp.float32,
    ) * HEAD_SIZE ** (-0.5)
    position = jnp.arange(key_total, dtype=jnp.int32)[None, :]
    row_index = jnp.arange(2 * tokens_dev, dtype=jnp.int32)[:, None]
    visible = jnp.where(
        position < context, position < cache_lengths[0], position - context <= row_index
    )
    attention_scores = jnp.where(visible, attention_scores, jnp.float32(-1e30))
    largest = jnp.max(attention_scores, -1, keepdims=True)
    weights = jnp.where(visible, jnp.exp(attention_scores - largest), jnp.float32(0.0))
    route_probability = (weights / jnp.sum(weights, -1, keepdims=True)).astype(jnp.bfloat16)
    layer_result = jnp.einsum(
        "qizo,oqx->zqix",
        route_probability,
        value_matrix.reshape(key_total, kv_heads, HEAD_SIZE),
        preferred_element_type=jnp.float32,
    )
    return layer_result.reshape(2 * tokens_dev, -1).astype(jnp.bfloat16)


def run_slots(weights, received):
    gate_up = jnp.einsum(
        "secq,egqf->secgf", received, weights[:, :2], preferred_element_type=jnp.float32
    )
    summed = lax.psum(gate_up.astype(jnp.bfloat16), "tp").astype(jnp.float32)
    hidden = (jax.nn.silu(summed[:, :, :, 0]) * summed[:, :, :, 1]).astype(jnp.bfloat16)
    layer_result = jnp.einsum(
        "secf,eqf->secq", hidden, weights[:, 2], preferred_element_type=jnp.float32
    ).astype(jnp.bfloat16)
    return lax.all_to_all(layer_result, "ep", split_axis=0, concat_axis=0, tiled=True)


def mix_block(normed_rows, resid_rows, routed, combine, slot_table, weights, capacity, groups):
    tokens_dev, top_count = routed.shape
    experts = slot_table.shape[0]
    local_slots = weights.shape[0]
    quarter = normed_rows.shape[1]
    slot_index = lookup(slot_table, routed)
    picked_mask = routed[:, :, None] == jnp.arange(experts, dtype=jnp.int32)[None, None, :]
    expert_marks = picked_mask.any(1).astype(jnp.bfloat16)
    earlier = (jnp.arange(tokens_dev)[:, None] > jnp.arange(tokens_dev)[None, :]).astype(
        jnp.bfloat16
    )
    before = jnp.dot(earlier, expert_marks, preferred_element_type=jnp.float32)
    slot_rank = jnp.sum(jnp.where(picked_mask, before[:, None, :], 0.0), -1).astype(jnp.int32)
    buffer_row = (slot_index * capacity + slot_rank).reshape(-1)
    buffer_rows = (
        jnp.zeros((groups * local_slots * capacity, quarter), jnp.bfloat16)
        .at[buffer_row]
        .set(jnp.repeat(normed_rows, top_count, axis=0))
    )
    outgoing = buffer_rows.reshape(groups, local_slots, capacity, quarter)
    returned = run_slots(
        weights, lax.all_to_all(outgoing, "ep", split_axis=0, concat_axis=0, tiled=True)
    )
    gathered = returned.reshape(-1, quarter)[buffer_row].reshape(tokens_dev, top_count, quarter)
    mixed_rows = resid_rows.astype(jnp.float32) + jnp.sum(
        combine[:, :, None] * gathered.astype(jnp.float32), 1
    )
    return mixed_rows.astype(jnp.bfloat16)


MESH = pl.DeviceIdType.MESH
PIECES = 4
LINE_PIECES = 4
WEIGHT_PIECES = 2


def line_order(planes):
    table = []
    for z in range(planes):
        table.append(
            sorted(
                range(planes),
                key=lambda t: (abs(t - z), (z if t < z else planes - 1 - z) if t != z else 0),
            )
        )
    return table


def gather_order(planes):
    tables = []
    for side in range(2):
        table = []
        for z in range(planes):
            rest = sorted(
                range(planes), key=lambda t: (t != z, t // (planes // 2) != side, abs(t - z))
            )
            table.append(rest)
        tables.append(table)
    return tables


def plane_at(table, z, p):
    value = jnp.int32(0)
    for i, row in enumerate(table):
        value = value + jnp.where(z == i, jnp.int32(row[p]), 0)
    return value


def layer_kernel(
    planes,
    tokens,
    head_group,
    queries,
    fresh,
    cache,
    lengths,
    out_weight,
    hidden_states,
    router,
    experts,
    routed,
    slots,
    out,
    keys,
    values,
    bias,
    attention,
    out_blocks,
    hidden_in,
    kept,
    parts_out,
    parts_in,
    resid,
    gate_up,
    down,
    routers,
    all_marks,
    hidden,
    product,
    own_total,
    core_out,
    core_in,
    line_out,
    line_in,
    local_sem,
    weight_send,
    weight_recv,
    weight_rep_send,
    weight_rep_recv,
    router_send,
    router_recv,
    rows_send,
    rows_recv,
    heads_send,
    heads_recv,
    marks_send,
    marks_recv,
    block_line_send,
    block_line_recv,
    block_rep_send,
    block_rep_recv,
    parts_send,
    parts_recv,
    piece_line_send,
    piece_line_recv,
    piece_tp_send,
    piece_tp_recv,
    piece_core_send,
    piece_core_recv,
    hidden_send,
    hidden_recv,
    core_send,
    core_recv,
    line_send,
    line_recv,
):
    y, e, x = lax.axis_index("rep"), lax.axis_index("ep"), lax.axis_index("tp")
    z, c = e // 2, e % 2
    group = 2 * planes
    half_planes = planes // 2
    table = line_order(planes)
    width = out_weight.shape[1]
    depth = out_weight.shape[0]
    half = hidden_states.shape[1]
    has = (z > 0, z < planes - 1)
    beside = (e - 2, e + 2)
    tp_mate = (y, e, 1 - x)
    rep_mate = (1 - y, e, x)
    mate = e + 1 - 2 * c
    core_mate = (y, mate, x)
    chunk = depth // 2 // PIECES
    own_rows = pl.ds(pl.multiple_of(c * tokens, tokens), tokens)
    mate_rows = pl.ds(pl.multiple_of((1 - c) * tokens, tokens), tokens)

    def remote(src, dst, send, recv, target):
        return pltpu.make_async_remote_copy(
            src_ref=src,
            dst_ref=dst,
            send_sem=send,
            recv_sem=recv,
            device_id=target,
            device_id_type=MESH,
        )

    barrier = pltpu.get_barrier_semaphore()
    for step in range(1, group):
        pl.semaphore_signal(
            barrier, inc=1, device_id=(y, (e + step) % group, x), device_id_type=MESH
        )
    pl.semaphore_signal(barrier, inc=1, device_id=tp_mate, device_id_type=MESH)
    pl.semaphore_signal(barrier, inc=1, device_id=rep_mate, device_id_type=MESH)

    context = cache.shape[2]
    local = [
        pltpu.make_async_copy(cache.at[0, 0], keys.at[pl.ds(0, context)], local_sem.at[0]),
        pltpu.make_async_copy(cache.at[0, 1], values.at[pl.ds(0, context)], local_sem.at[1]),
    ]
    late = [
        pltpu.make_async_copy(out_weight, out_blocks.at[z], local_sem.at[4]),
        pltpu.make_async_copy(hidden_states, hidden_in.at[own_rows], local_sem.at[5]),
        pltpu.make_async_copy(
            experts.at[x, pl.ds(0, 2)],
            gate_up.at[:, pl.ds(pl.multiple_of(x * half, half), half)],
            local_sem.at[6],
        ),
        pltpu.make_async_copy(experts.at[0, 2], down.at[0], local_sem.at[7]),
        pltpu.make_async_copy(experts.at[1, 2], down.at[1], local_sem.at[8]),
        pltpu.make_async_copy(
            router, routers.at[:, pl.ds(pl.multiple_of(x * half, half), half)], local_sem.at[9]
        ),
    ]
    for copy in local:
        copy.start()

    number = router.shape[0]
    eye = (
        lax.broadcasted_iota(jnp.int32, (number, number), 0)
        == lax.broadcasted_iota(jnp.int32, (number, number), 1)
    ).astype(jnp.bfloat16)
    blocks, top_count, block_tokens = routed.shape
    expert = lax.broadcasted_iota(jnp.int32, (number, block_tokens), 0)
    for block in range(blocks):
        named = jnp.zeros((number, block_tokens), jnp.int32)
        for k in range(top_count):
            named += (routed[block, k : k + 1, :] == expert).astype(jnp.int32)
        all_marks[e, :, block * block_tokens : (block + 1) * block_tokens] = named.astype(
            jnp.float32
        ).astype(jnp.bfloat16)

    pl.semaphore_wait(barrier, group + 1)

    def block_chunk(block, side, s):
        return out_blocks.at[
            block, pl.ds(pl.multiple_of(side * (depth // 2) + s * chunk, chunk), chunk)
        ]

    def block_line(block, s, way):
        piece = block_chunk(block, y, s)
        return remote(
            piece,
            piece,
            block_line_send.at[way, block, s],
            block_line_recv.at[block, s],
            (y, beside[way], x),
        )

    def block_own(s, way):
        return remote(
            out_weight.at[pl.ds(pl.multiple_of(y * (depth // 2) + s * chunk, chunk), chunk)],
            block_chunk(z, y, s),
            block_line_send.at[way, z, s],
            block_line_recv.at[z, s],
            (y, beside[way], x),
        )

    def block_rep(block, side, s):
        piece = block_chunk(block, side, s)
        return remote(piece, piece, block_rep_send.at[block, s], block_rep_recv.at[block, s], rep_mate)

    for s in range(PIECES):
        for way in range(2):
            pl.when(has[way])(block_own(s, way).start)
    rows_copy = remote(hidden_states, hidden_in.at[own_rows], rows_send, rows_recv, core_mate)
    rows_copy.start()
    marks_copies = []
    for step in range(1, group):
        copy = remote(
            all_marks.at[e],
            all_marks.at[e],
            marks_send.at[step - 1],
            marks_recv.at[step - 1],
            (y, (e + step) % group, x),
        )
        copy.start()
        marks_copies.append(copy)
    router_copy = remote(
        router,
        routers.at[:, pl.ds(pl.multiple_of(x * half, half), half)],
        router_send,
        router_recv,
        tp_mate,
    )
    router_copy.start()
    share_rows = half // (2 * WEIGHT_PIECES)

    def weight_share(kind, s, tp_side, rep_side):
        start = tp_side * half + (rep_side * WEIGHT_PIECES + s) * share_rows
        return gate_up.at[kind, pl.ds(pl.multiple_of(start, share_rows), share_rows)]

    def weight_tp(kind, s):
        start = pl.multiple_of((y * WEIGHT_PIECES + s) * share_rows, share_rows)
        return remote(
            experts.at[1 - x, kind, pl.ds(start, share_rows)],
            weight_share(kind, s, x, y),
            weight_send.at[kind, s],
            weight_recv.at[kind, s],
            tp_mate,
        )

    def weight_rep(kind, s, side):
        ref = weight_share(kind, s, 1 - x, side)
        return remote(
            ref, ref, weight_rep_send.at[kind, s], weight_rep_recv.at[kind, s], rep_mate
        )

    weight_list = [(kind, s) for s in range(WEIGHT_PIECES) for kind in range(2)]
    for kind, s in weight_list:
        weight_tp(kind, s).start()
    for copy in late:
        copy.start()

    key_total = keys.shape[0]
    position = lax.broadcasted_iota(jnp.int32, (tokens, key_total), 1)
    row = lax.broadcasted_iota(jnp.int32, (tokens, key_total), 0)
    visible = jnp.where(
        position < context,
        (position < lengths[0]).astype(jnp.int32),
        (position - context <= row).astype(jnp.int32),
    )
    bias[...] = jnp.where(visible > 0, jnp.float32(0.0), jnp.float32(-1e30))
    for block in range(blocks):
        start = context + block * block_tokens
        keys[start : start + block_tokens] = fresh[block, :, 0, :]
        values[start : start + block_tokens] = fresh[block, :, 1, :]
    for copy in local:
        copy.wait()
    kv_heads = keys.shape[1] // HEAD_SIZE

    def attend(kv, first, count):
        key_part = keys[:, kv * HEAD_SIZE : (kv + 1) * HEAD_SIZE]
        value_part = values[:, kv * HEAD_SIZE : (kv + 1) * HEAD_SIZE]

        def one(q, _):
            column = pl.ds(
                pl.multiple_of((kv * head_group + q) * HEAD_SIZE, HEAD_SIZE), HEAD_SIZE
            )
            query = queries[:, column]
            scores = (
                lax.dot_general(
                    query, key_part, (((1,), (1,)), ((), ())), preferred_element_type=jnp.float32
                )
                * HEAD_SIZE ** (-0.5)
                + bias[...]
            )
            raised = jnp.exp(scores - jnp.max(scores, -1, keepdims=True))
            total = jnp.sum(raised, -1, keepdims=True)
            mixed = jnp.dot(
                raised.astype(jnp.bfloat16), value_part, preferred_element_type=jnp.float32
            )
            attention[own_rows, column] = (mixed / total).astype(jnp.bfloat16)
            return 0

        lax.fori_loop(first, first + count, one, 0)

    def take_chunk(p, s):
        block = plane_at(table, z, p)
        block_line(block, s, 0).wait_recv()
        pl.when((block > z) & has[0])(block_line(block, s, 0).start)
        pl.when((block < z) & has[1])(block_line(block, s, 1).start)
        block_rep(block, y, s).start()

    heads_copy = remote(
        attention.at[own_rows], attention.at[own_rows], heads_send, heads_recv, core_mate
    )
    at_end = (z == 0) | (z == planes - 1)
    inside = (z > 0) & (z < planes - 1)
    section = kv_heads * head_group // PIECES
    for s in range(PIECES):
        attend(s * section // head_group, s * section % head_group, section)
        if s == PIECES - 1:
            heads_copy.start()
        take_chunk(1, s)
        pl.when(inside)(functools.partial(take_chunk, 2, s))

    def column_block(side, core, b):
        return 2 * (half_planes * side + b) + core

    def piece(t, side, core, b):
        start = pl.multiple_of(column_block(side, core, b) * width, width)
        return resid.at[t, :, pl.ds(start, width)]

    def piece_line(t, b, way):
        ref = piece(t, x, c, b)
        return remote(
            ref,
            ref,
            piece_line_send.at[way, t, b],
            piece_line_recv.at[t, b],
            (y, beside[way], x),
        )

    def piece_tp(t, b, side):
        ref = piece(t, side, c, b)
        return remote(ref, ref, piece_tp_send.at[t, b], piece_tp_recv.at[t, b], tp_mate)

    def piece_core(t, b, kind, core):
        ref = piece(t, x if kind == 0 else 1 - x, core, b)
        return remote(
            ref, ref, piece_core_send.at[kind, t, b], piece_core_recv.at[kind, t, b], core_mate
        )

    def parts_copy(b):
        return remote(parts_out.at[b], parts_in.at[b], parts_send.at[b], parts_recv.at[b], tp_mate)

    def project(p):
        block = plane_at(table, z, p)
        if p == 0:
            late[0].wait()
            heads_copy.wait_recv()
        else:
            for s in range(PIECES):
                block_rep(block, 1 - y, s).wait_recv()
        part = jnp.dot(attention[...], out_blocks[block], preferred_element_type=jnp.float32)
        b = block % half_planes
        mine = block // half_planes == x

        @pl.when(mine)
        def _():
            kept[b] = part

        @pl.when(block // half_planes != x)
        def _():
            parts_out[b] = part.astype(jnp.bfloat16)
            parts_copy(b).start()

    def settle(p):
        block = plane_at(table, z, p)
        b = block % half_planes

        @pl.when(block // half_planes == x)
        def _():
            parts_copy(b).wait_recv()
            start = pl.multiple_of((2 * b + c) * width, width)
            summed = (
                hidden_in[:, pl.ds(start, width)].astype(jnp.float32)
                + kept[b]
                + parts_in[b].astype(jnp.float32)
            )
            target = pl.multiple_of(column_block(x, c, b) * width, width)
            resid[z, :, pl.ds(target, width)] = summed.astype(jnp.bfloat16)
            for way in range(2):
                pl.when(has[way])(piece_line(z, b, way).start)
            piece_tp(z, b, x).start()
            piece_core(z, b, 0, c).start()

    late[1].wait()
    rows_copy.wait_recv()
    gather_first, gather_second = gather_order(planes)

    def gather_at(side, q):
        return jnp.where(
            side == 0, plane_at(gather_first, z, q), plane_at(gather_second, z, q)
        )

    def take_plane(t):
        for i in range(half_planes):
            b = x * i + (1 - x) * (half_planes - 1 - i)
            piece_line(t, b, 0).wait_recv()
            pl.when((t > z) & has[0])(piece_line(t, b, 0).start)
            pl.when((t < z) & has[1])(piece_line(t, b, 1).start)
            piece_tp(t, b, x).start()
            piece_core(t, b, 0, c).start()

    nearest = gather_at(x, 1)
    direct = (nearest == z + 1) | (nearest == z - 1)
    project(0)
    for p in range(2, planes):
        for s in range(PIECES):
            if p == 2:
                pl.when(at_end)(functools.partial(take_chunk, p, s))
            else:
                take_chunk(p, s)
            if s == 0 and p > 2:
                project(p - 2)
            if s == PIECES - 2:
                settle(p - 2)
    for kind, s in weight_list:
        weight_tp(kind, s).wait_recv()
        weight_rep(kind, s, y).start()
    project(planes - 2)
    project(planes - 1)
    settle(planes - 2)
    pl.when(direct)(functools.partial(take_plane, nearest))
    settle(planes - 1)

    for q in range(1, planes + 1):
        if q == 1:
            pl.when(jnp.logical_not(direct))(functools.partial(take_plane, nearest))
        elif q < planes:
            take_plane(gather_at(x, q))
        t = gather_at(1 - x, q - 1)
        for b in range(half_planes):
            piece_tp(t, b, 1 - x).wait_recv()
            piece_core(t, b, 1, c).start()

    for copy in late[2:]:
        copy.wait()
    for kind, s in weight_list:
        weight_rep(kind, s, 1 - y).wait_recv()
    router_copy.wait_recv()
    for copy in marks_copies:
        copy.wait_recv()
    def hidden_copy(t, side):
        ref = hidden.at[side, t]
        return remote(ref, ref, hidden_send.at[t], hidden_recv.at[t], tp_mate)

    def open_plane(t):
        for b in range(half_planes):
            for kind in range(2):
                piece_core(t, b, kind, 1 - c).wait_recv()
        rows = resid[t]
        wide = rows.astype(jnp.float32)
        scale = lax.rsqrt(jnp.sum(wide * wide, 1, keepdims=True) / D + 1e-06)
        gate = jnp.dot(rows, gate_up[0], preferred_element_type=jnp.float32) * scale
        up = jnp.dot(rows, gate_up[1], preferred_element_type=jnp.float32) * scale
        logits = (
            lax.dot_general(
                rows, routers[...], (((1,), (1,)), ((), ())), preferred_element_type=jnp.float32
            )
            * scale
        )
        chosen = jnp.concatenate(
            [
                lax.dot_general(
                    all_marks[2 * t + core],
                    eye,
                    (((0,), (0,)), ((), ())),
                    preferred_element_type=jnp.float32,
                )
                for core in range(2)
            ],
            0,
        )
        raised = jnp.where(chosen > 0.5, jnp.exp(logits), 0.0)
        share = jnp.sum(
            jnp.where(slots[...] == 2 * e + x, raised, 0.0), 1, keepdims=True
        ) / jnp.sum(raised, 1, keepdims=True)
        hidden[x, t] = (gate / (1.0 + jnp.exp(-gate)) * up * share).astype(jnp.bfloat16)
        hidden_copy(t, x).start()

    for p in reversed(range(planes)):
        open_plane(plane_at(table, z, p))

    def core_copy(t):
        return remote(core_out.at[t], core_in.at[t], core_send.at[t], core_recv.at[t], core_mate)

    part_width = half // LINE_PIECES

    def line_copy(t, i, way):
        columns = pl.ds(i * part_width, part_width)
        return remote(
            line_out.at[t, :, columns],
            line_in.at[way, t, :, columns],
            line_send.at[t, i],
            line_recv.at[way, t, i],
            (y, beside[way], x),
        )

    def close_plane(t):
        hidden_copy(t, 1 - x).wait_recv()
        product[...] = lax.dot_general(
            hidden[0, t], down[0], (((1,), (1,)), ((), ())), preferred_element_type=jnp.float32
        ) + lax.dot_general(
            hidden[1, t], down[1], (((1,), (1,)), ((), ())), preferred_element_type=jnp.float32
        )
        core_out[t] = product[mate_rows].astype(jnp.bfloat16)
        core_copy(t).start()
        own_total[t] = product[own_rows]

    def pass_on(t):
        core_copy(t).wait_recv()
        for i in range(LINE_PIECES):
            columns = pl.ds(i * part_width, part_width)
            own_total[t, :, columns] += core_in[t, :, columns].astype(jnp.float32)

            @pl.when((t >= z) & has[0])
            def _():
                line_copy(t, i, 1).wait_recv()
                own_total[t, :, columns] += line_in[1, t, :, columns].astype(jnp.float32)

            @pl.when((t <= z) & has[1])
            def _():
                line_copy(t, i, 0).wait_recv()
                own_total[t, :, columns] += line_in[0, t, :, columns].astype(jnp.float32)

            @pl.when(t != z)
            def _():
                line_out[t, :, columns] = own_total[t, :, columns].astype(jnp.bfloat16)

            pl.when(t > z)(line_copy(t, i, 1).start)
            pl.when(t < z)(line_copy(t, i, 0).start)

    for p in reversed(range(planes)):
        close_plane(plane_at(table, z, p))
        if p > 0:
            pl.when(at_end)(functools.partial(pass_on, plane_at(table, z, p)))
        if p + 1 < planes:
            pl.when(inside)(functools.partial(pass_on, plane_at(table, z, p + 1)))
    pass_on(z)
    own_resid = resid[z, own_rows, pl.ds(pl.multiple_of(x * half, half), half)]
    out[...] = (own_resid.astype(jnp.float32) + own_total[z]).astype(jnp.bfloat16)

    rows_copy.wait_send()
    heads_copy.wait_send()
    router_copy.wait_send()
    for kind, s in weight_list:
        weight_tp(kind, s).wait_send()
        weight_rep(kind, s, y).wait_send()
    for copy in marks_copies:
        copy.wait_send()
    for s in range(PIECES):
        for way in range(2):
            pl.when(has[way])(block_own(s, way).wait_send)
    for p in range(1, planes):
        t = plane_at(table, z, p)
        for s in range(PIECES):
            pl.when((t > z) & has[0])(block_line(t, s, 0).wait_send)
            pl.when((t < z) & has[1])(block_line(t, s, 1).wait_send)
            block_rep(t, y, s).wait_send()
        for b in range(half_planes):
            pl.when((t > z) & has[0])(piece_line(t, b, 0).wait_send)
            pl.when((t < z) & has[1])(piece_line(t, b, 1).wait_send)
        for i in range(LINE_PIECES):
            pl.when(t > z)(line_copy(t, i, 1).wait_send)
            pl.when(t < z)(line_copy(t, i, 0).wait_send)
    for b in range(half_planes):
        parts_copy(b).wait_send()
        for way in range(2):
            pl.when(has[way])(piece_line(z, b, way).wait_send)
    for t in range(planes):
        for b in range(half_planes):
            piece_tp(t, b, x).wait_send()
            piece_core(t, b, 0, c).wait_send()
            piece_core(t, b, 1, c).wait_send()
        hidden_copy(t, x).wait_send()
        core_copy(t).wait_send()


def one_kernel_layer(
    hidden_states, queries, fresh_key_value, cache, lengths, out_weight, router, experts, expert_ids, slots
):
    group = lax.axis_size("ep")
    planes = group // 2
    half_planes = planes // 2
    tokens, half = hidden_states.shape
    depth, width = out_weight.shape
    number = router.shape[1]
    kv_width = cache.shape[3]
    key_total = cache.shape[2] + tokens
    units = experts.shape[3]
    vmem, anywhere = (pl.BlockSpec(memory_space=m) for m in (pltpu.VMEM, pl.ANY))
    dma = pltpu.SemaphoreType.DMA
    bf16, f32 = jnp.bfloat16, jnp.float32
    return pl.pallas_call(
        functools.partial(layer_kernel, planes, tokens, queries.shape[1] // kv_width),
        out_shape=jax.ShapeDtypeStruct((tokens, half), bf16),
        in_specs=[
            vmem,
            vmem,
            anywhere,
            pl.BlockSpec(memory_space=pltpu.SMEM),
            anywhere,
            anywhere,
            vmem,
            anywhere,
            vmem,
            vmem,
        ],
        out_specs=vmem,
        scratch_shapes=[
            pltpu.VMEM((key_total, kv_width), bf16),
            pltpu.VMEM((key_total, kv_width), bf16),
            pltpu.VMEM((tokens, key_total), f32),
            pltpu.VMEM((2 * tokens, depth), bf16),
            pltpu.VMEM((planes, depth, width), bf16),
            pltpu.VMEM((2 * tokens, half), bf16),
            pltpu.VMEM((half_planes, 2 * tokens, width), f32),
            pltpu.VMEM((half_planes, 2 * tokens, width), bf16),
            pltpu.VMEM((half_planes, 2 * tokens, width), bf16),
            pltpu.VMEM((planes, 2 * tokens, 2 * half), bf16),
            pltpu.VMEM((2, 2 * half, units), bf16),
            pltpu.VMEM((2, half, units), bf16),
            pltpu.VMEM((number, 2 * half), bf16),
            pltpu.VMEM((group, number, tokens), bf16),
            pltpu.VMEM((2, planes, 2 * tokens, units), bf16),
            pltpu.VMEM((2 * tokens, half), f32),
            pltpu.VMEM((planes, tokens, half), f32),
            pltpu.VMEM((planes, tokens, half), bf16),
            pltpu.VMEM((planes, tokens, half), bf16),
            pltpu.VMEM((planes, tokens, half), bf16),
            pltpu.VMEM((2, planes, tokens, half), bf16),
            dma((10,)),
            dma((2, WEIGHT_PIECES)),
            dma((2, WEIGHT_PIECES)),
            dma((2, WEIGHT_PIECES)),
            dma((2, WEIGHT_PIECES)),
            dma,
            dma,
            dma,
            dma,
            dma,
            dma,
            dma((group - 1,)),
            dma((group - 1,)),
            dma((2, planes, PIECES)),
            dma((planes, PIECES)),
            dma((planes, PIECES)),
            dma((planes, PIECES)),
            dma((half_planes,)),
            dma((half_planes,)),
            dma((2, planes, half_planes)),
            dma((planes, half_planes)),
            dma((planes, half_planes)),
            dma((planes, half_planes)),
            dma((2, planes, half_planes)),
            dma((2, planes, half_planes)),
            dma((planes,)),
            dma((planes,)),
            dma((planes,)),
            dma((planes,)),
            dma((planes, LINE_PIECES)),
            dma((2, planes, LINE_PIECES)),
        ],
        compiler_params=pltpu.CompilerParams(
            collective_id=0, has_side_effects=True, vmem_limit_bytes=56 * 1024 * 1024
        ),
    )(
        queries,
        fresh_key_value,
        cache,
        lengths,
        out_weight,
        hidden_states,
        router.T,
        experts,
        jnp.swapaxes(expert_ids, 1, 2),
        slots.reshape(1, number),
    )


def per_device(
    hidden_states,
    queries,
    fresh_key_value,
    cache,
    cache_lengths,
    out_weight,
    router_weight,
    expert_weights,
    expert_ids,
    old_slots,
    new_slots,
    moved_experts,
):
    tokens_dev = hidden_states.shape[1]
    quarter = hidden_states.shape[2]
    experts = router_weight.shape[1]
    top_count = expert_ids.shape[2]
    groups = lax.axis_size("ep")
    local_slots = expert_weights.shape[0]
    capacity = min(tokens_dev, 3 * tokens_dev * top_count // (2 * experts))
    routed = expert_ids.reshape(2 * tokens_dev, top_count)
    if (
        lax.axis_size("rep") == 2
        and lax.axis_size("tp") == 2
        and groups == 8
        and local_slots == 2
        and tokens_dev % 16 == 0
    ):
        mixed = one_kernel_layer(
            hidden_states.reshape(2 * tokens_dev, quarter),
            queries.reshape(2 * tokens_dev, queries.shape[2]),
            fresh_key_value,
            cache,
            cache_lengths,
            out_weight,
            router_weight,
            expert_weights,
            expert_ids,
            old_slots,
        )
        return mixed.reshape(2, tokens_dev, quarter)
    attention = attend_local(queries, fresh_key_value, cache, cache_lengths)
    head_terms = jnp.dot(
        attention,
        lax.all_gather(out_weight, "ep", axis=1, tiled=True),
        preferred_element_type=jnp.float32,
    )
    attn_out = lax.psum_scatter(
        head_terms.astype(jnp.bfloat16), "tp", scatter_dimension=1, tiled=True
    ).astype(jnp.float32)
    residual = (
        hidden_states.reshape(2 * tokens_dev, quarter).astype(jnp.float32) + attn_out
    ).astype(jnp.bfloat16)
    wide = residual.astype(jnp.float32)
    squares = lax.psum(jnp.sum(wide * wide, 1), "tp")
    normed = (wide * lax.rsqrt(squares / D + 1e-06)[:, None]).astype(jnp.bfloat16)
    logits = lax.psum(
        jnp.dot(normed, router_weight, preferred_element_type=jnp.float32).astype(jnp.bfloat16),
        "tp",
    ).astype(jnp.float32)
    selected = jnp.sum(
        jnp.where(
            routed[:, :, None] == jnp.arange(experts, dtype=jnp.int32)[None, None, :],
            logits[:, None, :],
            0.0,
        ),
        -1,
    )
    raised = jnp.exp(selected)
    combine = raised / jnp.sum(raised, 1, keepdims=True)
    outputs = []
    for lower in (0, tokens_dev):
        upper = lower + tokens_dev
        outputs.append(
            mix_block(
                normed[lower:upper],
                residual[lower:upper],
                routed[lower:upper],
                combine[lower:upper],
                old_slots,
                expert_weights,
                capacity,
                groups,
            )
        )
    return jnp.stack(outputs)


def solution(mesh):
    return jax.shard_map(
        per_device,
        mesh=mesh,
        in_specs=(
            P(None, ("rep", "ep"), "tp"),
            P(None, ("rep", "ep"), "tp"),
            P(None, ("rep", "ep"), None, "tp"),
            P(("rep", "ep"), None, None, "tp"),
            P(("rep", "ep")),
            P("tp", "ep"),
            P("tp", None),
            P("ep", None, "tp", None),
            P(None, ("rep", "ep"), None),
            P(),
            P(),
            P(),
        ),
        out_specs=P(None, ("rep", "ep"), "tp"),
        check_vma=False,
    )
```

```python
import functools

import jax
import jax.numpy as jnp
from jax import lax
from jax.experimental import pallas as pl
from jax.experimental.pallas import tpu as pltpu
from jax.sharding import PartitionSpec as P

D = 2048
HEAD_SIZE = 128


def lookup(entries, wanted_keys):
    return jnp.sum(
        jnp.where(
            wanted_keys[..., None] == jnp.arange(entries.shape[0], dtype=jnp.int32), entries, 0
        ),
        -1,
    )


def attend_local(queries, fresh_key_value, cache, cache_lengths):
    tokens_dev = queries.shape[1]
    kv_heads = fresh_key_value.shape[3] // HEAD_SIZE
    query_group_width = queries.shape[2] // HEAD_SIZE // kv_heads
    key_matrix = jnp.concatenate(
        [cache[0, 0], fresh_key_value[0, :, 0], fresh_key_value[1, :, 0]], 0
    )
    value_matrix = jnp.concatenate(
        [cache[0, 1], fresh_key_value[0, :, 1], fresh_key_value[1, :, 1]], 0
    )
    key_total = key_matrix.shape[0]
    context = cache.shape[2]
    query_matrix = queries.reshape(2 * tokens_dev, kv_heads, query_group_width, HEAD_SIZE)
    attention_scores = jnp.einsum(
        "meqt,wet->eqmw",
        query_matrix,
        key_matrix.reshape(key_total, kv_heads, HEAD_SIZE),
        preferred_element_type=jnp.float32,
    ) * HEAD_SIZE ** (-0.5)
    position = jnp.arange(key_total, dtype=jnp.int32)[None, :]
    row_index = jnp.arange(2 * tokens_dev, dtype=jnp.int32)[:, None]
    visible = jnp.where(
        position < context, position < cache_lengths[0], position - context <= row_index
    )
    attention_scores = jnp.where(visible, attention_scores, jnp.float32(-1e30))
    largest = jnp.max(attention_scores, -1, keepdims=True)
    weights = jnp.where(visible, jnp.exp(attention_scores - largest), jnp.float32(0.0))
    route_probability = (weights / jnp.sum(weights, -1, keepdims=True)).astype(jnp.bfloat16)
    layer_result = jnp.einsum(
        "qizo,oqx->zqix",
        route_probability,
        value_matrix.reshape(key_total, kv_heads, HEAD_SIZE),
        preferred_element_type=jnp.float32,
    )
    return layer_result.reshape(2 * tokens_dev, -1).astype(jnp.bfloat16)


def run_slots(weights, received):
    gate_up = jnp.einsum(
        "secq,egqf->secgf", received, weights[:, :2], preferred_element_type=jnp.float32
    )
    summed = lax.psum(gate_up.astype(jnp.bfloat16), "tp").astype(jnp.float32)
    hidden = (jax.nn.silu(summed[:, :, :, 0]) * summed[:, :, :, 1]).astype(jnp.bfloat16)
    layer_result = jnp.einsum(
        "secf,eqf->secq", hidden, weights[:, 2], preferred_element_type=jnp.float32
    ).astype(jnp.bfloat16)
    return lax.all_to_all(layer_result, "ep", split_axis=0, concat_axis=0, tiled=True)


def mix_block(normed_rows, resid_rows, routed, combine, slot_table, weights, capacity, groups):
    tokens_dev, top_count = routed.shape
    experts = slot_table.shape[0]
    local_slots = weights.shape[0]
    quarter = normed_rows.shape[1]
    slot_index = lookup(slot_table, routed)
    picked_mask = routed[:, :, None] == jnp.arange(experts, dtype=jnp.int32)[None, None, :]
    expert_marks = picked_mask.any(1).astype(jnp.bfloat16)
    earlier = (jnp.arange(tokens_dev)[:, None] > jnp.arange(tokens_dev)[None, :]).astype(
        jnp.bfloat16
    )
    before = jnp.dot(earlier, expert_marks, preferred_element_type=jnp.float32)
    slot_rank = jnp.sum(jnp.where(picked_mask, before[:, None, :], 0.0), -1).astype(jnp.int32)
    buffer_row = (slot_index * capacity + slot_rank).reshape(-1)
    buffer_rows = (
        jnp.zeros((groups * local_slots * capacity, quarter), jnp.bfloat16)
        .at[buffer_row]
        .set(jnp.repeat(normed_rows, top_count, axis=0))
    )
    outgoing = buffer_rows.reshape(groups, local_slots, capacity, quarter)
    returned = run_slots(
        weights, lax.all_to_all(outgoing, "ep", split_axis=0, concat_axis=0, tiled=True)
    )
    gathered = returned.reshape(-1, quarter)[buffer_row].reshape(tokens_dev, top_count, quarter)
    mixed_rows = resid_rows.astype(jnp.float32) + jnp.sum(
        combine[:, :, None] * gathered.astype(jnp.float32), 1
    )
    return mixed_rows.astype(jnp.bfloat16)


MESH = pl.DeviceIdType.MESH
PIECES = 4
LINE_PIECES = 4
WEIGHT_PIECES = 2


def line_order(planes):
    table = []
    for z in range(planes):
        table.append(
            sorted(
                range(planes),
                key=lambda t: (abs(t - z), (z if t < z else planes - 1 - z) if t != z else 0),
            )
        )
    return table


def gather_order(planes):
    tables = []
    for side in range(2):
        table = []
        for z in range(planes):
            rest = sorted(
                range(planes), key=lambda t: (t != z, t // (planes // 2) != side, abs(t - z))
            )
            table.append(rest)
        tables.append(table)
    return tables


def plane_at(table, z, p):
    value = jnp.int32(0)
    for i, row in enumerate(table):
        value = value + jnp.where(z == i, jnp.int32(row[p]), 0)
    return value


def layer_kernel(
    planes,
    tokens,
    head_group,
    queries,
    fresh,
    cache,
    lengths,
    out_weight,
    hidden_states,
    router,
    experts,
    routed,
    slots,
    out,
    keys,
    values,
    bias,
    attention,
    out_blocks,
    hidden_in,
    kept,
    parts_out,
    parts_in,
    resid,
    gate_up,
    down,
    routers,
    all_marks,
    hidden,
    product,
    own_total,
    core_out,
    core_in,
    line_out,
    line_in,
    local_sem,
    weight_send,
    weight_recv,
    weight_rep_send,
    weight_rep_recv,
    router_send,
    router_recv,
    rows_send,
    rows_recv,
    heads_send,
    heads_recv,
    marks_line_send,
    marks_line_recv,
    marks_core_send,
    marks_core_recv,
    block_line_send,
    block_line_recv,
    block_rep_send,
    block_rep_recv,
    parts_send,
    parts_recv,
    piece_line_send,
    piece_line_recv,
    piece_tp_send,
    piece_tp_recv,
    piece_core_send,
    piece_core_recv,
    hidden_send,
    hidden_recv,
    core_send,
    core_recv,
    line_send,
    line_recv,
):
    y, e, x = lax.axis_index("rep"), lax.axis_index("ep"), lax.axis_index("tp")
    z, c = e // 2, e % 2
    group = 2 * planes
    half_planes = planes // 2
    table = line_order(planes)
    width = out_weight.shape[1]
    depth = out_weight.shape[0]
    half = hidden_states.shape[1]
    has = (z > 0, z < planes - 1)
    beside = (e - 2, e + 2)
    tp_mate = (y, e, 1 - x)
    rep_mate = (1 - y, e, x)
    mate = e + 1 - 2 * c
    core_mate = (y, mate, x)
    chunk = depth // 2 // PIECES
    own_rows = pl.ds(pl.multiple_of(c * tokens, tokens), tokens)
    mate_rows = pl.ds(pl.multiple_of((1 - c) * tokens, tokens), tokens)

    def remote(src, dst, send, recv, target):
        return pltpu.make_async_remote_copy(
            src_ref=src,
            dst_ref=dst,
            send_sem=send,
            recv_sem=recv,
            device_id=target,
            device_id_type=MESH,
        )

    barrier = pltpu.get_barrier_semaphore()
    for target in (tp_mate, rep_mate, core_mate):
        pl.semaphore_signal(barrier, inc=1, device_id=target, device_id_type=MESH)
    for way in range(2):

        @pl.when(has[way])
        def _():
            pl.semaphore_signal(
                barrier, inc=1, device_id=(y, beside[way], x), device_id_type=MESH
            )

    context = cache.shape[2]
    local = [
        pltpu.make_async_copy(cache.at[0, 0], keys.at[pl.ds(0, context)], local_sem.at[0]),
        pltpu.make_async_copy(cache.at[0, 1], values.at[pl.ds(0, context)], local_sem.at[1]),
    ]
    late = [
        pltpu.make_async_copy(out_weight, out_blocks.at[z], local_sem.at[4]),
        pltpu.make_async_copy(hidden_states, hidden_in.at[own_rows], local_sem.at[5]),
        pltpu.make_async_copy(
            experts.at[x, pl.ds(0, 2)],
            gate_up.at[:, pl.ds(pl.multiple_of(x * half, half), half)],
            local_sem.at[6],
        ),
        pltpu.make_async_copy(experts.at[0, 2], down.at[0], local_sem.at[7]),
        pltpu.make_async_copy(experts.at[1, 2], down.at[1], local_sem.at[8]),
        pltpu.make_async_copy(
            router, routers.at[:, pl.ds(pl.multiple_of(x * half, half), half)], local_sem.at[9]
        ),
    ]
    for copy in local:
        copy.start()

    number = router.shape[0]
    eye = (
        lax.broadcasted_iota(jnp.int32, (number, number), 0)
        == lax.broadcasted_iota(jnp.int32, (number, number), 1)
    ).astype(jnp.bfloat16)
    blocks, top_count, block_tokens = routed.shape
    expert = lax.broadcasted_iota(jnp.int32, (number, block_tokens), 0)
    for block in range(blocks):
        named = jnp.zeros((number, block_tokens), jnp.int32)
        for k in range(top_count):
            named += (routed[block, k : k + 1, :] == expert).astype(jnp.int32)
        all_marks[e, :, block * block_tokens : (block + 1) * block_tokens] = named.astype(
            jnp.float32
        ).astype(jnp.bfloat16)

    pl.semaphore_wait(barrier, 3 + has[0].astype(jnp.int32) + has[1].astype(jnp.int32))

    def block_chunk(block, side, s):
        return out_blocks.at[
            block, pl.ds(pl.multiple_of(side * (depth // 2) + s * chunk, chunk), chunk)
        ]

    def block_line(block, s, way):
        piece = block_chunk(block, y, s)
        return remote(
            piece,
            piece,
            block_line_send.at[way, block, s],
            block_line_recv.at[block, s],
            (y, beside[way], x),
        )

    def block_own(s, way):
        return remote(
            out_weight.at[pl.ds(pl.multiple_of(y * (depth // 2) + s * chunk, chunk), chunk)],
            block_chunk(z, y, s),
            block_line_send.at[way, z, s],
            block_line_recv.at[z, s],
            (y, beside[way], x),
        )

    def block_rep(block, side, s):
        piece = block_chunk(block, side, s)
        return remote(piece, piece, block_rep_send.at[block, s], block_rep_recv.at[block, s], rep_mate)

    for s in range(PIECES):
        for way in range(2):
            pl.when(has[way])(block_own(s, way).start)
    rows_copy = remote(hidden_states, hidden_in.at[own_rows], rows_send, rows_recv, core_mate)
    rows_copy.start()
    def marks_line(t, way):
        ref = all_marks.at[2 * t + c]
        return remote(
            ref,
            ref,
            marks_line_send.at[way * planes + t],
            marks_line_recv.at[t],
            (y, beside[way], x),
        )

    def marks_core(t, core):
        ref = all_marks.at[2 * t + core]
        return remote(ref, ref, marks_core_send.at[t], marks_core_recv.at[t], core_mate)

    for way in range(2):
        pl.when(has[way])(marks_line(z, way).start)
    marks_core(z, c).start()
    router_copy = remote(
        router,
        routers.at[:, pl.ds(pl.multiple_of(x * half, half), half)],
        router_send,
        router_recv,
        tp_mate,
    )
    router_copy.start()
    share_rows = half // (2 * WEIGHT_PIECES)

    def weight_share(kind, s, tp_side, rep_side):
        start = tp_side * half + (rep_side * WEIGHT_PIECES + s) * share_rows
        return gate_up.at[kind, pl.ds(pl.multiple_of(start, share_rows), share_rows)]

    def weight_tp(kind, s):
        start = pl.multiple_of((y * WEIGHT_PIECES + s) * share_rows, share_rows)
        return remote(
            experts.at[1 - x, kind, pl.ds(start, share_rows)],
            weight_share(kind, s, x, y),
            weight_send.at[kind, s],
            weight_recv.at[kind, s],
            tp_mate,
        )

    def weight_rep(kind, s, side):
        ref = weight_share(kind, s, 1 - x, side)
        return remote(
            ref, ref, weight_rep_send.at[kind, s], weight_rep_recv.at[kind, s], rep_mate
        )

    weight_list = [(kind, s) for s in range(WEIGHT_PIECES) for kind in range(2)]
    for kind, s in weight_list:
        weight_tp(kind, s).start()
    for copy in late:
        copy.start()

    key_total = keys.shape[0]
    position = lax.broadcasted_iota(jnp.int32, (tokens, key_total), 1)
    row = lax.broadcasted_iota(jnp.int32, (tokens, key_total), 0)
    visible = jnp.where(
        position < context,
        (position < lengths[0]).astype(jnp.int32),
        (position - context <= row).astype(jnp.int32),
    )
    bias[...] = jnp.where(visible > 0, jnp.float32(0.0), jnp.float32(-1e30))
    for block in range(blocks):
        start = context + block * block_tokens
        keys[start : start + block_tokens] = fresh[block, :, 0, :]
        values[start : start + block_tokens] = fresh[block, :, 1, :]
    for copy in local:
        copy.wait()
    kv_heads = keys.shape[1] // HEAD_SIZE

    def attend(kv, first, count):
        key_part = keys[:, kv * HEAD_SIZE : (kv + 1) * HEAD_SIZE]
        value_part = values[:, kv * HEAD_SIZE : (kv + 1) * HEAD_SIZE]

        def one(q, _):
            column = pl.ds(
                pl.multiple_of((kv * head_group + q) * HEAD_SIZE, HEAD_SIZE), HEAD_SIZE
            )
            query = queries[:, column]
            scores = (
                lax.dot_general(
                    query, key_part, (((1,), (1,)), ((), ())), preferred_element_type=jnp.float32
                )
                * HEAD_SIZE ** (-0.5)
                + bias[...]
            )
            raised = jnp.exp(scores - jnp.max(scores, -1, keepdims=True))
            total = jnp.sum(raised, -1, keepdims=True)
            mixed = jnp.dot(
                raised.astype(jnp.bfloat16), value_part, preferred_element_type=jnp.float32
            )
            attention[own_rows, column] = (mixed / total).astype(jnp.bfloat16)
            return 0

        lax.fori_loop(first, first + count, one, 0)

    def take_chunk(p, s):
        block = plane_at(table, z, p)
        block_line(block, s, 0).wait_recv()
        pl.when((block > z) & has[0])(block_line(block, s, 0).start)
        pl.when((block < z) & has[1])(block_line(block, s, 1).start)
        block_rep(block, y, s).start()
        if s == PIECES - 1:
            marks_line(block, 0).wait_recv()
            pl.when((block > z) & has[0])(marks_line(block, 0).start)
            pl.when((block < z) & has[1])(marks_line(block, 1).start)
            marks_core(block, c).start()

    heads_copy = remote(
        attention.at[own_rows], attention.at[own_rows], heads_send, heads_recv, core_mate
    )
    at_end = (z == 0) | (z == planes - 1)
    inside = (z > 0) & (z < planes - 1)
    section = kv_heads * head_group // PIECES
    for s in range(PIECES):
        attend(s * section // head_group, s * section % head_group, section)
        if s == PIECES - 1:
            heads_copy.start()
        take_chunk(1, s)
        pl.when(inside)(functools.partial(take_chunk, 2, s))

    def column_block(side, core, b):
        return 2 * (half_planes * side + b) + core

    def piece(t, side, core, b):
        start = pl.multiple_of(column_block(side, core, b) * width, width)
        return resid.at[t, :, pl.ds(start, width)]

    def piece_line(t, b, way):
        ref = piece(t, x, c, b)
        return remote(
            ref,
            ref,
            piece_line_send.at[way, t, b],
            piece_line_recv.at[t, b],
            (y, beside[way], x),
        )

    def piece_tp(t, b, side):
        ref = piece(t, side, c, b)
        return remote(ref, ref, piece_tp_send.at[t, b], piece_tp_recv.at[t, b], tp_mate)

    def piece_core(t, b, kind, core):
        ref = piece(t, x if kind == 0 else 1 - x, core, b)
        return remote(
            ref, ref, piece_core_send.at[kind, t, b], piece_core_recv.at[kind, t, b], core_mate
        )

    def parts_copy(b):
        return remote(parts_out.at[b], parts_in.at[b], parts_send.at[b], parts_recv.at[b], tp_mate)

    def project(p):
        block = plane_at(table, z, p)
        if p == 0:
            late[0].wait()
            heads_copy.wait_recv()
        else:
            for s in range(PIECES):
                block_rep(block, 1 - y, s).wait_recv()
        part = jnp.dot(attention[...], out_blocks[block], preferred_element_type=jnp.float32)
        b = block % half_planes
        mine = block // half_planes == x

        @pl.when(mine)
        def _():
            kept[b] = part

        @pl.when(block // half_planes != x)
        def _():
            parts_out[b] = part.astype(jnp.bfloat16)
            parts_copy(b).start()

    def settle(p):
        block = plane_at(table, z, p)
        b = block % half_planes

        @pl.when(block // half_planes == x)
        def _():
            parts_copy(b).wait_recv()
            start = pl.multiple_of((2 * b + c) * width, width)
            summed = (
                hidden_in[:, pl.ds(start, width)].astype(jnp.float32)
                + kept[b]
                + parts_in[b].astype(jnp.float32)
            )
            target = pl.multiple_of(column_block(x, c, b) * width, width)
            resid[z, :, pl.ds(target, width)] = summed.astype(jnp.bfloat16)
            for way in range(2):
                pl.when(has[way])(piece_line(z, b, way).start)
            piece_tp(z, b, x).start()
            piece_core(z, b, 0, c).start()

    late[1].wait()
    rows_copy.wait_recv()
    gather_first, gather_second = gather_order(planes)

    def gather_at(side, q):
        return jnp.where(
            side == 0, plane_at(gather_first, z, q), plane_at(gather_second, z, q)
        )

    def take_plane(t):
        for i in range(half_planes):
            b = x * i + (1 - x) * (half_planes - 1 - i)
            piece_line(t, b, 0).wait_recv()
            pl.when((t > z) & has[0])(piece_line(t, b, 0).start)
            pl.when((t < z) & has[1])(piece_line(t, b, 1).start)
            piece_tp(t, b, x).start()
            piece_core(t, b, 0, c).start()

    nearest = gather_at(x, 1)
    direct = (nearest == z + 1) | (nearest == z - 1)
    project(0)
    for p in range(2, planes):
        for s in range(PIECES):
            if p == 2:
                pl.when(at_end)(functools.partial(take_chunk, p, s))
            else:
                take_chunk(p, s)
            if s == 0 and p > 2:
                project(p - 2)
            if s == PIECES - 2:
                settle(p - 2)
    for kind, s in weight_list:
        weight_tp(kind, s).wait_recv()
        weight_rep(kind, s, y).start()
    project(planes - 2)
    project(planes - 1)
    settle(planes - 2)
    pl.when(direct)(functools.partial(take_plane, nearest))
    settle(planes - 1)

    for q in range(1, planes + 1):
        if q == 1:
            pl.when(jnp.logical_not(direct))(functools.partial(take_plane, nearest))
        elif q < planes:
            take_plane(gather_at(x, q))
        t = gather_at(1 - x, q - 1)
        for b in range(half_planes):
            piece_tp(t, b, 1 - x).wait_recv()
            piece_core(t, b, 1, c).start()

    for copy in late[2:]:
        copy.wait()
    for kind, s in weight_list:
        weight_rep(kind, s, 1 - y).wait_recv()
    router_copy.wait_recv()
    for t in range(planes):
        marks_core(t, 1 - c).wait_recv()
    def hidden_copy(t, side):
        ref = hidden.at[side, t]
        return remote(ref, ref, hidden_send.at[t], hidden_recv.at[t], tp_mate)

    def open_plane(t):
        for b in range(half_planes):
            for kind in range(2):
                piece_core(t, b, kind, 1 - c).wait_recv()
        rows = resid[t]
        wide = rows.astype(jnp.float32)
        scale = lax.rsqrt(jnp.sum(wide * wide, 1, keepdims=True) / D + 1e-06)
        gate = jnp.dot(rows, gate_up[0], preferred_element_type=jnp.float32) * scale
        up = jnp.dot(rows, gate_up[1], preferred_element_type=jnp.float32) * scale
        logits = (
            lax.dot_general(
                rows, routers[...], (((1,), (1,)), ((), ())), preferred_element_type=jnp.float32
            )
            * scale
        )
        chosen = jnp.concatenate(
            [
                lax.dot_general(
                    all_marks[2 * t + core],
                    eye,
                    (((0,), (0,)), ((), ())),
                    preferred_element_type=jnp.float32,
                )
                for core in range(2)
            ],
            0,
        )
        raised = jnp.where(chosen > 0.5, jnp.exp(logits), 0.0)
        share = jnp.sum(
            jnp.where(slots[...] == 2 * e + x, raised, 0.0), 1, keepdims=True
        ) / jnp.sum(raised, 1, keepdims=True)
        hidden[x, t] = (gate / (1.0 + jnp.exp(-gate)) * up * share).astype(jnp.bfloat16)
        hidden_copy(t, x).start()

    for p in reversed(range(planes)):
        open_plane(plane_at(table, z, p))

    def core_copy(t):
        return remote(core_out.at[t], core_in.at[t], core_send.at[t], core_recv.at[t], core_mate)

    part_width = half // LINE_PIECES

    def line_copy(t, i, way):
        columns = pl.ds(i * part_width, part_width)
        return remote(
            line_out.at[t, :, columns],
            line_in.at[way, t, :, columns],
            line_send.at[t, i],
            line_recv.at[way, t, i],
            (y, beside[way], x),
        )

    def close_plane(t):
        hidden_copy(t, 1 - x).wait_recv()
        product[...] = lax.dot_general(
            hidden[0, t], down[0], (((1,), (1,)), ((), ())), preferred_element_type=jnp.float32
        ) + lax.dot_general(
            hidden[1, t], down[1], (((1,), (1,)), ((), ())), preferred_element_type=jnp.float32
        )
        core_out[t] = product[mate_rows].astype(jnp.bfloat16)
        core_copy(t).start()
        own_total[t] = product[own_rows]

    def pass_on(t):
        core_copy(t).wait_recv()
        for i in range(LINE_PIECES):
            columns = pl.ds(i * part_width, part_width)
            own_total[t, :, columns] += core_in[t, :, columns].astype(jnp.float32)

            @pl.when((t >= z) & has[0])
            def _():
                line_copy(t, i, 1).wait_recv()
                own_total[t, :, columns] += line_in[1, t, :, columns].astype(jnp.float32)

            @pl.when((t <= z) & has[1])
            def _():
                line_copy(t, i, 0).wait_recv()
                own_total[t, :, columns] += line_in[0, t, :, columns].astype(jnp.float32)

            @pl.when(t != z)
            def _():
                line_out[t, :, columns] = own_total[t, :, columns].astype(jnp.bfloat16)

            pl.when(t > z)(line_copy(t, i, 1).start)
            pl.when(t < z)(line_copy(t, i, 0).start)

    for p in reversed(range(planes)):
        close_plane(plane_at(table, z, p))
        if p > 0:
            pl.when(at_end)(functools.partial(pass_on, plane_at(table, z, p)))
        if p + 1 < planes:
            pl.when(inside)(functools.partial(pass_on, plane_at(table, z, p + 1)))
    pass_on(z)
    own_resid = resid[z, own_rows, pl.ds(pl.multiple_of(x * half, half), half)]
    out[...] = (own_resid.astype(jnp.float32) + own_total[z]).astype(jnp.bfloat16)

    rows_copy.wait_send()
    heads_copy.wait_send()
    router_copy.wait_send()
    for kind, s in weight_list:
        weight_tp(kind, s).wait_send()
        weight_rep(kind, s, y).wait_send()
    for t in range(planes):
        marks_core(t, c).wait_send()
    for way in range(2):
        pl.when(has[way])(marks_line(z, way).wait_send)
    for s in range(PIECES):
        for way in range(2):
            pl.when(has[way])(block_own(s, way).wait_send)
    for p in range(1, planes):
        t = plane_at(table, z, p)
        pl.when((t > z) & has[0])(marks_line(t, 0).wait_send)
        pl.when((t < z) & has[1])(marks_line(t, 1).wait_send)
        for s in range(PIECES):
            pl.when((t > z) & has[0])(block_line(t, s, 0).wait_send)
            pl.when((t < z) & has[1])(block_line(t, s, 1).wait_send)
            block_rep(t, y, s).wait_send()
        for b in range(half_planes):
            pl.when((t > z) & has[0])(piece_line(t, b, 0).wait_send)
            pl.when((t < z) & has[1])(piece_line(t, b, 1).wait_send)
        for i in range(LINE_PIECES):
            pl.when(t > z)(line_copy(t, i, 1).wait_send)
            pl.when(t < z)(line_copy(t, i, 0).wait_send)
    for b in range(half_planes):
        parts_copy(b).wait_send()
        for way in range(2):
            pl.when(has[way])(piece_line(z, b, way).wait_send)
    for t in range(planes):
        for b in range(half_planes):
            piece_tp(t, b, x).wait_send()
            piece_core(t, b, 0, c).wait_send()
            piece_core(t, b, 1, c).wait_send()
        hidden_copy(t, x).wait_send()
        core_copy(t).wait_send()


def one_kernel_layer(
    hidden_states, queries, fresh_key_value, cache, lengths, out_weight, router, experts, expert_ids, slots
):
    group = lax.axis_size("ep")
    planes = group // 2
    half_planes = planes // 2
    tokens, half = hidden_states.shape
    depth, width = out_weight.shape
    number = router.shape[1]
    kv_width = cache.shape[3]
    key_total = cache.shape[2] + tokens
    units = experts.shape[3]
    vmem, anywhere = (pl.BlockSpec(memory_space=m) for m in (pltpu.VMEM, pl.ANY))
    dma = pltpu.SemaphoreType.DMA
    bf16, f32 = jnp.bfloat16, jnp.float32
    return pl.pallas_call(
        functools.partial(layer_kernel, planes, tokens, queries.shape[1] // kv_width),
        out_shape=jax.ShapeDtypeStruct((tokens, half), bf16),
        in_specs=[
            vmem,
            vmem,
            anywhere,
            pl.BlockSpec(memory_space=pltpu.SMEM),
            anywhere,
            anywhere,
            vmem,
            anywhere,
            vmem,
            vmem,
        ],
        out_specs=vmem,
        scratch_shapes=[
            pltpu.VMEM((key_total, kv_width), bf16),
            pltpu.VMEM((key_total, kv_width), bf16),
            pltpu.VMEM((tokens, key_total), f32),
            pltpu.VMEM((2 * tokens, depth), bf16),
            pltpu.VMEM((planes, depth, width), bf16),
            pltpu.VMEM((2 * tokens, half), bf16),
            pltpu.VMEM((half_planes, 2 * tokens, width), f32),
            pltpu.VMEM((half_planes, 2 * tokens, width), bf16),
            pltpu.VMEM((half_planes, 2 * tokens, width), bf16),
            pltpu.VMEM((planes, 2 * tokens, 2 * half), bf16),
            pltpu.VMEM((2, 2 * half, units), bf16),
            pltpu.VMEM((2, half, units), bf16),
            pltpu.VMEM((number, 2 * half), bf16),
            pltpu.VMEM((group, number, tokens), bf16),
            pltpu.VMEM((2, planes, 2 * tokens, units), bf16),
            pltpu.VMEM((2 * tokens, half), f32),
            pltpu.VMEM((planes, tokens, half), f32),
            pltpu.VMEM((planes, tokens, half), bf16),
            pltpu.VMEM((planes, tokens, half), bf16),
            pltpu.VMEM((planes, tokens, half), bf16),
            pltpu.VMEM((2, planes, tokens, half), bf16),
            dma((10,)),
            dma((2, WEIGHT_PIECES)),
            dma((2, WEIGHT_PIECES)),
            dma((2, WEIGHT_PIECES)),
            dma((2, WEIGHT_PIECES)),
            dma,
            dma,
            dma,
            dma,
            dma,
            dma,
            dma((2 * planes,)),
            dma((planes,)),
            dma((planes,)),
            dma((planes,)),
            dma((2, planes, PIECES)),
            dma((planes, PIECES)),
            dma((planes, PIECES)),
            dma((planes, PIECES)),
            dma((half_planes,)),
            dma((half_planes,)),
            dma((2, planes, half_planes)),
            dma((planes, half_planes)),
            dma((planes, half_planes)),
            dma((planes, half_planes)),
            dma((2, planes, half_planes)),
            dma((2, planes, half_planes)),
            dma((planes,)),
            dma((planes,)),
            dma((planes,)),
            dma((planes,)),
            dma((planes, LINE_PIECES)),
            dma((2, planes, LINE_PIECES)),
        ],
        compiler_params=pltpu.CompilerParams(
            collective_id=0, has_side_effects=True, vmem_limit_bytes=56 * 1024 * 1024
        ),
    )(
        queries,
        fresh_key_value,
        cache,
        lengths,
        out_weight,
        hidden_states,
        router.T,
        experts,
        jnp.swapaxes(expert_ids, 1, 2),
        slots.reshape(1, number),
    )


def per_device(
    hidden_states,
    queries,
    fresh_key_value,
    cache,
    cache_lengths,
    out_weight,
    router_weight,
    expert_weights,
    expert_ids,
    old_slots,
    new_slots,
    moved_experts,
):
    tokens_dev = hidden_states.shape[1]
    quarter = hidden_states.shape[2]
    experts = router_weight.shape[1]
    top_count = expert_ids.shape[2]
    groups = lax.axis_size("ep")
    local_slots = expert_weights.shape[0]
    capacity = min(tokens_dev, 3 * tokens_dev * top_count // (2 * experts))
    routed = expert_ids.reshape(2 * tokens_dev, top_count)
    if (
        lax.axis_size("rep") == 2
        and lax.axis_size("tp") == 2
        and groups == 8
        and local_slots == 2
        and tokens_dev % 16 == 0
    ):
        mixed = one_kernel_layer(
            hidden_states.reshape(2 * tokens_dev, quarter),
            queries.reshape(2 * tokens_dev, queries.shape[2]),
            fresh_key_value,
            cache,
            cache_lengths,
            out_weight,
            router_weight,
            expert_weights,
            expert_ids,
            old_slots,
        )
        return mixed.reshape(2, tokens_dev, quarter)
    attention = attend_local(queries, fresh_key_value, cache, cache_lengths)
    head_terms = jnp.dot(
        attention,
        lax.all_gather(out_weight, "ep", axis=1, tiled=True),
        preferred_element_type=jnp.float32,
    )
    attn_out = lax.psum_scatter(
        head_terms.astype(jnp.bfloat16), "tp", scatter_dimension=1, tiled=True
    ).astype(jnp.float32)
    residual = (
        hidden_states.reshape(2 * tokens_dev, quarter).astype(jnp.float32) + attn_out
    ).astype(jnp.bfloat16)
    wide = residual.astype(jnp.float32)
    squares = lax.psum(jnp.sum(wide * wide, 1), "tp")
    normed = (wide * lax.rsqrt(squares / D + 1e-06)[:, None]).astype(jnp.bfloat16)
    logits = lax.psum(
        jnp.dot(normed, router_weight, preferred_element_type=jnp.float32).astype(jnp.bfloat16),
        "tp",
    ).astype(jnp.float32)
    selected = jnp.sum(
        jnp.where(
            routed[:, :, None] == jnp.arange(experts, dtype=jnp.int32)[None, None, :],
            logits[:, None, :],
            0.0,
        ),
        -1,
    )
    raised = jnp.exp(selected)
    combine = raised / jnp.sum(raised, 1, keepdims=True)
    outputs = []
    for lower in (0, tokens_dev):
        upper = lower + tokens_dev
        outputs.append(
            mix_block(
                normed[lower:upper],
                residual[lower:upper],
                routed[lower:upper],
                combine[lower:upper],
                old_slots,
                expert_weights,
                capacity,
                groups,
            )
        )
    return jnp.stack(outputs)


def solution(mesh):
    return jax.shard_map(
        per_device,
        mesh=mesh,
        in_specs=(
            P(None, ("rep", "ep"), "tp"),
            P(None, ("rep", "ep"), "tp"),
            P(None, ("rep", "ep"), None, "tp"),
            P(("rep", "ep"), None, None, "tp"),
            P(("rep", "ep")),
            P("tp", "ep"),
            P("tp", None),
            P("ep", None, "tp", None),
            P(None, ("rep", "ep"), None),
            P(),
            P(),
            P(),
        ),
        out_specs=P(None, ("rep", "ep"), "tp"),
        check_vma=False,
    )
```

```python
import functools

import jax
import jax.numpy as jnp
from jax import lax
from jax.experimental import pallas as pl
from jax.experimental.pallas import tpu as pltpu
from jax.sharding import PartitionSpec as P

D = 2048
HEAD_SIZE = 128


def lookup(entries, wanted_keys):
    return jnp.sum(
        jnp.where(
            wanted_keys[..., None] == jnp.arange(entries.shape[0], dtype=jnp.int32), entries, 0
        ),
        -1,
    )


def attend_local(queries, fresh_key_value, cache, cache_lengths):
    tokens_dev = queries.shape[1]
    kv_heads = fresh_key_value.shape[3] // HEAD_SIZE
    query_group_width = queries.shape[2] // HEAD_SIZE // kv_heads
    key_matrix = jnp.concatenate(
        [cache[0, 0], fresh_key_value[0, :, 0], fresh_key_value[1, :, 0]], 0
    )
    value_matrix = jnp.concatenate(
        [cache[0, 1], fresh_key_value[0, :, 1], fresh_key_value[1, :, 1]], 0
    )
    key_total = key_matrix.shape[0]
    context = cache.shape[2]
    query_matrix = queries.reshape(2 * tokens_dev, kv_heads, query_group_width, HEAD_SIZE)
    attention_scores = jnp.einsum(
        "meqt,wet->eqmw",
        query_matrix,
        key_matrix.reshape(key_total, kv_heads, HEAD_SIZE),
        preferred_element_type=jnp.float32,
    ) * HEAD_SIZE ** (-0.5)
    position = jnp.arange(key_total, dtype=jnp.int32)[None, :]
    row_index = jnp.arange(2 * tokens_dev, dtype=jnp.int32)[:, None]
    visible = jnp.where(
        position < context, position < cache_lengths[0], position - context <= row_index
    )
    attention_scores = jnp.where(visible, attention_scores, jnp.float32(-1e30))
    largest = jnp.max(attention_scores, -1, keepdims=True)
    weights = jnp.where(visible, jnp.exp(attention_scores - largest), jnp.float32(0.0))
    route_probability = (weights / jnp.sum(weights, -1, keepdims=True)).astype(jnp.bfloat16)
    layer_result = jnp.einsum(
        "qizo,oqx->zqix",
        route_probability,
        value_matrix.reshape(key_total, kv_heads, HEAD_SIZE),
        preferred_element_type=jnp.float32,
    )
    return layer_result.reshape(2 * tokens_dev, -1).astype(jnp.bfloat16)


def run_slots(weights, received):
    gate_up = jnp.einsum(
        "secq,egqf->secgf", received, weights[:, :2], preferred_element_type=jnp.float32
    )
    summed = lax.psum(gate_up.astype(jnp.bfloat16), "tp").astype(jnp.float32)
    hidden = (jax.nn.silu(summed[:, :, :, 0]) * summed[:, :, :, 1]).astype(jnp.bfloat16)
    layer_result = jnp.einsum(
        "secf,eqf->secq", hidden, weights[:, 2], preferred_element_type=jnp.float32
    ).astype(jnp.bfloat16)
    return lax.all_to_all(layer_result, "ep", split_axis=0, concat_axis=0, tiled=True)


def mix_block(normed_rows, resid_rows, routed, combine, slot_table, weights, capacity, groups):
    tokens_dev, top_count = routed.shape
    experts = slot_table.shape[0]
    local_slots = weights.shape[0]
    quarter = normed_rows.shape[1]
    slot_index = lookup(slot_table, routed)
    picked_mask = routed[:, :, None] == jnp.arange(experts, dtype=jnp.int32)[None, None, :]
    expert_marks = picked_mask.any(1).astype(jnp.bfloat16)
    earlier = (jnp.arange(tokens_dev)[:, None] > jnp.arange(tokens_dev)[None, :]).astype(
        jnp.bfloat16
    )
    before = jnp.dot(earlier, expert_marks, preferred_element_type=jnp.float32)
    slot_rank = jnp.sum(jnp.where(picked_mask, before[:, None, :], 0.0), -1).astype(jnp.int32)
    buffer_row = (slot_index * capacity + slot_rank).reshape(-1)
    buffer_rows = (
        jnp.zeros((groups * local_slots * capacity, quarter), jnp.bfloat16)
        .at[buffer_row]
        .set(jnp.repeat(normed_rows, top_count, axis=0))
    )
    outgoing = buffer_rows.reshape(groups, local_slots, capacity, quarter)
    returned = run_slots(
        weights, lax.all_to_all(outgoing, "ep", split_axis=0, concat_axis=0, tiled=True)
    )
    gathered = returned.reshape(-1, quarter)[buffer_row].reshape(tokens_dev, top_count, quarter)
    mixed_rows = resid_rows.astype(jnp.float32) + jnp.sum(
        combine[:, :, None] * gathered.astype(jnp.float32), 1
    )
    return mixed_rows.astype(jnp.bfloat16)


MESH = pl.DeviceIdType.MESH
PIECES = 4
LINE_PIECES = 4
WEIGHT_PIECES = 2


def line_order(planes):
    table = []
    for z in range(planes):
        table.append(
            sorted(
                range(planes),
                key=lambda t: (abs(t - z), (z if t < z else planes - 1 - z) if t != z else 0),
            )
        )
    return table


def gather_order(planes):
    tables = []
    for side in range(2):
        table = []
        for z in range(planes):
            rest = sorted(
                range(planes), key=lambda t: (t != z, t // (planes // 2) != side, abs(t - z))
            )
            table.append(rest)
        tables.append(table)
    return tables


def plane_at(table, z, p):
    value = jnp.int32(0)
    for i, row in enumerate(table):
        value = value + jnp.where(z == i, jnp.int32(row[p]), 0)
    return value


def layer_kernel(
    planes,
    tokens,
    head_group,
    queries,
    fresh,
    cache,
    lengths,
    out_weight,
    hidden_states,
    router,
    experts,
    routed,
    slots,
    out,
    keys,
    values,
    bias,
    attention,
    out_blocks,
    hidden_in,
    kept,
    parts_out,
    parts_in,
    resid,
    gate_up,
    down,
    routers,
    all_marks,
    hidden,
    product,
    own_total,
    core_out,
    core_in,
    line_out,
    line_in,
    local_sem,
    weight_send,
    weight_recv,
    weight_rep_send,
    weight_rep_recv,
    router_send,
    router_recv,
    rows_send,
    rows_recv,
    heads_send,
    heads_recv,
    marks_line_send,
    marks_line_recv,
    marks_core_send,
    marks_core_recv,
    block_line_send,
    block_line_recv,
    block_rep_send,
    block_rep_recv,
    parts_send,
    parts_recv,
    piece_line_send,
    piece_line_recv,
    piece_tp_send,
    piece_tp_recv,
    piece_core_send,
    piece_core_recv,
    hidden_send,
    hidden_recv,
    core_send,
    core_recv,
    line_send,
    line_recv,
):
    y, e, x = lax.axis_index("rep"), lax.axis_index("ep"), lax.axis_index("tp")
    z, c = e // 2, e % 2
    group = 2 * planes
    half_planes = planes // 2
    table = line_order(planes)
    width = out_weight.shape[1]
    depth = out_weight.shape[0]
    half = hidden_states.shape[1]
    ffw = experts.shape[3]
    has = (z > 0, z < planes - 1)
    beside = (e - 2, e + 2)
    tp_mate = (y, e, 1 - x)
    rep_mate = (1 - y, e, x)
    mate = e + 1 - 2 * c
    core_mate = (y, mate, x)
    chunk = depth // 2 // PIECES
    own_rows = pl.ds(pl.multiple_of(c * tokens, tokens), tokens)
    mate_rows = pl.ds(pl.multiple_of((1 - c) * tokens, tokens), tokens)

    def remote(src, dst, send, recv, target):
        return pltpu.make_async_remote_copy(
            src_ref=src,
            dst_ref=dst,
            send_sem=send,
            recv_sem=recv,
            device_id=target,
            device_id_type=MESH,
        )

    barrier = pltpu.get_barrier_semaphore()
    for target in (tp_mate, rep_mate, core_mate):
        pl.semaphore_signal(barrier, inc=1, device_id=target, device_id_type=MESH)
    for way in range(2):

        @pl.when(has[way])
        def _():
            pl.semaphore_signal(
                barrier, inc=1, device_id=(y, beside[way], x), device_id_type=MESH
            )

    context = cache.shape[2]
    local = [
        pltpu.make_async_copy(cache.at[0, 0], keys.at[pl.ds(0, context)], local_sem.at[0]),
        pltpu.make_async_copy(cache.at[0, 1], values.at[pl.ds(0, context)], local_sem.at[1]),
    ]
    late = [
        pltpu.make_async_copy(out_weight, out_blocks.at[z], local_sem.at[4]),
        pltpu.make_async_copy(hidden_states, hidden_in.at[own_rows], local_sem.at[5]),
        pltpu.make_async_copy(
            experts.at[x, 0],
            gate_up.at[pl.ds(pl.multiple_of(x * half, half), half), pl.ds(0, ffw)],
            local_sem.at[6],
        ),
        pltpu.make_async_copy(
            experts.at[x, 1],
            gate_up.at[pl.ds(pl.multiple_of(x * half, half), half), pl.ds(ffw, ffw)],
            local_sem.at[10],
        ),
        pltpu.make_async_copy(experts.at[0, 2], down.at[0], local_sem.at[7]),
        pltpu.make_async_copy(experts.at[1, 2], down.at[1], local_sem.at[8]),
        pltpu.make_async_copy(
            router, routers.at[:, pl.ds(pl.multiple_of(x * half, half), half)], local_sem.at[9]
        ),
    ]
    for copy in local:
        copy.start()

    number = router.shape[0]
    eye = (
        lax.broadcasted_iota(jnp.int32, (number, number), 0)
        == lax.broadcasted_iota(jnp.int32, (number, number), 1)
    ).astype(jnp.bfloat16)
    blocks, top_count, block_tokens = routed.shape
    expert = lax.broadcasted_iota(jnp.int32, (number, block_tokens), 0)
    for block in range(blocks):
        named = jnp.zeros((number, block_tokens), jnp.int32)
        for k in range(top_count):
            named += (routed[block, k : k + 1, :] == expert).astype(jnp.int32)
        all_marks[e, :, block * block_tokens : (block + 1) * block_tokens] = named.astype(
            jnp.float32
        ).astype(jnp.bfloat16)

    pl.semaphore_wait(barrier, 3 + has[0].astype(jnp.int32) + has[1].astype(jnp.int32))

    def block_chunk(block, side, s):
        return out_blocks.at[
            block, pl.ds(pl.multiple_of(side * (depth // 2) + s * chunk, chunk), chunk)
        ]

    def block_line(block, s, way):
        piece = block_chunk(block, y, s)
        return remote(
            piece,
            piece,
            block_line_send.at[way, block, s],
            block_line_recv.at[block, s],
            (y, beside[way], x),
        )

    def block_own(s, way):
        return remote(
            out_weight.at[pl.ds(pl.multiple_of(y * (depth // 2) + s * chunk, chunk), chunk)],
            block_chunk(z, y, s),
            block_line_send.at[way, z, s],
            block_line_recv.at[z, s],
            (y, beside[way], x),
        )

    def block_rep(block, side, s):
        piece = block_chunk(block, side, s)
        return remote(piece, piece, block_rep_send.at[block, s], block_rep_recv.at[block, s], rep_mate)

    for s in range(PIECES):
        for way in range(2):
            pl.when(has[way])(block_own(s, way).start)
    rows_copy = remote(hidden_states, hidden_in.at[own_rows], rows_send, rows_recv, core_mate)
    rows_copy.start()
    def marks_line(t, way):
        ref = all_marks.at[2 * t + c]
        return remote(
            ref,
            ref,
            marks_line_send.at[way * planes + t],
            marks_line_recv.at[t],
            (y, beside[way], x),
        )

    def marks_core(t, core):
        ref = all_marks.at[2 * t + core]
        return remote(ref, ref, marks_core_send.at[t], marks_core_recv.at[t], core_mate)

    for way in range(2):
        pl.when(has[way])(marks_line(z, way).start)
    marks_core(z, c).start()
    router_copy = remote(
        router,
        routers.at[:, pl.ds(pl.multiple_of(x * half, half), half)],
        router_send,
        router_recv,
        tp_mate,
    )
    router_copy.start()
    share_rows = half // (2 * WEIGHT_PIECES)

    def weight_share(kind, s, tp_side, rep_side):
        start = tp_side * half + (rep_side * WEIGHT_PIECES + s) * share_rows
        rows = pl.ds(pl.multiple_of(start, share_rows), share_rows)
        return gate_up.at[rows, pl.ds(kind * ffw, ffw)]

    def weight_tp(kind, s):
        start = pl.multiple_of((y * WEIGHT_PIECES + s) * share_rows, share_rows)
        return remote(
            experts.at[1 - x, kind, pl.ds(start, share_rows)],
            weight_share(kind, s, x, y),
            weight_send.at[kind, s],
            weight_recv.at[kind, s],
            tp_mate,
        )

    def weight_rep(kind, s, side):
        ref = weight_share(kind, s, 1 - x, side)
        return remote(
            ref, ref, weight_rep_send.at[kind, s], weight_rep_recv.at[kind, s], rep_mate
        )

    weight_list = [(kind, s) for s in range(WEIGHT_PIECES) for kind in range(2)]
    for kind, s in weight_list:
        weight_tp(kind, s).start()
    for copy in late:
        copy.start()

    key_total = keys.shape[0]
    position = lax.broadcasted_iota(jnp.int32, (tokens, key_total), 1)
    row = lax.broadcasted_iota(jnp.int32, (tokens, key_total), 0)
    visible = jnp.where(
        position < context,
        (position < lengths[0]).astype(jnp.int32),
        (position - context <= row).astype(jnp.int32),
    )
    bias[...] = jnp.where(visible > 0, jnp.float32(0.0), jnp.float32(-1e30))
    for block in range(blocks):
        start = context + block * block_tokens
        keys[start : start + block_tokens] = fresh[block, :, 0, :]
        values[start : start + block_tokens] = fresh[block, :, 1, :]
    for copy in local:
        copy.wait()
    kv_heads = keys.shape[1] // HEAD_SIZE

    def attend(kv, first, count):
        key_part = keys[:, kv * HEAD_SIZE : (kv + 1) * HEAD_SIZE]
        value_part = values[:, kv * HEAD_SIZE : (kv + 1) * HEAD_SIZE]

        def one(q, _):
            column = pl.ds(
                pl.multiple_of((kv * head_group + q) * HEAD_SIZE, HEAD_SIZE), HEAD_SIZE
            )
            query = queries[:, column]
            scores = (
                lax.dot_general(
                    query, key_part, (((1,), (1,)), ((), ())), preferred_element_type=jnp.float32
                )
                * HEAD_SIZE ** (-0.5)
                + bias[...]
            )
            raised = jnp.exp(scores - jnp.max(scores, -1, keepdims=True))
            total = jnp.sum(raised, -1, keepdims=True)
            mixed = jnp.dot(
                raised.astype(jnp.bfloat16), value_part, preferred_element_type=jnp.float32
            )
            attention[own_rows, column] = (mixed / total).astype(jnp.bfloat16)
            return 0

        lax.fori_loop(first, first + count, one, 0)

    def take_chunk(p, s):
        block = plane_at(table, z, p)
        block_line(block, s, 0).wait_recv()
        pl.when((block > z) & has[0])(block_line(block, s, 0).start)
        pl.when((block < z) & has[1])(block_line(block, s, 1).start)
        block_rep(block, y, s).start()
        if s == PIECES - 1:
            marks_line(block, 0).wait_recv()
            pl.when((block > z) & has[0])(marks_line(block, 0).start)
            pl.when((block < z) & has[1])(marks_line(block, 1).start)
            marks_core(block, c).start()

    heads_copy = remote(
        attention.at[own_rows], attention.at[own_rows], heads_send, heads_recv, core_mate
    )
    at_end = (z == 0) | (z == planes - 1)
    inside = (z > 0) & (z < planes - 1)
    section = kv_heads * head_group // PIECES
    for s in range(PIECES):
        attend(s * section // head_group, s * section % head_group, section)
        if s == PIECES - 1:
            heads_copy.start()
        take_chunk(1, s)
        pl.when(inside)(functools.partial(take_chunk, 2, s))

    def column_block(side, core, b):
        return 2 * (half_planes * side + b) + core

    def piece(t, side, core, b):
        start = pl.multiple_of(column_block(side, core, b) * width, width)
        return resid.at[t, :, pl.ds(start, width)]

    def piece_line(t, b, way):
        ref = piece(t, x, c, b)
        return remote(
            ref,
            ref,
            piece_line_send.at[way, t, b],
            piece_line_recv.at[t, b],
            (y, beside[way], x),
        )

    def piece_tp(t, b, side):
        ref = piece(t, side, c, b)
        return remote(ref, ref, piece_tp_send.at[t, b], piece_tp_recv.at[t, b], tp_mate)

    def piece_core(t, b, kind, core):
        ref = piece(t, x if kind == 0 else 1 - x, core, b)
        return remote(
            ref, ref, piece_core_send.at[kind, t, b], piece_core_recv.at[kind, t, b], core_mate
        )

    def parts_copy(b):
        return remote(parts_out.at[b], parts_in.at[b], parts_send.at[b], parts_recv.at[b], tp_mate)

    def project(p):
        block = plane_at(table, z, p)
        if p == 0:
            late[0].wait()
            heads_copy.wait_recv()
        else:
            for s in range(PIECES):
                block_rep(block, 1 - y, s).wait_recv()
        part = jnp.dot(attention[...], out_blocks[block], preferred_element_type=jnp.float32)
        b = block % half_planes
        mine = block // half_planes == x

        @pl.when(mine)
        def _():
            kept[b] = part

        @pl.when(block // half_planes != x)
        def _():
            parts_out[b] = part.astype(jnp.bfloat16)
            parts_copy(b).start()

    def settle(p):
        block = plane_at(table, z, p)
        b = block % half_planes

        @pl.when(block // half_planes == x)
        def _():
            parts_copy(b).wait_recv()
            start = pl.multiple_of((2 * b + c) * width, width)
            summed = (
                hidden_in[:, pl.ds(start, width)].astype(jnp.float32)
                + kept[b]
                + parts_in[b].astype(jnp.float32)
            )
            target = pl.multiple_of(column_block(x, c, b) * width, width)
            resid[z, :, pl.ds(target, width)] = summed.astype(jnp.bfloat16)
            for way in range(2):
                pl.when(has[way])(piece_line(z, b, way).start)
            piece_tp(z, b, x).start()
            piece_core(z, b, 0, c).start()

    late[1].wait()
    rows_copy.wait_recv()
    gather_first, gather_second = gather_order(planes)

    def gather_at(side, q):
        return jnp.where(
            side == 0, plane_at(gather_first, z, q), plane_at(gather_second, z, q)
        )

    def take_plane(t):
        for i in range(half_planes):
            b = x * i + (1 - x) * (half_planes - 1 - i)
            piece_line(t, b, 0).wait_recv()
            pl.when((t > z) & has[0])(piece_line(t, b, 0).start)
            pl.when((t < z) & has[1])(piece_line(t, b, 1).start)
            piece_tp(t, b, x).start()
            piece_core(t, b, 0, c).start()

    nearest = gather_at(x, 1)
    direct = (nearest == z + 1) | (nearest == z - 1)
    project(0)
    for p in range(2, planes):
        for s in range(PIECES):
            if p == 2:
                pl.when(at_end)(functools.partial(take_chunk, p, s))
            else:
                take_chunk(p, s)
            if s == 0 and p > 2:
                project(p - 2)
            if s == PIECES - 2:
                settle(p - 2)
    for kind, s in weight_list:
        weight_tp(kind, s).wait_recv()
        weight_rep(kind, s, y).start()
    project(planes - 2)
    project(planes - 1)
    settle(planes - 2)
    pl.when(direct)(functools.partial(take_plane, nearest))
    settle(planes - 1)

    for q in range(1, planes + 1):
        if q == 1:
            pl.when(jnp.logical_not(direct))(functools.partial(take_plane, nearest))
        elif q < planes:
            take_plane(gather_at(x, q))
        t = gather_at(1 - x, q - 1)
        for b in range(half_planes):
            piece_tp(t, b, 1 - x).wait_recv()
            piece_core(t, b, 1, c).start()

    for copy in late[2:]:
        copy.wait()
    for kind, s in weight_list:
        weight_rep(kind, s, 1 - y).wait_recv()
    router_copy.wait_recv()
    for t in range(planes):
        marks_core(t, 1 - c).wait_recv()
    def hidden_copy(t, side):
        ref = hidden.at[side, t]
        return remote(ref, ref, hidden_send.at[t], hidden_recv.at[t], tp_mate)

    def open_plane(t):
        for b in range(half_planes):
            for kind in range(2):
                piece_core(t, b, kind, 1 - c).wait_recv()
        rows = resid[t]
        wide = rows.astype(jnp.float32)
        scale = lax.rsqrt(jnp.sum(wide * wide, 1, keepdims=True) / D + 1e-06)
        both = jnp.dot(rows, gate_up[...], preferred_element_type=jnp.float32) * scale
        gate, up = both[:, :ffw], both[:, ffw:]
        logits = (
            lax.dot_general(
                rows, routers[...], (((1,), (1,)), ((), ())), preferred_element_type=jnp.float32
            )
            * scale
        )
        chosen = jnp.concatenate(
            [
                lax.dot_general(
                    all_marks[2 * t + core],
                    eye,
                    (((0,), (0,)), ((), ())),
                    preferred_element_type=jnp.float32,
                )
                for core in range(2)
            ],
            0,
        )
        raised = jnp.where(chosen > 0.5, jnp.exp(logits), 0.0)
        share = jnp.sum(
            jnp.where(slots[...] == 2 * e + x, raised, 0.0), 1, keepdims=True
        ) / jnp.sum(raised, 1, keepdims=True)
        hidden[x, t] = (gate / (1.0 + jnp.exp(-gate)) * up * share).astype(jnp.bfloat16)
        hidden_copy(t, x).start()

    for p in reversed(range(planes)):
        open_plane(plane_at(table, z, p))

    def core_copy(t):
        return remote(core_out.at[t], core_in.at[t], core_send.at[t], core_recv.at[t], core_mate)

    part_width = half // LINE_PIECES

    def line_copy(t, i, way):
        columns = pl.ds(i * part_width, part_width)
        return remote(
            line_out.at[t, :, columns],
            line_in.at[way, t, :, columns],
            line_send.at[t, i],
            line_recv.at[way, t, i],
            (y, beside[way], x),
        )

    def close_plane(t):
        hidden_copy(t, 1 - x).wait_recv()
        product[...] = lax.dot_general(
            hidden[0, t], down[0], (((1,), (1,)), ((), ())), preferred_element_type=jnp.float32
        ) + lax.dot_general(
            hidden[1, t], down[1], (((1,), (1,)), ((), ())), preferred_element_type=jnp.float32
        )
        core_out[t] = product[mate_rows].astype(jnp.bfloat16)
        core_copy(t).start()
        own_total[t] = product[own_rows]

    def pass_on(t):
        core_copy(t).wait_recv()
        for i in range(LINE_PIECES):
            columns = pl.ds(i * part_width, part_width)
            own_total[t, :, columns] += core_in[t, :, columns].astype(jnp.float32)

            @pl.when((t >= z) & has[0])
            def _():
                line_copy(t, i, 1).wait_recv()
                own_total[t, :, columns] += line_in[1, t, :, columns].astype(jnp.float32)

            @pl.when((t <= z) & has[1])
            def _():
                line_copy(t, i, 0).wait_recv()
                own_total[t, :, columns] += line_in[0, t, :, columns].astype(jnp.float32)

            @pl.when(t != z)
            def _():
                line_out[t, :, columns] = own_total[t, :, columns].astype(jnp.bfloat16)

            pl.when(t > z)(line_copy(t, i, 1).start)
            pl.when(t < z)(line_copy(t, i, 0).start)

    for p in reversed(range(planes)):
        close_plane(plane_at(table, z, p))
        if p > 0:
            pl.when(at_end)(functools.partial(pass_on, plane_at(table, z, p)))
        if p + 1 < planes:
            pl.when(inside)(functools.partial(pass_on, plane_at(table, z, p + 1)))
    pass_on(z)
    own_resid = resid[z, own_rows, pl.ds(pl.multiple_of(x * half, half), half)]
    out[...] = (own_resid.astype(jnp.float32) + own_total[z]).astype(jnp.bfloat16)

    rows_copy.wait_send()
    heads_copy.wait_send()
    router_copy.wait_send()
    for kind, s in weight_list:
        weight_tp(kind, s).wait_send()
        weight_rep(kind, s, y).wait_send()
    for t in range(planes):
        marks_core(t, c).wait_send()
    for way in range(2):
        pl.when(has[way])(marks_line(z, way).wait_send)
    for s in range(PIECES):
        for way in range(2):
            pl.when(has[way])(block_own(s, way).wait_send)
    for p in range(1, planes):
        t = plane_at(table, z, p)
        pl.when((t > z) & has[0])(marks_line(t, 0).wait_send)
        pl.when((t < z) & has[1])(marks_line(t, 1).wait_send)
        for s in range(PIECES):
            pl.when((t > z) & has[0])(block_line(t, s, 0).wait_send)
            pl.when((t < z) & has[1])(block_line(t, s, 1).wait_send)
            block_rep(t, y, s).wait_send()
        for b in range(half_planes):
            pl.when((t > z) & has[0])(piece_line(t, b, 0).wait_send)
            pl.when((t < z) & has[1])(piece_line(t, b, 1).wait_send)
        for i in range(LINE_PIECES):
            pl.when(t > z)(line_copy(t, i, 1).wait_send)
            pl.when(t < z)(line_copy(t, i, 0).wait_send)
    for b in range(half_planes):
        parts_copy(b).wait_send()
        for way in range(2):
            pl.when(has[way])(piece_line(z, b, way).wait_send)
    for t in range(planes):
        for b in range(half_planes):
            piece_tp(t, b, x).wait_send()
            piece_core(t, b, 0, c).wait_send()
            piece_core(t, b, 1, c).wait_send()
        hidden_copy(t, x).wait_send()
        core_copy(t).wait_send()


def one_kernel_layer(
    hidden_states, queries, fresh_key_value, cache, lengths, out_weight, router, experts, expert_ids, slots
):
    group = lax.axis_size("ep")
    planes = group // 2
    half_planes = planes // 2
    tokens, half = hidden_states.shape
    depth, width = out_weight.shape
    number = router.shape[1]
    kv_width = cache.shape[3]
    key_total = cache.shape[2] + tokens
    units = experts.shape[3]
    vmem, anywhere = (pl.BlockSpec(memory_space=m) for m in (pltpu.VMEM, pl.ANY))
    dma = pltpu.SemaphoreType.DMA
    bf16, f32 = jnp.bfloat16, jnp.float32
    return pl.pallas_call(
        functools.partial(layer_kernel, planes, tokens, queries.shape[1] // kv_width),
        out_shape=jax.ShapeDtypeStruct((tokens, half), bf16),
        in_specs=[
            vmem,
            vmem,
            anywhere,
            pl.BlockSpec(memory_space=pltpu.SMEM),
            anywhere,
            anywhere,
            vmem,
            anywhere,
            vmem,
            vmem,
        ],
        out_specs=vmem,
        scratch_shapes=[
            pltpu.VMEM((key_total, kv_width), bf16),
            pltpu.VMEM((key_total, kv_width), bf16),
            pltpu.VMEM((tokens, key_total), f32),
            pltpu.VMEM((2 * tokens, depth), bf16),
            pltpu.VMEM((planes, depth, width), bf16),
            pltpu.VMEM((2 * tokens, half), bf16),
            pltpu.VMEM((half_planes, 2 * tokens, width), f32),
            pltpu.VMEM((half_planes, 2 * tokens, width), bf16),
            pltpu.VMEM((half_planes, 2 * tokens, width), bf16),
            pltpu.VMEM((planes, 2 * tokens, 2 * half), bf16),
            pltpu.VMEM((2 * half, 2 * units), bf16),
            pltpu.VMEM((2, half, units), bf16),
            pltpu.VMEM((number, 2 * half), bf16),
            pltpu.VMEM((group, number, tokens), bf16),
            pltpu.VMEM((2, planes, 2 * tokens, units), bf16),
            pltpu.VMEM((2 * tokens, half), f32),
            pltpu.VMEM((planes, tokens, half), f32),
            pltpu.VMEM((planes, tokens, half), bf16),
            pltpu.VMEM((planes, tokens, half), bf16),
            pltpu.VMEM((planes, tokens, half), bf16),
            pltpu.VMEM((2, planes, tokens, half), bf16),
            dma((11,)),
            dma((2, WEIGHT_PIECES)),
            dma((2, WEIGHT_PIECES)),
            dma((2, WEIGHT_PIECES)),
            dma((2, WEIGHT_PIECES)),
            dma,
            dma,
            dma,
            dma,
            dma,
            dma,
            dma((2 * planes,)),
            dma((planes,)),
            dma((planes,)),
            dma((planes,)),
            dma((2, planes, PIECES)),
            dma((planes, PIECES)),
            dma((planes, PIECES)),
            dma((planes, PIECES)),
            dma((half_planes,)),
            dma((half_planes,)),
            dma((2, planes, half_planes)),
            dma((planes, half_planes)),
            dma((planes, half_planes)),
            dma((planes, half_planes)),
            dma((2, planes, half_planes)),
            dma((2, planes, half_planes)),
            dma((planes,)),
            dma((planes,)),
            dma((planes,)),
            dma((planes,)),
            dma((planes, LINE_PIECES)),
            dma((2, planes, LINE_PIECES)),
        ],
        compiler_params=pltpu.CompilerParams(
            collective_id=0, has_side_effects=True, vmem_limit_bytes=56 * 1024 * 1024
        ),
    )(
        queries,
        fresh_key_value,
        cache,
        lengths,
        out_weight,
        hidden_states,
        router.T,
        experts,
        jnp.swapaxes(expert_ids, 1, 2),
        slots.reshape(1, number),
    )


def per_device(
    hidden_states,
    queries,
    fresh_key_value,
    cache,
    cache_lengths,
    out_weight,
    router_weight,
    expert_weights,
    expert_ids,
    old_slots,
    new_slots,
    moved_experts,
):
    tokens_dev = hidden_states.shape[1]
    quarter = hidden_states.shape[2]
    experts = router_weight.shape[1]
    top_count = expert_ids.shape[2]
    groups = lax.axis_size("ep")
    local_slots = expert_weights.shape[0]
    capacity = min(tokens_dev, 3 * tokens_dev * top_count // (2 * experts))
    routed = expert_ids.reshape(2 * tokens_dev, top_count)
    if (
        lax.axis_size("rep") == 2
        and lax.axis_size("tp") == 2
        and groups == 8
        and local_slots == 2
        and tokens_dev % 16 == 0
    ):
        mixed = one_kernel_layer(
            hidden_states.reshape(2 * tokens_dev, quarter),
            queries.reshape(2 * tokens_dev, queries.shape[2]),
            fresh_key_value,
            cache,
            cache_lengths,
            out_weight,
            router_weight,
            expert_weights,
            expert_ids,
            old_slots,
        )
        return mixed.reshape(2, tokens_dev, quarter)
    attention = attend_local(queries, fresh_key_value, cache, cache_lengths)
    head_terms = jnp.dot(
        attention,
        lax.all_gather(out_weight, "ep", axis=1, tiled=True),
        preferred_element_type=jnp.float32,
    )
    attn_out = lax.psum_scatter(
        head_terms.astype(jnp.bfloat16), "tp", scatter_dimension=1, tiled=True
    ).astype(jnp.float32)
    residual = (
        hidden_states.reshape(2 * tokens_dev, quarter).astype(jnp.float32) + attn_out
    ).astype(jnp.bfloat16)
    wide = residual.astype(jnp.float32)
    squares = lax.psum(jnp.sum(wide * wide, 1), "tp")
    normed = (wide * lax.rsqrt(squares / D + 1e-06)[:, None]).astype(jnp.bfloat16)
    logits = lax.psum(
        jnp.dot(normed, router_weight, preferred_element_type=jnp.float32).astype(jnp.bfloat16),
        "tp",
    ).astype(jnp.float32)
    selected = jnp.sum(
        jnp.where(
            routed[:, :, None] == jnp.arange(experts, dtype=jnp.int32)[None, None, :],
            logits[:, None, :],
            0.0,
        ),
        -1,
    )
    raised = jnp.exp(selected)
    combine = raised / jnp.sum(raised, 1, keepdims=True)
    outputs = []
    for lower in (0, tokens_dev):
        upper = lower + tokens_dev
        outputs.append(
            mix_block(
                normed[lower:upper],
                residual[lower:upper],
                routed[lower:upper],
                combine[lower:upper],
                old_slots,
                expert_weights,
                capacity,
                groups,
            )
        )
    return jnp.stack(outputs)


def solution(mesh):
    return jax.shard_map(
        per_device,
        mesh=mesh,
        in_specs=(
            P(None, ("rep", "ep"), "tp"),
            P(None, ("rep", "ep"), "tp"),
            P(None, ("rep", "ep"), None, "tp"),
            P(("rep", "ep"), None, None, "tp"),
            P(("rep", "ep")),
            P("tp", "ep"),
            P("tp", None),
            P("ep", None, "tp", None),
            P(None, ("rep", "ep"), None),
            P(),
            P(),
            P(),
        ),
        out_specs=P(None, ("rep", "ep"), "tp"),
        check_vma=False,
    )
```

```python
import functools

import jax
import jax.numpy as jnp
from jax import lax
from jax.experimental import pallas as pl
from jax.experimental.pallas import tpu as pltpu
from jax.sharding import PartitionSpec as P

D = 2048
HEAD_SIZE = 128


def lookup(entries, wanted_keys):
    return jnp.sum(
        jnp.where(
            wanted_keys[..., None] == jnp.arange(entries.shape[0], dtype=jnp.int32), entries, 0
        ),
        -1,
    )


def attend_local(queries, fresh_key_value, cache, cache_lengths):
    tokens_dev = queries.shape[1]
    kv_heads = fresh_key_value.shape[3] // HEAD_SIZE
    query_group_width = queries.shape[2] // HEAD_SIZE // kv_heads
    key_matrix = jnp.concatenate(
        [cache[0, 0], fresh_key_value[0, :, 0], fresh_key_value[1, :, 0]], 0
    )
    value_matrix = jnp.concatenate(
        [cache[0, 1], fresh_key_value[0, :, 1], fresh_key_value[1, :, 1]], 0
    )
    key_total = key_matrix.shape[0]
    context = cache.shape[2]
    query_matrix = queries.reshape(2 * tokens_dev, kv_heads, query_group_width, HEAD_SIZE)
    attention_scores = jnp.einsum(
        "meqt,wet->eqmw",
        query_matrix,
        key_matrix.reshape(key_total, kv_heads, HEAD_SIZE),
        preferred_element_type=jnp.float32,
    ) * HEAD_SIZE ** (-0.5)
    position = jnp.arange(key_total, dtype=jnp.int32)[None, :]
    row_index = jnp.arange(2 * tokens_dev, dtype=jnp.int32)[:, None]
    visible = jnp.where(
        position < context, position < cache_lengths[0], position - context <= row_index
    )
    attention_scores = jnp.where(visible, attention_scores, jnp.float32(-1e30))
    largest = jnp.max(attention_scores, -1, keepdims=True)
    weights = jnp.where(visible, jnp.exp(attention_scores - largest), jnp.float32(0.0))
    route_probability = (weights / jnp.sum(weights, -1, keepdims=True)).astype(jnp.bfloat16)
    layer_result = jnp.einsum(
        "qizo,oqx->zqix",
        route_probability,
        value_matrix.reshape(key_total, kv_heads, HEAD_SIZE),
        preferred_element_type=jnp.float32,
    )
    return layer_result.reshape(2 * tokens_dev, -1).astype(jnp.bfloat16)


def run_slots(weights, received):
    gate_up = jnp.einsum(
        "secq,egqf->secgf", received, weights[:, :2], preferred_element_type=jnp.float32
    )
    summed = lax.psum(gate_up.astype(jnp.bfloat16), "tp").astype(jnp.float32)
    hidden = (jax.nn.silu(summed[:, :, :, 0]) * summed[:, :, :, 1]).astype(jnp.bfloat16)
    layer_result = jnp.einsum(
        "secf,eqf->secq", hidden, weights[:, 2], preferred_element_type=jnp.float32
    ).astype(jnp.bfloat16)
    return lax.all_to_all(layer_result, "ep", split_axis=0, concat_axis=0, tiled=True)


def mix_block(normed_rows, resid_rows, routed, combine, slot_table, weights, capacity, groups):
    tokens_dev, top_count = routed.shape
    experts = slot_table.shape[0]
    local_slots = weights.shape[0]
    quarter = normed_rows.shape[1]
    slot_index = lookup(slot_table, routed)
    picked_mask = routed[:, :, None] == jnp.arange(experts, dtype=jnp.int32)[None, None, :]
    expert_marks = picked_mask.any(1).astype(jnp.bfloat16)
    earlier = (jnp.arange(tokens_dev)[:, None] > jnp.arange(tokens_dev)[None, :]).astype(
        jnp.bfloat16
    )
    before = jnp.dot(earlier, expert_marks, preferred_element_type=jnp.float32)
    slot_rank = jnp.sum(jnp.where(picked_mask, before[:, None, :], 0.0), -1).astype(jnp.int32)
    buffer_row = (slot_index * capacity + slot_rank).reshape(-1)
    buffer_rows = (
        jnp.zeros((groups * local_slots * capacity, quarter), jnp.bfloat16)
        .at[buffer_row]
        .set(jnp.repeat(normed_rows, top_count, axis=0))
    )
    outgoing = buffer_rows.reshape(groups, local_slots, capacity, quarter)
    returned = run_slots(
        weights, lax.all_to_all(outgoing, "ep", split_axis=0, concat_axis=0, tiled=True)
    )
    gathered = returned.reshape(-1, quarter)[buffer_row].reshape(tokens_dev, top_count, quarter)
    mixed_rows = resid_rows.astype(jnp.float32) + jnp.sum(
        combine[:, :, None] * gathered.astype(jnp.float32), 1
    )
    return mixed_rows.astype(jnp.bfloat16)


MESH = pl.DeviceIdType.MESH
PIECES = 4
LINE_PIECES = 4
WEIGHT_PIECES = 2


def line_order(planes):
    table = []
    for z in range(planes):
        table.append(
            sorted(
                range(planes),
                key=lambda t: (abs(t - z), (z if t < z else planes - 1 - z) if t != z else 0),
            )
        )
    return table


def gather_order(planes):
    tables = []
    for side in range(2):
        table = []
        for z in range(planes):
            rest = sorted(
                range(planes), key=lambda t: (t != z, t // (planes // 2) != side, abs(t - z))
            )
            table.append(rest)
        tables.append(table)
    return tables


def plane_at(table, z, p):
    value = jnp.int32(0)
    for i, row in enumerate(table):
        value = value + jnp.where(z == i, jnp.int32(row[p]), 0)
    return value


def layer_kernel(
    planes,
    tokens,
    head_group,
    queries,
    fresh,
    cache,
    lengths,
    out_weight,
    hidden_states,
    router,
    experts,
    routed,
    slots,
    out,
    keys,
    values,
    bias,
    attention,
    out_blocks,
    hidden_in,
    kept,
    parts_out,
    parts_in,
    resid,
    gate_up,
    down,
    routers,
    all_marks,
    hidden,
    product,
    own_total,
    core_out,
    core_in,
    line_out,
    line_in,
    local_sem,
    weight_send,
    weight_recv,
    weight_rep_send,
    weight_rep_recv,
    router_send,
    router_recv,
    rows_send,
    rows_recv,
    heads_send,
    heads_recv,
    marks_line_send,
    marks_line_recv,
    marks_core_send,
    marks_core_recv,
    block_line_send,
    block_line_recv,
    block_rep_send,
    block_rep_recv,
    parts_send,
    parts_recv,
    piece_line_send,
    piece_line_recv,
    piece_tp_send,
    piece_tp_recv,
    piece_core_send,
    piece_core_recv,
    hidden_send,
    hidden_recv,
    core_send,
    core_recv,
    line_send,
    line_recv,
):
    y, e, x = lax.axis_index("rep"), lax.axis_index("ep"), lax.axis_index("tp")
    z, c = e // 2, e % 2
    group = 2 * planes
    half_planes = planes // 2
    table = line_order(planes)
    width = out_weight.shape[1]
    depth = out_weight.shape[0]
    half = hidden_states.shape[1]
    ffw = experts.shape[3]
    has = (z > 0, z < planes - 1)
    beside = (e - 2, e + 2)
    tp_mate = (y, e, 1 - x)
    rep_mate = (1 - y, e, x)
    mate = e + 1 - 2 * c
    core_mate = (y, mate, x)
    chunk = depth // 2 // PIECES
    own_rows = pl.ds(pl.multiple_of(c * tokens, tokens), tokens)
    mate_rows = pl.ds(pl.multiple_of((1 - c) * tokens, tokens), tokens)

    def remote(src, dst, send, recv, target):
        return pltpu.make_async_remote_copy(
            src_ref=src,
            dst_ref=dst,
            send_sem=send,
            recv_sem=recv,
            device_id=target,
            device_id_type=MESH,
        )

    barrier = pltpu.get_barrier_semaphore()
    for target in (tp_mate, rep_mate, core_mate):
        pl.semaphore_signal(barrier, inc=1, device_id=target, device_id_type=MESH)
    for way in range(2):

        @pl.when(has[way])
        def _():
            pl.semaphore_signal(
                barrier, inc=1, device_id=(y, beside[way], x), device_id_type=MESH
            )

    context = cache.shape[2]
    local = [
        pltpu.make_async_copy(cache.at[0, 0], keys.at[pl.ds(0, context)], local_sem.at[0]),
        pltpu.make_async_copy(cache.at[0, 1], values.at[pl.ds(0, context)], local_sem.at[1]),
    ]
    late = [
        pltpu.make_async_copy(out_weight, out_blocks.at[z], local_sem.at[4]),
        pltpu.make_async_copy(hidden_states, hidden_in.at[own_rows], local_sem.at[5]),
        pltpu.make_async_copy(
            experts.at[x, 0],
            gate_up.at[pl.ds(pl.multiple_of(x * half, half), half), pl.ds(0, ffw)],
            local_sem.at[6],
        ),
        pltpu.make_async_copy(
            experts.at[x, 1],
            gate_up.at[pl.ds(pl.multiple_of(x * half, half), half), pl.ds(ffw, ffw)],
            local_sem.at[10],
        ),
        pltpu.make_async_copy(experts.at[0, 2], down.at[0], local_sem.at[7]),
        pltpu.make_async_copy(experts.at[1, 2], down.at[1], local_sem.at[8]),
        pltpu.make_async_copy(
            router, routers.at[:, pl.ds(pl.multiple_of(x * half, half), half)], local_sem.at[9]
        ),
    ]
    for copy in local:
        copy.start()

    number = router.shape[0]
    eye = (
        lax.broadcasted_iota(jnp.int32, (number, number), 0)
        == lax.broadcasted_iota(jnp.int32, (number, number), 1)
    ).astype(jnp.bfloat16)
    blocks, top_count, block_tokens = routed.shape
    expert = lax.broadcasted_iota(jnp.int32, (number, block_tokens), 0)
    for block in range(blocks):
        named = jnp.zeros((number, block_tokens), jnp.int32)
        for k in range(top_count):
            named += (routed[block, k : k + 1, :] == expert).astype(jnp.int32)
        all_marks[e, :, block * block_tokens : (block + 1) * block_tokens] = named.astype(
            jnp.float32
        ).astype(jnp.bfloat16)

    pl.semaphore_wait(barrier, 3 + has[0].astype(jnp.int32) + has[1].astype(jnp.int32))

    def block_chunk(block, side, s):
        return out_blocks.at[
            block, pl.ds(pl.multiple_of(side * (depth // 2) + s * chunk, chunk), chunk)
        ]

    def block_line(block, s, way):
        piece = block_chunk(block, y, s)
        return remote(
            piece,
            piece,
            block_line_send.at[way, block, s],
            block_line_recv.at[block, s],
            (y, beside[way], x),
        )

    def block_own(s, way):
        return remote(
            out_weight.at[pl.ds(pl.multiple_of(y * (depth // 2) + s * chunk, chunk), chunk)],
            block_chunk(z, y, s),
            block_line_send.at[way, z, s],
            block_line_recv.at[z, s],
            (y, beside[way], x),
        )

    def block_rep(block, side, s):
        piece = block_chunk(block, side, s)
        return remote(piece, piece, block_rep_send.at[block, s], block_rep_recv.at[block, s], rep_mate)

    for s in range(PIECES):
        for way in range(2):
            pl.when(has[way])(block_own(s, way).start)
    rows_copy = remote(hidden_states, hidden_in.at[own_rows], rows_send, rows_recv, core_mate)
    rows_copy.start()
    def marks_line(t, way):
        ref = all_marks.at[2 * t + c]
        return remote(
            ref,
            ref,
            marks_line_send.at[way * planes + t],
            marks_line_recv.at[t],
            (y, beside[way], x),
        )

    def marks_core(t, core):
        ref = all_marks.at[2 * t + core]
        return remote(ref, ref, marks_core_send.at[t], marks_core_recv.at[t], core_mate)

    for way in range(2):
        pl.when(has[way])(marks_line(z, way).start)
    marks_core(z, c).start()
    router_copy = remote(
        router,
        routers.at[:, pl.ds(pl.multiple_of(x * half, half), half)],
        router_send,
        router_recv,
        tp_mate,
    )
    router_copy.start()
    share_rows = half // (2 * WEIGHT_PIECES)

    def weight_share(kind, s, tp_side, rep_side):
        start = tp_side * half + (rep_side * WEIGHT_PIECES + s) * share_rows
        rows = pl.ds(pl.multiple_of(start, share_rows), share_rows)
        return gate_up.at[rows, pl.ds(kind * ffw, ffw)]

    def weight_tp(kind, s):
        start = pl.multiple_of((y * WEIGHT_PIECES + s) * share_rows, share_rows)
        return remote(
            experts.at[1 - x, kind, pl.ds(start, share_rows)],
            weight_share(kind, s, x, y),
            weight_send.at[kind, s],
            weight_recv.at[kind, s],
            tp_mate,
        )

    def weight_rep(kind, s, side):
        ref = weight_share(kind, s, 1 - x, side)
        return remote(
            ref, ref, weight_rep_send.at[kind, s], weight_rep_recv.at[kind, s], rep_mate
        )

    weight_list = [(kind, s) for s in range(WEIGHT_PIECES) for kind in range(2)]
    for kind, s in weight_list:
        weight_tp(kind, s).start()
    for copy in late:
        copy.start()

    key_total = keys.shape[0]
    position = lax.broadcasted_iota(jnp.int32, (tokens, key_total), 1)
    row = lax.broadcasted_iota(jnp.int32, (tokens, key_total), 0)
    visible = jnp.where(
        position < context,
        (position < lengths[0]).astype(jnp.int32),
        (position - context <= row).astype(jnp.int32),
    )
    bias[...] = jnp.where(visible > 0, jnp.float32(0.0), jnp.float32(-1e30))
    for block in range(blocks):
        start = context + block * block_tokens
        keys[start : start + block_tokens] = fresh[block, :, 0, :]
        values[start : start + block_tokens] = fresh[block, :, 1, :]
    for copy in local:
        copy.wait()
    kv_heads = keys.shape[1] // HEAD_SIZE

    def attend(kv, first, count):
        key_part = keys[:, kv * HEAD_SIZE : (kv + 1) * HEAD_SIZE]
        value_part = values[:, kv * HEAD_SIZE : (kv + 1) * HEAD_SIZE]

        def one(q, _):
            column = pl.ds(
                pl.multiple_of((kv * head_group + q) * HEAD_SIZE, HEAD_SIZE), HEAD_SIZE
            )
            query = queries[:, column]
            scores = (
                lax.dot_general(
                    query, key_part, (((1,), (1,)), ((), ())), preferred_element_type=jnp.float32
                )
                * HEAD_SIZE ** (-0.5)
                + bias[...]
            )
            raised = jnp.exp(scores - jnp.max(scores, -1, keepdims=True))
            total = jnp.sum(raised, -1, keepdims=True)
            mixed = jnp.dot(
                raised.astype(jnp.bfloat16), value_part, preferred_element_type=jnp.float32
            )
            attention[own_rows, column] = (mixed / total).astype(jnp.bfloat16)
            return 0

        lax.fori_loop(first, first + count, one, 0)

    def take_chunk(p, s):
        block = plane_at(table, z, p)
        block_line(block, s, 0).wait_recv()
        pl.when((block > z) & has[0])(block_line(block, s, 0).start)
        pl.when((block < z) & has[1])(block_line(block, s, 1).start)
        block_rep(block, y, s).start()
        if s == PIECES - 1:
            marks_line(block, 0).wait_recv()
            pl.when((block > z) & has[0])(marks_line(block, 0).start)
            pl.when((block < z) & has[1])(marks_line(block, 1).start)
            marks_core(block, c).start()

    heads_copy = remote(
        attention.at[own_rows], attention.at[own_rows], heads_send, heads_recv, core_mate
    )
    at_end = (z == 0) | (z == planes - 1)
    inside = (z > 0) & (z < planes - 1)
    section = kv_heads * head_group // PIECES
    for s in range(PIECES):
        attend(s * section // head_group, s * section % head_group, section)
        if s == PIECES - 1:
            heads_copy.start()
        take_chunk(1, s)
        pl.when(inside)(functools.partial(take_chunk, 2, s))

    def column_block(side, core, b):
        return 2 * (half_planes * side + b) + core

    def piece(t, side, core, b):
        start = pl.multiple_of(column_block(side, core, b) * width, width)
        return resid.at[t, :, pl.ds(start, width)]

    def piece_line(t, b, way):
        ref = piece(t, x, c, b)
        return remote(
            ref,
            ref,
            piece_line_send.at[way, t, b],
            piece_line_recv.at[t, b],
            (y, beside[way], x),
        )

    def piece_tp(t, b, side):
        ref = piece(t, side, c, b)
        return remote(ref, ref, piece_tp_send.at[t, b], piece_tp_recv.at[t, b], tp_mate)

    def piece_core(t, b, kind, core):
        ref = piece(t, x if kind == 0 else 1 - x, core, b)
        return remote(
            ref, ref, piece_core_send.at[kind, t, b], piece_core_recv.at[kind, t, b], core_mate
        )

    def parts_copy(b):
        return remote(parts_out.at[b], parts_in.at[b], parts_send.at[b], parts_recv.at[b], tp_mate)

    def project(p):
        block = plane_at(table, z, p)
        if p == 0:
            late[0].wait()
            heads_copy.wait_recv()
        else:
            for s in range(PIECES):
                block_rep(block, 1 - y, s).wait_recv()
        part = jnp.dot(attention[...], out_blocks[block], preferred_element_type=jnp.float32)
        b = block % half_planes
        mine = block // half_planes == x

        @pl.when(mine)
        def _():
            kept[b] = part

        @pl.when(block // half_planes != x)
        def _():
            parts_out[b] = part.astype(jnp.bfloat16)
            parts_copy(b).start()

    def settle(p):
        block = plane_at(table, z, p)
        b = block % half_planes

        @pl.when(block // half_planes == x)
        def _():
            parts_copy(b).wait_recv()
            start = pl.multiple_of((2 * b + c) * width, width)
            summed = (
                hidden_in[:, pl.ds(start, width)].astype(jnp.float32)
                + kept[b]
                + parts_in[b].astype(jnp.float32)
            )
            target = pl.multiple_of(column_block(x, c, b) * width, width)
            resid[z, :, pl.ds(target, width)] = summed.astype(jnp.bfloat16)
            for way in range(2):
                pl.when(has[way])(piece_line(z, b, way).start)
            piece_tp(z, b, x).start()
            piece_core(z, b, 0, c).start()

    late[1].wait()
    rows_copy.wait_recv()
    gather_first, gather_second = gather_order(planes)

    def gather_at(side, q):
        return jnp.where(
            side == 0, plane_at(gather_first, z, q), plane_at(gather_second, z, q)
        )

    def take_plane(t):
        for i in range(half_planes):
            b = x * i + (1 - x) * (half_planes - 1 - i)
            piece_line(t, b, 0).wait_recv()
            piece_tp(t, b, x).start()
            pl.when((t > z) & has[0])(piece_line(t, b, 0).start)
            pl.when((t < z) & has[1])(piece_line(t, b, 1).start)
            piece_core(t, b, 0, c).start()

    nearest = gather_at(x, 1)
    direct = (nearest == z + 1) | (nearest == z - 1)
    project(0)
    for p in range(2, planes):
        for s in range(PIECES):
            if p == 2:
                pl.when(at_end)(functools.partial(take_chunk, p, s))
            else:
                take_chunk(p, s)
            if s == 0 and p > 2:
                project(p - 2)
            if s == PIECES - 2:
                settle(p - 2)
    for kind, s in weight_list:
        weight_tp(kind, s).wait_recv()
        weight_rep(kind, s, y).start()
    project(planes - 2)
    project(planes - 1)
    settle(planes - 2)
    pl.when(direct)(functools.partial(take_plane, nearest))
    settle(planes - 1)

    for q in range(1, planes + 1):
        if q == 1:
            pl.when(jnp.logical_not(direct))(functools.partial(take_plane, nearest))
        elif q < planes:
            take_plane(gather_at(x, q))
        t = gather_at(1 - x, q - 1)
        for b in range(half_planes):
            piece_tp(t, b, 1 - x).wait_recv()
            piece_core(t, b, 1, c).start()

    for copy in late[2:]:
        copy.wait()
    for kind, s in weight_list:
        weight_rep(kind, s, 1 - y).wait_recv()
    router_copy.wait_recv()
    for t in range(planes):
        marks_core(t, 1 - c).wait_recv()
    def hidden_copy(t, side):
        ref = hidden.at[side, t]
        return remote(ref, ref, hidden_send.at[t], hidden_recv.at[t], tp_mate)

    def open_plane(t):
        for b in range(half_planes):
            for kind in range(2):
                piece_core(t, b, kind, 1 - c).wait_recv()
        rows = resid[t]
        wide = rows.astype(jnp.float32)
        scale = lax.rsqrt(jnp.sum(wide * wide, 1, keepdims=True) / D + 1e-06)
        both = jnp.dot(rows, gate_up[...], preferred_element_type=jnp.float32) * scale
        gate, up = both[:, :ffw], both[:, ffw:]
        logits = (
            lax.dot_general(
                rows, routers[...], (((1,), (1,)), ((), ())), preferred_element_type=jnp.float32
            )
            * scale
        )
        chosen = jnp.concatenate(
            [
                lax.dot_general(
                    all_marks[2 * t + core],
                    eye,
                    (((0,), (0,)), ((), ())),
                    preferred_element_type=jnp.float32,
                )
                for core in range(2)
            ],
            0,
        )
        raised = jnp.where(chosen > 0.5, jnp.exp(logits), 0.0)
        share = jnp.sum(
            jnp.where(slots[...] == 2 * e + x, raised, 0.0), 1, keepdims=True
        ) / jnp.sum(raised, 1, keepdims=True)
        hidden[x, t] = (gate / (1.0 + jnp.exp(-gate)) * up * share).astype(jnp.bfloat16)
        hidden_copy(t, x).start()

    for p in reversed(range(planes)):
        open_plane(plane_at(table, z, p))

    def core_copy(t):
        return remote(core_out.at[t], core_in.at[t], core_send.at[t], core_recv.at[t], core_mate)

    part_width = half // LINE_PIECES

    def line_copy(t, i, way):
        columns = pl.ds(i * part_width, part_width)
        return remote(
            line_out.at[t, :, columns],
            line_in.at[way, t, :, columns],
            line_send.at[t, i],
            line_recv.at[way, t, i],
            (y, beside[way], x),
        )

    def close_plane(t):
        hidden_copy(t, 1 - x).wait_recv()
        product[...] = lax.dot_general(
            hidden[0, t], down[0], (((1,), (1,)), ((), ())), preferred_element_type=jnp.float32
        ) + lax.dot_general(
            hidden[1, t], down[1], (((1,), (1,)), ((), ())), preferred_element_type=jnp.float32
        )
        core_out[t] = product[mate_rows].astype(jnp.bfloat16)
        core_copy(t).start()
        own_total[t] = product[own_rows]

    def pass_on(t):
        core_copy(t).wait_recv()
        for i in range(LINE_PIECES):
            columns = pl.ds(i * part_width, part_width)
            own_total[t, :, columns] += core_in[t, :, columns].astype(jnp.float32)

            @pl.when((t >= z) & has[0])
            def _():
                line_copy(t, i, 1).wait_recv()
                own_total[t, :, columns] += line_in[1, t, :, columns].astype(jnp.float32)

            @pl.when((t <= z) & has[1])
            def _():
                line_copy(t, i, 0).wait_recv()
                own_total[t, :, columns] += line_in[0, t, :, columns].astype(jnp.float32)

            @pl.when(t != z)
            def _():
                line_out[t, :, columns] = own_total[t, :, columns].astype(jnp.bfloat16)

            pl.when(t > z)(line_copy(t, i, 1).start)
            pl.when(t < z)(line_copy(t, i, 0).start)

    for p in reversed(range(planes)):
        close_plane(plane_at(table, z, p))
        if p > 0:
            pl.when(at_end)(functools.partial(pass_on, plane_at(table, z, p)))
        if p + 1 < planes:
            pl.when(inside)(functools.partial(pass_on, plane_at(table, z, p + 1)))
    pass_on(z)
    own_resid = resid[z, own_rows, pl.ds(pl.multiple_of(x * half, half), half)]
    out[...] = (own_resid.astype(jnp.float32) + own_total[z]).astype(jnp.bfloat16)

    rows_copy.wait_send()
    heads_copy.wait_send()
    router_copy.wait_send()
    for kind, s in weight_list:
        weight_tp(kind, s).wait_send()
        weight_rep(kind, s, y).wait_send()
    for t in range(planes):
        marks_core(t, c).wait_send()
    for way in range(2):
        pl.when(has[way])(marks_line(z, way).wait_send)
    for s in range(PIECES):
        for way in range(2):
            pl.when(has[way])(block_own(s, way).wait_send)
    for p in range(1, planes):
        t = plane_at(table, z, p)
        pl.when((t > z) & has[0])(marks_line(t, 0).wait_send)
        pl.when((t < z) & has[1])(marks_line(t, 1).wait_send)
        for s in range(PIECES):
            pl.when((t > z) & has[0])(block_line(t, s, 0).wait_send)
            pl.when((t < z) & has[1])(block_line(t, s, 1).wait_send)
            block_rep(t, y, s).wait_send()
        for b in range(half_planes):
            pl.when((t > z) & has[0])(piece_line(t, b, 0).wait_send)
            pl.when((t < z) & has[1])(piece_line(t, b, 1).wait_send)
        for i in range(LINE_PIECES):
            pl.when(t > z)(line_copy(t, i, 1).wait_send)
            pl.when(t < z)(line_copy(t, i, 0).wait_send)
    for b in range(half_planes):
        parts_copy(b).wait_send()
        for way in range(2):
            pl.when(has[way])(piece_line(z, b, way).wait_send)
    for t in range(planes):
        for b in range(half_planes):
            piece_tp(t, b, x).wait_send()
            piece_core(t, b, 0, c).wait_send()
            piece_core(t, b, 1, c).wait_send()
        hidden_copy(t, x).wait_send()
        core_copy(t).wait_send()


def one_kernel_layer(
    hidden_states, queries, fresh_key_value, cache, lengths, out_weight, router, experts, expert_ids, slots
):
    group = lax.axis_size("ep")
    planes = group // 2
    half_planes = planes // 2
    tokens, half = hidden_states.shape
    depth, width = out_weight.shape
    number = router.shape[1]
    kv_width = cache.shape[3]
    key_total = cache.shape[2] + tokens
    units = experts.shape[3]
    vmem, anywhere = (pl.BlockSpec(memory_space=m) for m in (pltpu.VMEM, pl.ANY))
    dma = pltpu.SemaphoreType.DMA
    bf16, f32 = jnp.bfloat16, jnp.float32
    return pl.pallas_call(
        functools.partial(layer_kernel, planes, tokens, queries.shape[1] // kv_width),
        out_shape=jax.ShapeDtypeStruct((tokens, half), bf16),
        in_specs=[
            vmem,
            vmem,
            anywhere,
            pl.BlockSpec(memory_space=pltpu.SMEM),
            anywhere,
            anywhere,
            vmem,
            anywhere,
            vmem,
            vmem,
        ],
        out_specs=vmem,
        scratch_shapes=[
            pltpu.VMEM((key_total, kv_width), bf16),
            pltpu.VMEM((key_total, kv_width), bf16),
            pltpu.VMEM((tokens, key_total), f32),
            pltpu.VMEM((2 * tokens, depth), bf16),
            pltpu.VMEM((planes, depth, width), bf16),
            pltpu.VMEM((2 * tokens, half), bf16),
            pltpu.VMEM((half_planes, 2 * tokens, width), f32),
            pltpu.VMEM((half_planes, 2 * tokens, width), bf16),
            pltpu.VMEM((half_planes, 2 * tokens, width), bf16),
            pltpu.VMEM((planes, 2 * tokens, 2 * half), bf16),
            pltpu.VMEM((2 * half, 2 * units), bf16),
            pltpu.VMEM((2, half, units), bf16),
            pltpu.VMEM((number, 2 * half), bf16),
            pltpu.VMEM((group, number, tokens), bf16),
            pltpu.VMEM((2, planes, 2 * tokens, units), bf16),
            pltpu.VMEM((2 * tokens, half), f32),
            pltpu.VMEM((planes, tokens, half), f32),
            pltpu.VMEM((planes, tokens, half), bf16),
            pltpu.VMEM((planes, tokens, half), bf16),
            pltpu.VMEM((planes, tokens, half), bf16),
            pltpu.VMEM((2, planes, tokens, half), bf16),
            dma((11,)),
            dma((2, WEIGHT_PIECES)),
            dma((2, WEIGHT_PIECES)),
            dma((2, WEIGHT_PIECES)),
            dma((2, WEIGHT_PIECES)),
            dma,
            dma,
            dma,
            dma,
            dma,
            dma,
            dma((2 * planes,)),
            dma((planes,)),
            dma((planes,)),
            dma((planes,)),
            dma((2, planes, PIECES)),
            dma((planes, PIECES)),
            dma((planes, PIECES)),
            dma((planes, PIECES)),
            dma((half_planes,)),
            dma((half_planes,)),
            dma((2, planes, half_planes)),
            dma((planes, half_planes)),
            dma((planes, half_planes)),
            dma((planes, half_planes)),
            dma((2, planes, half_planes)),
            dma((2, planes, half_planes)),
            dma((planes,)),
            dma((planes,)),
            dma((planes,)),
            dma((planes,)),
            dma((planes, LINE_PIECES)),
            dma((2, planes, LINE_PIECES)),
        ],
        compiler_params=pltpu.CompilerParams(
            collective_id=0, has_side_effects=True, vmem_limit_bytes=56 * 1024 * 1024
        ),
    )(
        queries,
        fresh_key_value,
        cache,
        lengths,
        out_weight,
        hidden_states,
        router.T,
        experts,
        jnp.swapaxes(expert_ids, 1, 2),
        slots.reshape(1, number),
    )


def per_device(
    hidden_states,
    queries,
    fresh_key_value,
    cache,
    cache_lengths,
    out_weight,
    router_weight,
    expert_weights,
    expert_ids,
    old_slots,
    new_slots,
    moved_experts,
):
    tokens_dev = hidden_states.shape[1]
    quarter = hidden_states.shape[2]
    experts = router_weight.shape[1]
    top_count = expert_ids.shape[2]
    groups = lax.axis_size("ep")
    local_slots = expert_weights.shape[0]
    capacity = min(tokens_dev, 3 * tokens_dev * top_count // (2 * experts))
    routed = expert_ids.reshape(2 * tokens_dev, top_count)
    if (
        lax.axis_size("rep") == 2
        and lax.axis_size("tp") == 2
        and groups == 8
        and local_slots == 2
        and tokens_dev % 16 == 0
    ):
        mixed = one_kernel_layer(
            hidden_states.reshape(2 * tokens_dev, quarter),
            queries.reshape(2 * tokens_dev, queries.shape[2]),
            fresh_key_value,
            cache,
            cache_lengths,
            out_weight,
            router_weight,
            expert_weights,
            expert_ids,
            old_slots,
        )
        return mixed.reshape(2, tokens_dev, quarter)
    attention = attend_local(queries, fresh_key_value, cache, cache_lengths)
    head_terms = jnp.dot(
        attention,
        lax.all_gather(out_weight, "ep", axis=1, tiled=True),
        preferred_element_type=jnp.float32,
    )
    attn_out = lax.psum_scatter(
        head_terms.astype(jnp.bfloat16), "tp", scatter_dimension=1, tiled=True
    ).astype(jnp.float32)
    residual = (
        hidden_states.reshape(2 * tokens_dev, quarter).astype(jnp.float32) + attn_out
    ).astype(jnp.bfloat16)
    wide = residual.astype(jnp.float32)
    squares = lax.psum(jnp.sum(wide * wide, 1), "tp")
    normed = (wide * lax.rsqrt(squares / D + 1e-06)[:, None]).astype(jnp.bfloat16)
    logits = lax.psum(
        jnp.dot(normed, router_weight, preferred_element_type=jnp.float32).astype(jnp.bfloat16),
        "tp",
    ).astype(jnp.float32)
    selected = jnp.sum(
        jnp.where(
            routed[:, :, None] == jnp.arange(experts, dtype=jnp.int32)[None, None, :],
            logits[:, None, :],
            0.0,
        ),
        -1,
    )
    raised = jnp.exp(selected)
    combine = raised / jnp.sum(raised, 1, keepdims=True)
    outputs = []
    for lower in (0, tokens_dev):
        upper = lower + tokens_dev
        outputs.append(
            mix_block(
                normed[lower:upper],
                residual[lower:upper],
                routed[lower:upper],
                combine[lower:upper],
                old_slots,
                expert_weights,
                capacity,
                groups,
            )
        )
    return jnp.stack(outputs)


def solution(mesh):
    return jax.shard_map(
        per_device,
        mesh=mesh,
        in_specs=(
            P(None, ("rep", "ep"), "tp"),
            P(None, ("rep", "ep"), "tp"),
            P(None, ("rep", "ep"), None, "tp"),
            P(("rep", "ep"), None, None, "tp"),
            P(("rep", "ep")),
            P("tp", "ep"),
            P("tp", None),
            P("ep", None, "tp", None),
            P(None, ("rep", "ep"), None),
            P(),
            P(),
            P(),
        ),
        out_specs=P(None, ("rep", "ep"), "tp"),
        check_vma=False,
    )
```
